32 devices in a mesh: grp: 2 (over z_hi), tile: 8 (over y, x, core), spec: 2 (over z_lo).
Axes of the slice: x: 2, y: 2, z: 4 (z_hi: 2, z_lo: 2; z = z_hi * 2 + z_lo), core: 2. Of those that a mesh axis runs over, the one named last changes fastest.
Arguments:
- spectrum: float32 [2, 32, 36, 64, 256], P('grp', None, 'spec', 'tile'), may hold values from 0.01 to 1
- wind: float32 [2, 64, 256], P(None, 'tile'), may hold values from -48 to 48
- land_mask: int32 [64, 256], P('tile'), may hold values 0 or 1
- intersection: int32 [64, 256], P('tile'), may hold values from 0 to 255, as said below
- ocean_state: float32 [2, 3, 16, 256, 64], P('grp', None, 'spec', 'tile'), may hold values from -1 to 1
- sea_level: float32 [2, 256, 64], P('grp', 'tile'), may hold values from -1 to 1
Outputs:
- spectrum_next: float32 [2, 32, 36, 64, 256], P('grp', None, 'spec', 'tile')
- ocean_next: float32 [2, 3, 16, 256, 64], P('grp', None, 'spec', 'tile')
The draws below stay inside these ranges and needn't reach their ends.
Inputs may be any that keep to these rules, and one draw needn't show every extreme that they name: In each row i, intersection[i, j] = (j + s_i) mod 256 for a shift s_i of that row.
All inputs are finite; a program needn't handle non-finite values. No bound on the sum of `land_mask` on one device may be relied on, other than what follows from the above.
Results may differ from the reference program's by a relative error of at most 0.0001.
Values sent between devices are 32-bit elements; how exact they have to be, the bound alone decides.
No kernel may reach another device: no remote copies, remote signals or barrier semaphores. Data moves between devices by JAX's collectives and lax.ppermute only.
A program may use at most 128 MiB of HBM per device.

```python
import math
import jax
import jax.numpy as jnp
from jax import lax

FREQS = 32
DIRS = 36
NX = 256
LEVELS = 16
WSTEPS = 4
OSTEPS = 2
NY = 64


def draw_intersection(key, part):
    shifts = jax.random.randint(key, (NY, 1), 0, NX)
    columns = jnp.arange(NX, dtype=jnp.int32)[None, :]
    return ((columns + shifts) % NX).astype(jnp.int32)


def place_ends(values, own_key, least, high):
    shape = values.shape
    index_at = [jax.random.randint(jax.random.fold_in(own_key, axis), (), 0, shape[axis]) for axis in range(len(shape))]
    values = values.at[tuple(index_at)].set(least)
    longest = shape.index(max(shape))
    index_at[longest] = (index_at[longest] + 1) % shape[longest]
    return values.at[tuple(index_at)].set(high)


def block_scale(own_key, extent, shards, smallest, largest):
    gain, own = 1.0, jax.random.fold_in(own_key, 6)
    for dim, parts in shards:
        draws = jnp.exp(jax.random.uniform(jax.random.fold_in(own, dim), (parts,), jnp.float32, smallest / len(shards), largest / len(shards)))
        gain = gain * jnp.repeat(draws, extent[dim] // parts).reshape([-1 if axis == dim else 1 for axis in range(len(extent))])
    return gain


def noise(stream_key, dims, spread, limit, pieces=(), held_as=jnp.bfloat16):
    result = spread * jax.random.normal(stream_key, dims, jnp.float32)
    if pieces:
        result = result * block_scale(stream_key, dims, pieces, -0.22, 0.18)
    return jnp.clip(result, -limit, limit).astype(held_as)


def setup_inputs(seed: int = 0) -> dict:
    seeds = jax.random.split(jax.random.key(seed), 7)
    return {
        "spectrum": jnp.clip(jnp.exp(math.log(1.0) - 4.6051702 * jax.random.uniform(seeds[0], (2, FREQS, DIRS, NY, NX), jnp.float32) ** block_scale(seeds[0], (2, FREQS, DIRS, NY, NX), ((0, 2), (2, 2), (3, 8)), -0.2, 0.2)), 0.01, 1.0),
        "wind": noise(seeds[1], (2, NY, NX), 8.0, 48.0, ((1, 8),), jnp.float32),
        "land_mask": place_ends((jax.random.randint(seeds[2], (NY, NX), 0, 4) < 3).astype(jnp.int32), jax.random.fold_in(seeds[2], 1), 0, 1),
        "intersection": draw_intersection(jax.random.fold_in(seeds[6], 71), 0),
        "ocean_state": jnp.clip(jax.random.uniform(seeds[4], (2, 3, LEVELS, NX, NY), jnp.float32, -1.0, 1.0) * block_scale(seeds[4], (2, 3, LEVELS, NX, NY), ((0, 2), (2, 2), (3, 8)), -0.4, 0.0), -1.0, 1.0),
        "sea_level": jnp.clip(jax.random.uniform(seeds[5], (2, NX, NY), jnp.float32, -1.0, 1.0) * block_scale(seeds[5], (2, NX, NY), ((0, 2), (1, 8)), -0.4, 0.0), -1.0, 1.0),
    }


exact_precision = lax.Precision.HIGHEST


def wave_tables():
    freq_index = jnp.arange(FREQS, dtype=jnp.float32)
    frequency = 0.04 * 1.1 ** freq_index
    celerity = 1.56 / frequency
    group_speed = 0.4 * 1.1 ** (-freq_index)
    bin_width = 0.1 * frequency * (2.0 * math.pi / DIRS)
    angles = 2.0 * math.pi * (jnp.arange(DIRS, dtype=jnp.float32) + 0.5) / DIRS
    return frequency, celerity, group_speed, bin_width, jnp.cos(angles), jnp.sin(angles)


def level_tables():
    level_depth = (jnp.arange(LEVELS, dtype=jnp.float32) + 0.5) / LEVELS
    profile = jnp.exp(-2.0 * level_depth)
    return profile / jnp.sum(profile), profile


def east_west(energy, speeds):
    widths = [(0, 0)] * (energy.ndim - 1) + [(1, 1)]
    padded_energy = jnp.pad(energy, widths)
    padded_speed = jnp.pad(speeds, widths)
    fluxes = jnp.maximum(padded_speed[..., :-1], 0.0) * padded_energy[..., :-1] + jnp.minimum(padded_speed[..., 1:], 0.0) * padded_energy[..., 1:]
    return fluxes[..., 1:] - fluxes[..., :-1]


def north_south(with_rims, speed_rims):
    fluxes = jnp.maximum(speed_rims[..., :-1, :], 0.0) * with_rims[..., :-1, :] + jnp.minimum(speed_rims[..., 1:, :], 0.0) * with_rims[..., 1:, :]
    return fluxes[..., 1:, :] - fluxes[..., :-1, :]


def band_terms(advected, growth, breaking, energy, dir_cosines, dir_sines, bin_width, celerity, frequency):
    pushing = growth * breaking * advected
    stirring = jnp.stack([jnp.einsum("fdrx,d->frx", pushing, dir_cosines, precision=exact_precision), jnp.einsum("fdrx,d->frx", pushing, dir_sines, precision=exact_precision)])
    drifting = jnp.stack([jnp.einsum("fdrx,d->frx", energy, dir_cosines, precision=exact_precision), jnp.einsum("fdrx,d->frx", energy, dir_sines, precision=exact_precision)])
    stress = 5.0 * jnp.einsum("f,cfrx->crx", bin_width / celerity, stirring, precision=exact_precision)
    stokes = 20.0 * jnp.einsum("f,cfrx->crx", bin_width * frequency ** 3, drifting, precision=exact_precision)
    return jnp.concatenate([stress, stokes], axis=0)


def reorder(values, index):
    return jnp.take_along_axis(values, jnp.broadcast_to(index[None], values.shape), axis=2)


def ocean_update(ocean_fields, padded, ocean_mask, forcing, profile, top_level):
    lateral = padded[:, 1:-1, 2:, 1:-1] + padded[:, 1:-1, :-2, 1:-1] + padded[:, 1:-1, 1:-1, 2:] + padded[:, 1:-1, 1:-1, :-2] - 4.0 * ocean_fields
    vertical = padded[:, 2:, 1:-1, 1:-1] + padded[:, :-2, 1:-1, 1:-1] - 2.0 * ocean_fields
    diffused = ocean_fields + 0.1 * lateral + 0.2 * vertical
    shaped = profile[:, None, None]
    new_east = diffused[0] + 0.1 * (ocean_fields[1] + shaped * forcing[3]) + top_level * forcing[0]
    new_north = diffused[1] - 0.1 * (ocean_fields[0] + shaped * forcing[2]) + top_level * forcing[1]
    return jnp.stack([new_east, new_north, diffused[2]]) * ocean_mask


def reference(spectrum, wind, land_mask, intersection, ocean_state, sea_level):
    frequency, celerity, group_speed, bin_width, dir_cosines, dir_sines = wave_tables()
    weights, profile = level_tables()
    wet_cells = land_mask.astype(jnp.float32)
    ocean = ocean_state[1]
    currents = jnp.einsum("k,ckmi->cmi", weights, ocean[:2], precision=exact_precision)
    packed = jnp.concatenate([currents, sea_level[1][None]], axis=0)
    rows_form = jnp.transpose(packed, (0, 2, 1))
    picked = reorder(rows_form, intersection)
    water_depth = 10.0 + 4.0 * picked[2]
    speed_east = wet_cells * (group_speed[:, None, None, None] * dir_cosines[None, :, None, None] + 0.1 * picked[0])
    speed_north = wet_cells * (group_speed[:, None, None, None] * dir_sines[None, :, None, None] + 0.1 * picked[1])
    north_rims = jnp.pad(speed_north, ((0, 0), (0, 0), (1, 1), (0, 0)))
    drive = (wind[0][None] * dir_cosines[:, None, None] + wind[1][None] * dir_sines[:, None, None])[None] / celerity[:, None, None, None]
    growth = 0.05 * jnp.maximum(drive - 1.0, 0.0)
    energy = spectrum[0]
    for substep in range(WSTEPS):
        with_rims = jnp.pad(energy, ((0, 0), (0, 0), (1, 1), (0, 0)))
        advected = energy - east_west(energy, speed_east) - north_south(with_rims, north_rims)
        energy_total = jnp.tensordot(bin_width, jnp.sum(advected, axis=1), axes=1, precision=exact_precision)
        breaking = 1.0 / (1.0 + 25.0 * energy_total / (water_depth * water_depth))
        energy = wet_cells * breaking * advected * (1.0 + growth)
    band_fields = band_terms(advected, growth, breaking, energy, dir_cosines, dir_sines, bin_width, celerity, frequency)
    row_index = lax.broadcasted_iota(jnp.int32, intersection.shape, 0)
    col_index = lax.broadcasted_iota(jnp.int32, intersection.shape, 1)
    inverse = jnp.zeros(intersection.shape, jnp.int32).at[row_index, intersection].set(col_index)
    forcing = jnp.transpose(reorder(band_fields, inverse), (0, 2, 1))
    ocean_mask = jnp.transpose(jnp.take_along_axis(wet_cells, inverse, axis=1))
    top_level = (jnp.arange(LEVELS) == 0).astype(jnp.float32)[:, None, None]
    ocean_fields = ocean
    for substep in range(OSTEPS):
        padded = jnp.pad(ocean_fields, ((0, 0), (1, 1), (1, 1), (1, 1)))
        ocean_fields = ocean_update(ocean_fields, padded, ocean_mask, forcing, profile, top_level)
    spectrum_next = jnp.stack([energy, jnp.zeros_like(energy)])
    ocean_next = jnp.stack([jnp.zeros_like(ocean_fields), ocean_fields])
    return spectrum_next, ocean_next
```

```python
import functools
import math

import jax
import jax.numpy as jnp
import numpy as np
from jax import lax
from jax.experimental import pallas as pl
from jax.experimental.pallas import tpu as pltpu
from jax.sharding import PartitionSpec as P

WSTEPS = 4
OSTEPS = 2
LANES = 128
SUB = 8
UNROLL = 4
AXES = ("grp", "tile", "spec")

BW, GE, GN, WE, WN, SX, SY, DX, DY, INV = range(10)

VM = pl.BlockSpec(memory_space=pltpu.VMEM)
SM = pl.BlockSpec(memory_space=pltpu.SMEM)
HB = pl.BlockSpec(memory_space=pl.ANY)


def f32(*shape):
    return jax.ShapeDtypeStruct(shape, jnp.float32)


def wave_table(freqs, dirs, parts):
    frequency = 0.04 * 1.1 ** np.arange(freqs)
    celerity = 1.56 / frequency
    group = 0.4 * 1.1 ** (-np.arange(freqs, dtype=np.float64))
    width = 0.1 * frequency * (2.0 * math.pi / dirs)
    angle = 2.0 * math.pi * (np.arange(dirs) + 0.5) / dirs
    cos, sin, one = np.cos(angle), np.sin(angle), np.ones(dirs)
    columns = [
        np.outer(width, one),
        np.outer(group, cos),
        np.outer(group, sin),
        np.outer(0.05 / celerity, cos),
        np.outer(0.05 / celerity, sin),
        np.outer(5.0 / celerity, cos),
        np.outer(5.0 / celerity, sin),
        np.outer(20.0 * frequency**3, cos),
        np.outer(20.0 * frequency**3, sin),
        np.outer(1.0 / width, one),
    ]
    table = np.zeros((parts, freqs * dirs // parts, 16), np.float32)
    for k, column in enumerate(columns):
        split = column.reshape(freqs, parts, dirs // parts).transpose(1, 0, 2)
        table[:, :, k] = split.reshape(parts, -1)
    return table


def level_table(levels, parts, own):
    depth = (np.arange(levels) + 0.5) / levels
    profile = np.exp(-2.0 * depth)
    weights = profile / profile.sum()
    table = np.zeros((parts, 3, own + 4), np.float32)
    for s in range(parts):
        table[s, 0, :own] = weights[s * own : (s + 1) * own]
        for l in range(own + 4):
            g = s * own + l - 2
            if 0 <= g < levels:
                table[s, 1, l] = profile[g]
                table[s, 2, l] = 1.0
    return table


def lanes_of(shape):
    return lax.broadcasted_iota(jnp.int32, shape, len(shape) - 1)


def wide(column):
    return jnp.broadcast_to(column, (SUB, LANES))


def half(h):
    return slice(h * LANES, (h + 1) * LANES)


def barrel(values, shift, size, left):
    bit = 1
    while bit < size:
        taken = (shift & bit) != 0
        amount = size - bit if left else bit
        values = [jnp.where(taken, pltpu.roll(v, amount, 1), v) for v in values]
        bit *= 2
    return values


def send_kernel(n, level_ref, ocean_ref, sea_ref, out_ref, rim_ref):
    t_n, s_n, rows, cols, own, ny = n
    s = lax.axis_index("spec")
    pad = -(-ny // LANES) * LANES
    parts = []
    for c in range(2):
        total = None
        for k in range(own):
            term = level_ref[s, 0, k] * ocean_ref[c, k]
            total = term if total is None else total + term
        parts.append(total)
    parts.append(jnp.where(s == 0, sea_ref[...], 0.0))
    for c in range(3):
        rim_ref[c] = jnp.where(s == 0, ocean_ref[c, own - 2 : own], ocean_ref[c, 0:2])
    stack = jnp.concatenate(parts, axis=0)
    stack = jnp.pad(stack, ((0, LANES - 3 * cols), (0, pad - ny)))
    turned = jnp.transpose(stack)
    for t in range(t_n):
        for q in range(s_n):
            out_ref[t * s_n + q] = turned[t * rows : (t + 1) * rows, : 4 * cols]


def load_kernel(n, table_ref, spectrum_ref, wind_ref, ocean_ref, sea_ref, mid_ref, lo_ref, hi_ref, growth_ref, raw, windb, sem):
    rows, fd, nx, cols, own, chunks = n
    s = lax.axis_index("spec")
    part = fd * rows // chunks
    copies = []
    halves = nx // LANES
    for c in range(chunks):
        span = pl.ds(c * part, part)
        for h in range(halves):
            copy = pltpu.make_async_copy(spectrum_ref.at[span, half(h)], raw.at[h, span], sem.at[c, h])
            copy.start()
            copies.append(copy)
    for c in range(2):
        for r in range(rows):
            windb[c, r] = jnp.broadcast_to(wind_ref[c, r : r + 1], (SUB, nx))

    def grow(i, carry):
        for k in range(2):
            sl = pl.ds(pl.multiple_of(i * 2 * SUB + k * SUB, SUB), SUB)
            we, wn = wide(table_ref[s, sl, WE : WE + 1]), wide(table_ref[s, sl, WN : WN + 1])
            for r in range(rows):
                for h in range(nx // LANES):
                    drive = we * windb[0, r, :, half(h)] + wn * windb[1, r, :, half(h)]
                    growth_ref[r, sl, half(h)] = 1.0 + jnp.maximum(drive - 0.05, 0.0)
        return carry

    lax.fori_loop(0, fd // (2 * SUB), grow, 0)
    for c in range(chunks):
        for h in range(halves):
            copies[c * halves + h].wait()
        count = fd // chunks

        def turn(i, carry):
            at = pl.multiple_of(c * count + i * SUB, SUB)
            sl = pl.ds(at, SUB)
            bw = wide(table_ref[s, sl, BW : BW + 1])
            for r in range(rows):
                for h in range(nx // LANES):
                    value = bw * raw[h, pl.ds(at * rows + r, SUB, stride=rows), :]
                    if r == 0:
                        lo_ref[sl, half(h)] = value
                    elif r == rows - 1:
                        hi_ref[sl, half(h)] = value
                    else:
                        mid_ref[r - 1, sl, half(h)] = value
            return carry

        lax.fori_loop(0, count // SUB, turn, 0)

    ny = ocean_ref.shape[1]

    @pl.when(lax.axis_index("grp") == 1)
    def _():
        stack = 3 * own
        for k in range(2):
            for ref, at in ((lo_ref, k), (hi_ref, cols - 2 + k)):
                for m in range(stack):
                    ref[k * stack + m : k * stack + m + 1, 0:ny] = ocean_ref[m * cols + at : m * cols + at + 1, :]
                ref[2 * stack + k : 2 * stack + k + 1, 0:ny] = sea_ref[at : at + 1, :]


def pick_kernel(n, got_ref, mask_ref, cross_ref, u_ref, v_ref, depth_ref, rim_ref):
    t_n, s_n, rows, cols, nx = n
    lane = lanes_of((rows, LANES))
    per = LANES // cols
    fields = [[jnp.zeros((rows, LANES), jnp.float32) for _ in range(nx // LANES)] for _ in range(3)]
    for t in range(t_n):
        tile = got_ref[(t_n + t) * s_n]
        for q in range(1, s_n):
            tile = tile + got_ref[(t_n + t) * s_n + q]
        if tile.shape[1] < LANES:
            tile = jnp.pad(tile, ((0, 0), (0, LANES - tile.shape[1])))
        h, at = t // per, (t % per) * cols
        inside = (lane >= at) & (lane < at + cols)
        for c in range(3):
            moved = pltpu.roll(tile, (at - c * cols) % LANES, 1) if (at - c * cols) % LANES else tile
            fields[c][h] = jnp.where(inside, moved, fields[c][h])
    whole = [jnp.concatenate(f, axis=1) for f in fields]
    shift = jnp.broadcast_to(cross_ref[:, 0:1], (rows, nx))
    u, v, sea = barrel(whole, shift, nx, True)
    depth = 10.0 + 4.0 * sea
    u_ref[...] = 0.1 * u
    v_ref[...] = 0.1 * v
    depth_ref[...] = 25.0 / (depth * depth)
    rim_ref[0:rows] = mask_ref[...].astype(jnp.float32)
    rim_ref[rows : 2 * rows] = 0.1 * v


def advance(segments, fd, nx, s, table_ref, energy, growth, store, splat, acc, sums):
    halves = nx // LANES
    lane = lanes_of((SUB, LANES))
    first, last = lane == 0, lane == LANES - 1
    acc[...] = jnp.zeros(acc.shape, jnp.float32)

    def body(i, carry):
        totals = {}

        def add(key, value):
            totals[key] = totals[key] + value if key in totals else value

        for k in range(UNROLL):
            sl = pl.ds(pl.multiple_of((i * UNROLL + k) * SUB, SUB), SUB)
            ge, gn = wide(table_ref[s, sl, GE : GE + 1]), wide(table_ref[s, sl, GN : GN + 1])
            bands = [wide(table_ref[s, sl, b : b + 1]) for b in (SX, SY, DX, DY)] if sums else None
            for segment in segments:
                def state(r):
                    e = [energy(r, sl, h) * splat[2, r + 1, :, half(h)] for h in range(halves)]
                    north = [(gn + splat[1, r + 1, :, half(h)]) * e[h] for h in range(halves)]
                    return e, north

                here, below = state(segment[0]), state(segment[0] - 1)
                flow = [jnp.maximum(below[1][h], 0.0) + jnp.minimum(here[1][h], 0.0) for h in range(halves)]
                for r in segment:
                    above = state(r + 1)
                    e, north = here
                    upper = [jnp.maximum(north[h], 0.0) + jnp.minimum(above[1][h], 0.0) for h in range(halves)]
                    east = [(ge + splat[0, r + 1, :, half(h)]) * e[h] for h in range(halves)]
                    left = [pltpu.roll(x, LANES - 1, 1) for x in east]
                    flux = [
                        jnp.maximum(east[h], 0.0)
                        + jnp.minimum(jnp.where(last, left[h + 1] if h + 1 < halves else 0.0, left[h]), 0.0)
                        for h in range(halves)
                    ]
                    right = [pltpu.roll(x, 1, 1) for x in flux]
                    for h in range(halves):
                        behind = jnp.where(first, right[h - 1] if h else jnp.minimum(east[0], 0.0), right[h])
                        advected = (e[h] - (flux[h] - behind)) - (upper[h] - flow[h])
                        g = growth(r, sl, h)
                        add((0, r, h), advected)
                        if sums:
                            pushed = (g - 1.0) * advected
                            grown = advected + pushed
                            for b in range(2):
                                add((1 + b, r, h), bands[b] * pushed)
                                add((3 + b, r, h), bands[2 + b] * grown)
                        else:
                            grown = g * advected
                        store(r, sl, h, grown)
                    here, flow = above, upper
        for (kind, r, h), value in totals.items():
            acc[kind, r, :, half(h)] += value
        return carry

    lax.fori_loop(0, fd // (SUB * UNROLL), body, 0)


def folded(acc, kind, rows):
    return [jnp.sum(acc[kind, r], axis=0, keepdims=True) for r in rows]


def fill(splat, kind, row, value, nx):
    splat[kind, row + 1] = jnp.broadcast_to(value, (SUB, nx))


def middle_kernel(n, begin, sums, *refs):
    rows, fd, nx = n
    table_ref, u_ref, v_ref, *refs = refs
    s = lax.axis_index("spec")
    if begin:
        rim_ref, mid_ref, lo_ref, hi_ref, growth_ref, out_ref, total_ref, splat, acc = refs
        breaking = rim_ref[0:rows]
    else:
        (rim_ref, depth_ref, own_ref, got_ref, mid_ref, lo_ref, hi_ref, growth_ref,
         out_ref, total_ref, breaking_ref, splat, acc) = refs
        wet = rim_ref[0:rows]
        breaking = wet / (1.0 + (own_ref[...] + got_ref[...]) * depth_ref[...])
        breaking_ref[...] = breaking
    for r in range(rows):
        fill(splat, 0, r, u_ref[r : r + 1], nx)
        fill(splat, 1, r, v_ref[r : r + 1], nx)
        fill(splat, 2, r, breaking[r : r + 1], nx)

    def energy(r, sl, h):
        if r == 0:
            return lo_ref[sl, half(h)]
        if r == rows - 1:
            return hi_ref[sl, half(h)]
        return mid_ref[r - 1, sl, half(h)]

    def store(r, sl, h, value):
        out_ref[r - 1, sl, half(h)] = value

    inner = list(range(1, rows - 1))
    advance([inner], fd, nx, s, table_ref, energy, lambda r, sl, h: growth_ref[r, sl, half(h)], store, splat, acc, sums)
    zero = jnp.zeros((1, nx), jnp.float32)
    for kind in range(acc.shape[0]):
        total_ref[kind] = jnp.concatenate([zero] + folded(acc, kind, inner) + [zero], axis=0)


def edge_kernel(n, begin, sums, *refs):
    rows, fd, nx, t_n, s_n, cols, own = n
    (table_ref, u_ref, v_ref, breaking_ref, below_ref, above_ref, vb_ref, va_ref, rim_ref, mid_ref, lo_ref, hi_ref,
     hb_ref, ha_ref, growth_ref, part_ref, *refs) = refs
    s = lax.axis_index("spec")
    if begin:
        level_ref, newlo_ref, newhi_ref, total_ref, splat, acc = refs
    elif sums:
        cross_ref, newlo_ref, newhi_ref, send_ref, splat, acc = refs
    else:
        newlo_ref, newhi_ref, total_ref, splat, acc = refs
    for r in (0, 1, rows - 2, rows - 1):
        fill(splat, 0, r, u_ref[r : r + 1], nx)
        fill(splat, 1, r, v_ref[r : r + 1], nx)
        fill(splat, 2, r, breaking_ref[r : r + 1], nx)
    fill(splat, 1, -1, vb_ref[2 * rows - 1 : 2 * rows], nx)
    fill(splat, 2, -1, below_ref[rows - 1 : rows], nx)
    fill(splat, 1, rows, va_ref[rows : rows + 1], nx)
    fill(splat, 2, rows, above_ref[0:1], nx)

    def energy(r, sl, h):
        if r == -1:
            return hb_ref[sl, half(h)]
        if r == rows:
            return ha_ref[sl, half(h)]
        if r == 0:
            return lo_ref[sl, half(h)]
        if r == rows - 1:
            return hi_ref[sl, half(h)]
        return mid_ref[r - 1, sl, half(h)]

    def store(r, sl, h, value):
        (newlo_ref if r == 0 else newhi_ref)[sl, half(h)] = value

    advance([[0], [rows - 1]], fd, nx, s, table_ref, energy, lambda r, sl, h: growth_ref[r, sl, half(h)], store, splat, acc, sums)
    zero = jnp.zeros((rows - 2, nx), jnp.float32)
    kinds = []
    for kind in range(acc.shape[0]):
        low, high = folded(acc, kind, (0, rows - 1))
        kinds.append(part_ref[kind] + jnp.concatenate([low, zero, high], axis=0))
    if not sums:
        total_ref[...] = kinds[0]
    if begin:
        ny = level_ref.shape[1]

        @pl.when(lax.axis_index("grp") == 1)
        def _():
            for k in range(2):
                for ref, at in ((newlo_ref, k), (newhi_ref, cols - 2 + k)):
                    for c in range(6):
                        ref[k * SUB + c : k * SUB + c + 1, 0:ny] = level_ref[c * cols + at : c * cols + at + 1, :]

    if sums:
        wet = jnp.where(s == 0, rim_ref[0:rows], 0.0)
        shift = jnp.broadcast_to(cross_ref[:, 0:1], (rows, nx))
        moved = barrel(kinds + [wet], shift, nx, False)
        lane = lanes_of((rows, nx))
        size = cols + 8
        for t in range(t_n):
            chunk = jnp.zeros((rows, nx), jnp.float32)
            for q, value in enumerate(moved):
                amount = (q * size - (cols * t - 4)) % nx
                piece = pltpu.roll(value, amount, 1) if amount else value
                chunk = jnp.where((lane >= q * size) & (lane < (q + 1) * size), piece, chunk)
            for q in range(s_n):
                send_ref[(t_n + t) * s_n + q] = chunk
        mine = lax.axis_index("tile")
        for q in range(s_n):
            send_ref[mine * s_n + q] = kinds[0]


def last_kernel(n, table_ref, level_ref, got_ref, rim_ref, depth_ref, mid_ref, lo_ref, hi_ref, ocean_ref, sea_ref,
                hb_ref, ha_ref, cb_ref, ca_ref, lev_ref, waves_ref, next_ref,
                raw, brk, turn, field, mix, out, sem, osem):
    rows, fd, nx, t_n, s_n, cols, own, ny, chunks = n
    s = lax.axis_index("spec")
    g = lax.axis_index("grp")
    tile = lax.axis_index("tile")
    part = fd * rows // chunks
    count = fd // chunks
    pad = turn.shape[0]
    size = cols + 8

    halves = nx // LANES

    def writes(c, source):
        return [
            pltpu.make_async_copy(
                raw.at[h, pl.ds(source * part, part)], waves_ref.at[pl.ds(c * part, part), half(h)], sem.at[c, h])
            for h in range(halves)
        ]

    ocean_copy = pltpu.make_async_copy(out, next_ref, osem)

    @pl.when(g == 0)
    def _():
        total = got_ref[tile * s_n]
        for q in range(1, s_n):
            total = total + got_ref[tile * s_n + q]
        breaking = rim_ref[0:rows] / (1.0 + total * depth_ref[...])
        for r in range(rows):
            brk[r] = jnp.broadcast_to(breaking[r : r + 1], (SUB, nx))
        for c in range(chunks):

            def finish(i, carry):
                at = pl.multiple_of(c * count + i * SUB, SUB)
                sl = pl.ds(at, SUB)
                inv = wide(table_ref[s, sl, INV : INV + 1])
                for r in range(rows):
                    for h in range(nx // LANES):
                        if r == 0:
                            value = lo_ref[sl, half(h)]
                        elif r == rows - 1:
                            value = hi_ref[sl, half(h)]
                        else:
                            value = mid_ref[r - 1, sl, half(h)]
                        raw[h, pl.ds(at * rows + r, SUB, stride=rows), :] = value * brk[r, :, half(h)] * inv
                return carry

            lax.fori_loop(0, count // SUB, finish, 0)
            for copy in writes(c, c):
                copy.start()
        out[...] = jnp.zeros((3, own, cols, ny), jnp.float32)
        ocean_copy.start()
        ocean_copy.wait()
        for c in range(chunks):
            for copy in writes(c, c):
                copy.wait()

    @pl.when(g == 1)
    def _():
        def clear(i, carry):
            for h in range(halves):
                raw[h, pl.ds(pl.multiple_of(i * 64, 64), 64), :] = jnp.zeros((64, LANES), jnp.float32)
            return carry

        lax.fori_loop(0, part // 64, clear, 0)
        for c in range(chunks):
            for copy in writes(c, 0):
                copy.start()

        if pad > ny:
            turn[ny:pad] = jnp.zeros((pad - ny, nx), jnp.float32)
        for t in range(t_n):
            tilev = got_ref[t * s_n]
            for q in range(1, s_n):
                tilev = tilev + got_ref[t * s_n + q]
            turn[t * rows : (t + 1) * rows] = tilev
        turned = jnp.transpose(turn[...])
        total, sx, sy, dx, dy, wet = [turned[q * size : (q + 1) * size] for q in range(6)]
        row = lax.broadcasted_iota(jnp.int32, (size, pad), 0)
        column = row + (tile * cols - 4)
        wet = jnp.where((column >= 0) & (column < t_n * cols), wet, 0.0)
        stack = 3 * own
        mix[0] = jnp.zeros((size, pad), jnp.float32)
        mix[0, 4 : 4 + cols, 0:ny] = sea_ref[...]
        mix[0, 2:4, 0:ny] = hb_ref[2 * stack : 2 * stack + 2, 0:ny]
        mix[0, 4 + cols : 6 + cols, 0:ny] = ha_ref[2 * stack : 2 * stack + 2, 0:ny]
        depth = 10.0 + 4.0 * mix[0]
        breaking = 1.0 / (1.0 + 25.0 * total / (depth * depth))
        swept = wet * breaking
        sx, sy, dx, dy = sx * breaking, sy * breaking, dx * swept, dy * swept

        field[...] = jnp.zeros(field.shape, jnp.float32)
        ext = own + 4
        for c in range(3):
            for k in range(own):
                l = c * ext + 2 + k
                field[l, 4 : 4 + cols, 0:ny] = ocean_ref[c, k]
                for m in range(2):
                    at = m * stack + c * own + k
                    field[l, 2 + m : 3 + m, 0:ny] = hb_ref[at : at + 1, 0:ny]
                    field[l, 4 + cols + m : 5 + cols + m, 0:ny] = ha_ref[at : at + 1, 0:ny]
        for upper in range(2):
            @pl.when(s == 1 - upper)
            def _():
                for c in range(3):
                    for k in range(2):
                        l = c * ext + (own + 2 if upper else 0) + k
                        at = (c * 2 + k) * cols
                        field[l, 4 : 4 + cols, 0:ny] = lev_ref[at : at + cols, :]
                        for m in range(2):
                            at = m * SUB + c * 2 + k
                            field[l, 2 + m : 3 + m, 0:ny] = cb_ref[at : at + 1, 0:ny]
                            field[l, 4 + cols + m : 5 + cols + m, 0:ny] = ca_ref[at : at + 1, 0:ny]

        lane = lanes_of((size, pad))

        def new_fields(source, k):
            values = []
            for c in range(3):
                q = source[c * ext + k]
                lateral = (
                    pltpu.roll(q, size - 1, 0)
                    + pltpu.roll(q, 1, 0)
                    + jnp.where(lane == ny - 1, 0.0, pltpu.roll(q, pad - 1, 1))
                    + jnp.where(lane == 0, 0.0, pltpu.roll(q, 1, 1))
                    - 4.0 * q
                )
                vertical = source[c * ext + k + 1] + source[c * ext + k - 1] - 2.0 * q
                values.append((q, q + 0.1 * lateral + 0.2 * vertical))
            (u, du), (v, dv), (_, dt) = values
            shaped = level_ref[s, 1, k]
            top = jnp.where((s == 0) & (k == 2), 1.0, 0.0)
            east = du + 0.1 * (v + shaped * dy) + top * sx
            north = dv - 0.1 * (u + shaped * dx) + top * sy
            keep = wet * level_ref[s, 2, k]
            return keep * east, keep * north, keep * dt

        for k in range(1, ext - 1):
            for c, value in enumerate(new_fields(field, k)):
                mix[c * ext + k] = value
        for k in range(2, ext - 2):
            for c, value in enumerate(new_fields(mix, k)):
                out[c, k - 2] = value[4 : 4 + cols, 0:ny]
        ocean_copy.start()
        ocean_copy.wait()
        for c in range(chunks):
            for copy in writes(c, 0):
                copy.wait()


def body(spectrum, wind, land_mask, intersection, ocean_state, sea_level, *, mesh_shape):
    g_n, t_n, s_n = (mesh_shape[a] for a in AXES)
    _, freqs, dirs, rows, nx = spectrum.shape
    _, _, own, cols, ny = ocean_state.shape
    fd = freqs * dirs
    devices = g_n * t_n * s_n
    table = jnp.asarray(wave_table(freqs, dirs * s_n, s_n))
    levels = jnp.asarray(level_table(own * s_n, s_n, own))
    ocean = ocean_state[0]
    sea = sea_level[0]
    natural = spectrum.reshape(fd * rows, nx)
    flat = ocean_state.reshape(3 * own * cols, ny)
    chunks = 8
    params = pltpu.CompilerParams(vmem_limit_bytes=24 << 20)

    def up(x):
        return lax.ppermute(x, "tile", [(i, i + 1) for i in range(t_n - 1)])

    def down(x):
        return lax.ppermute(x, "tile", [(i + 1, i) for i in range(t_n - 1)])

    def others(x):
        result = None
        for k in range(1, s_n):
            got = lax.ppermute(x, "spec", [(i, (i + k) % s_n) for i in range(s_n)])
            result = got if result is None else result + got
        return result

    send, level_rim = pl.pallas_call(
        functools.partial(send_kernel, (t_n, s_n, rows, cols, own, ny)),
        out_shape=(f32(devices, rows, 4 * cols), f32(3, 2, cols, ny)),
        in_specs=[SM, VM, VM], out_specs=(VM, VM), compiler_params=params, name="send",
    )(levels, ocean, sea)
    arrived = lax.all_to_all(send, AXES, 0, 0, tiled=True)

    mid, lo, hi, growth = pl.pallas_call(
        functools.partial(load_kernel, (rows, fd, nx, cols, own, chunks)),
        out_shape=(f32(rows - 2, fd, nx), f32(fd, nx), f32(fd, nx), f32(rows, fd, nx)),
        in_specs=[VM, HB, VM, VM, VM], out_specs=(VM,) * 4,
        scratch_shapes=[pltpu.VMEM((nx // LANES, fd * rows, LANES), jnp.float32), pltpu.VMEM((2, rows, SUB, nx), jnp.float32),
                        pltpu.SemaphoreType.DMA((chunks, nx // LANES))],
        compiler_params=params, name="load",
    )(table, natural, wind, flat, sea)
    hb, ha = up(hi), down(lo)
    level_got = others(level_rim).reshape(6 * cols, ny)
    hb0, ha0 = hb, ha

    u, v, depth, rim = pl.pallas_call(
        functools.partial(pick_kernel, (t_n, s_n, rows, cols, nx)),
        out_shape=(f32(rows, nx), f32(rows, nx), f32(rows, nx), f32(2 * rows, nx)),
        in_specs=[VM] * 3, out_specs=(VM,) * 4, compiler_params=params, name="pick",
    )(arrived, land_mask, intersection)
    vb, va = up(rim), down(rim)

    breaking, below, above = rim, vb, va
    total = got = None
    for step in range(WSTEPS):
        begin, sums = step == 0, step == WSTEPS - 1
        kinds = 5 if sums else 1
        scratch = [pltpu.VMEM((3, rows + 2, SUB, nx), jnp.float32), pltpu.VMEM((kinds, rows, SUB, nx), jnp.float32)]
        shape = (f32(rows - 2, fd, nx), f32(kinds, rows, nx))
        args = (table, u, v, rim)
        if not begin:
            shape += (f32(rows, nx),)
            args += (depth, total, got)
        args += (mid, lo, hi, growth)
        outs = pl.pallas_call(
            functools.partial(middle_kernel, (rows, fd, nx), begin, sums),
            out_shape=shape, in_specs=[VM] * len(args), out_specs=(VM,) * len(shape),
            scratch_shapes=scratch, compiler_params=params, name=f"middle{step}",
        )(*args)
        if begin:
            newmid, partial = outs
        else:
            newmid, partial, breaking = outs
            below, above = up(breaking), down(breaking)
        args = (table, u, v, breaking, below, above, vb, va, rim, mid, lo, hi, hb, ha, growth, partial)
        if begin:
            args += (level_got,)
        if sums:
            args += (intersection,)
            shape = (f32(fd, nx), f32(fd, nx), f32(devices, rows, nx))
        else:
            shape = (f32(fd, nx), f32(fd, nx), f32(rows, nx))
        newlo, newhi, total = pl.pallas_call(
            functools.partial(edge_kernel, (rows, fd, nx, t_n, s_n, cols, own), begin, sums),
            out_shape=shape, in_specs=[VM] * len(args), out_specs=(VM,) * 3,
            scratch_shapes=scratch, compiler_params=params, name=f"edge{step}",
        )(*args)
        mid, lo, hi = newmid, newlo, newhi
        if not sums:
            got = others(total)
            hb, ha = up(hi), down(lo)
        if begin:
            hb1, ha1 = hb, ha

    landed = lax.all_to_all(total, AXES, 0, 0, tiled=True)
    pad = -(-ny // LANES) * LANES
    size = cols + 8
    ins = (table, levels, landed, rim, depth, mid, lo, hi, ocean, sea, hb0, ha0, hb1, ha1, level_got)
    waves, fields = pl.pallas_call(
        functools.partial(last_kernel, (rows, fd, nx, t_n, s_n, cols, own, ny, chunks)),
        out_shape=(f32(fd * rows, nx), f32(3, own, cols, ny)),
        in_specs=[VM, SM] + [VM] * (len(ins) - 2), out_specs=(HB, HB),
        scratch_shapes=[
            pltpu.VMEM((nx // LANES, fd * rows, LANES), jnp.float32),
            pltpu.VMEM((rows, SUB, nx), jnp.float32),
            pltpu.VMEM((pad, nx), jnp.float32),
            pltpu.VMEM((3 * (own + 4), size, pad), jnp.float32),
            pltpu.VMEM((3 * (own + 4), size, pad), jnp.float32),
            pltpu.VMEM((3, own, cols, ny), jnp.float32),
            pltpu.SemaphoreType.DMA((chunks, nx // LANES)),
            pltpu.SemaphoreType.DMA,
        ],
        compiler_params=params, name="last",
    )(*ins)
    return waves.reshape(spectrum.shape), fields.reshape(ocean_state.shape)


def solution(mesh):
    return jax.shard_map(
        functools.partial(body, mesh_shape=dict(mesh.shape)),
        mesh=mesh,
        in_specs=(
            P("grp", None, "spec", "tile", None),
            P(None, "tile", None),
            P("tile", None),
            P("tile", None),
            P("grp", None, "spec", "tile", None),
            P("grp", "tile", None),
        ),
        out_specs=(P("grp", None, "spec", "tile", None), P("grp", None, "spec", "tile", None)),
        check_vma=False,
    )
```

```python
import functools
import math

import jax
import jax.numpy as jnp
import numpy as np
from jax import lax
from jax.experimental import pallas as pl
from jax.experimental.pallas import tpu as pltpu
from jax.sharding import PartitionSpec as P

WSTEPS = 4
OSTEPS = 2
LANES = 128
SUB = 8
UNROLL = 4
AXES = ("grp", "tile", "spec")

BW, GE, GN, WE, WN, SX, SY, DX, DY, INV = range(10)

VM = pl.BlockSpec(memory_space=pltpu.VMEM)
SM = pl.BlockSpec(memory_space=pltpu.SMEM)
HB = pl.BlockSpec(memory_space=pltpu.HBM)


def f32(*shape):
    return jax.ShapeDtypeStruct(shape, jnp.float32)


def wave_table(freqs, dirs, parts):
    frequency = 0.04 * 1.1 ** np.arange(freqs)
    celerity = 1.56 / frequency
    group = 0.4 * 1.1 ** (-np.arange(freqs, dtype=np.float64))
    width = 0.1 * frequency * (2.0 * math.pi / dirs)
    angle = 2.0 * math.pi * (np.arange(dirs) + 0.5) / dirs
    cos, sin, one = np.cos(angle), np.sin(angle), np.ones(dirs)
    columns = [
        np.outer(width, one),
        np.outer(group, cos),
        np.outer(group, sin),
        np.outer(0.05 / celerity, cos),
        np.outer(0.05 / celerity, sin),
        np.outer(5.0 / celerity, cos),
        np.outer(5.0 / celerity, sin),
        np.outer(20.0 * frequency**3, cos),
        np.outer(20.0 * frequency**3, sin),
        np.outer(1.0 / width, one),
    ]
    table = np.zeros((parts, freqs * dirs // parts, 16), np.float32)
    for k, column in enumerate(columns):
        split = column.reshape(freqs, parts, dirs // parts).transpose(1, 0, 2)
        table[:, :, k] = split.reshape(parts, -1)
    return table


def level_table(levels, parts, own):
    depth = (np.arange(levels) + 0.5) / levels
    profile = np.exp(-2.0 * depth)
    weights = profile / profile.sum()
    table = np.zeros((parts, 3, own + 4), np.float32)
    for s in range(parts):
        table[s, 0, :own] = weights[s * own : (s + 1) * own]
        for l in range(own + 4):
            g = s * own + l - 2
            if 0 <= g < levels:
                table[s, 1, l] = profile[g]
                table[s, 2, l] = 1.0
    return table


def lanes_of(shape):
    return lax.broadcasted_iota(jnp.int32, shape, len(shape) - 1)


def wide(column):
    return jnp.broadcast_to(column, (SUB, LANES))


def half(h):
    return slice(h * LANES, (h + 1) * LANES)


def barrel(values, shift, size, left):
    bit = 1
    while bit < size:
        taken = (shift & bit) != 0
        amount = size - bit if left else bit
        values = [jnp.where(taken, pltpu.roll(v, amount, 1), v) for v in values]
        bit *= 2
    return values


def start_kernel(n, level_ref, spectrum_ref, ocean_hbm, sea_hbm, out_ref, rim_ref, lo_ref, hi_ref, raw, ocean, sea, sem):
    t_n, s_n, rows, cols, own, ny, fd, nx, chunks = n
    s = lax.axis_index("spec")
    pad = -(-ny // LANES) * LANES
    part = fd // chunks
    first = [
        pltpu.make_async_copy(ocean_hbm, ocean, sem.at[chunks]),
        pltpu.make_async_copy(sea_hbm, sea, sem.at[chunks + 1]),
    ]
    copies = [
        pltpu.make_async_copy(spectrum_ref.at[pl.ds(c * part, part)], raw.at[pl.ds(c * part, part)], sem.at[c])
        for c in range(chunks)
    ]
    for copy in first + copies:
        copy.start()
    for copy in first:
        copy.wait()
    parts = []
    for c in range(2):
        total = None
        for k in range(own):
            term = level_ref[s, 0, k] * ocean[c * own + k]
            total = term if total is None else total + term
        parts.append(total)
    parts.append(jnp.where(s == 0, sea[...], 0.0))
    for c in range(3):
        for k in range(2):
            rim_ref[c, k] = jnp.where(s == 0, ocean[c * own + own - 2 + k], ocean[c * own + k])
    stack = jnp.concatenate(parts, axis=0)
    stack = jnp.pad(stack, ((0, LANES - 3 * cols), (0, pad - ny)))
    turned = jnp.transpose(stack)
    for t in range(t_n):
        for q in range(s_n):
            out_ref[t * s_n + q] = turned[t * rows : (t + 1) * rows, : 4 * cols]

    for c in range(chunks):
        copies[c].wait()

        def turn(i, carry):
            sl = pl.ds(pl.multiple_of(c * part + i * SUB, SUB), SUB)
            for h in range(nx // LANES):
                planes = jnp.swapaxes(raw[sl, :, half(h)], 0, 1)
                lo_ref[sl, half(h)] = planes[0]
                hi_ref[sl, half(h)] = planes[rows - 1]
            return carry

        lax.fori_loop(0, part // SUB, turn, 0)

    @pl.when(lax.axis_index("grp") == 1)
    def _():
        stack = 3 * own
        for k in range(2):
            for ref, at in ((lo_ref, k), (hi_ref, cols - 2 + k)):
                for m in range(stack):
                    ref[k * stack + m : k * stack + m + 1, 0:ny] = ocean[m, at : at + 1, :]
                ref[2 * stack + k : 2 * stack + k + 1, 0:ny] = sea[at : at + 1, :]


def pick_kernel(n, got_ref, mask_ref, cross_ref, u_ref, v_ref, depth_ref, rim_ref):
    t_n, s_n, rows, cols, nx = n
    lane = lanes_of((rows, LANES))
    per = LANES // cols
    fields = [[jnp.zeros((rows, LANES), jnp.float32) for _ in range(nx // LANES)] for _ in range(3)]
    for t in range(t_n):
        tile = got_ref[(t_n + t) * s_n]
        for q in range(1, s_n):
            tile = tile + got_ref[(t_n + t) * s_n + q]
        if tile.shape[1] < LANES:
            tile = jnp.pad(tile, ((0, 0), (0, LANES - tile.shape[1])))
        h, at = t // per, (t % per) * cols
        inside = (lane >= at) & (lane < at + cols)
        for c in range(3):
            moved = pltpu.roll(tile, (at - c * cols) % LANES, 1) if (at - c * cols) % LANES else tile
            fields[c][h] = jnp.where(inside, moved, fields[c][h])
    whole = [jnp.concatenate(f, axis=1) for f in fields]
    shift = jnp.broadcast_to(cross_ref[:, 0:1], (rows, nx))
    u, v, sea = barrel(whole, shift, nx, True)
    depth = 10.0 + 4.0 * sea
    u_ref[...] = 0.1 * u
    v_ref[...] = 0.1 * v
    depth_ref[...] = 25.0 / (depth * depth)
    rim_ref[0:rows] = mask_ref[...].astype(jnp.float32)
    rim_ref[rows : 2 * rows] = 0.1 * v
    rim_ref[2 * rows : 3 * rows] = 25.0 / (depth * depth)


def advance(segments, fd, nx, s, table_ref, planes, store, splat, acc, sums, before=None):
    halves = nx // LANES
    lane = lanes_of((SUB, LANES))
    first, last = lane == 0, lane == LANES - 1
    acc[...] = jnp.zeros(acc.shape, jnp.float32)

    def body(i, carry):
        if before is not None:
            before(i)
        totals = {}

        def add(key, value):
            totals[key] = totals[key] + value if key in totals else value

        for k in range(UNROLL):
            sl = pl.ds(pl.multiple_of((i * UNROLL + k) * SUB, SUB), SUB)
            ge, gn = wide(table_ref[s, sl, GE : GE + 1]), wide(table_ref[s, sl, GN : GN + 1])
            bands = [wide(table_ref[s, sl, b : b + 1]) for b in (SX, SY, DX, DY)] if sums else None
            energy, growth = planes(sl)
            for segment in segments:
                def state(r):
                    e = [energy(r, h) * splat[2, r + 1, :, half(h)] for h in range(halves)]
                    north = [(gn + splat[1, r + 1, :, half(h)]) * e[h] for h in range(halves)]
                    return e, north

                here, below = state(segment[0]), state(segment[0] - 1)
                flow = [jnp.maximum(below[1][h], 0.0) + jnp.minimum(here[1][h], 0.0) for h in range(halves)]
                for r in segment:
                    above = state(r + 1)
                    e, north = here
                    upper = [jnp.maximum(north[h], 0.0) + jnp.minimum(above[1][h], 0.0) for h in range(halves)]
                    east = [(ge + splat[0, r + 1, :, half(h)]) * e[h] for h in range(halves)]
                    left = [pltpu.roll(x, LANES - 1, 1) for x in east]
                    flux = [
                        jnp.maximum(east[h], 0.0)
                        + jnp.minimum(jnp.where(last, left[h + 1] if h + 1 < halves else 0.0, left[h]), 0.0)
                        for h in range(halves)
                    ]
                    right = [pltpu.roll(x, 1, 1) for x in flux]
                    for h in range(halves):
                        behind = jnp.where(first, right[h - 1] if h else jnp.minimum(east[0], 0.0), right[h])
                        advected = (e[h] - (flux[h] - behind)) - (upper[h] - flow[h])
                        g = growth(r, h)
                        add((0, r, h), advected)
                        if sums:
                            pushed = (g - 1.0) * advected
                            grown = advected + pushed
                            for b in range(2):
                                add((1 + b, r, h), bands[b] * pushed)
                                add((3 + b, r, h), bands[2 + b] * grown)
                        else:
                            grown = g * advected
                        store(r, sl, h, grown)
                    here, flow = above, upper
        for (kind, r, h), value in totals.items():
            acc[kind, r, :, half(h)] += value
        return carry

    lax.fori_loop(0, fd // (SUB * UNROLL), body, 0)


def folded(acc, kind, rows):
    return [jnp.sum(acc[kind, r], axis=0, keepdims=True) for r in rows]


def fill(splat, kind, row, value, nx):
    splat[kind, row + 1] = jnp.broadcast_to(value, (SUB, nx))


def first_middle_kernel(n, table_ref, u_ref, v_ref, rim_ref, wind_ref, spectrum_ref,
                        out_ref, total_ref, growth_ref, inner_ref, raw, windb, splat, acc, sem):
    rows, fd, nx, chunks = n
    s = lax.axis_index("spec")
    part = fd // chunks
    turns = part // (SUB * UNROLL)

    def copy(c):
        span = pl.ds(pl.multiple_of(c * part, SUB), part)
        return pltpu.make_async_copy(spectrum_ref.at[span], raw.at[span], sem.at[c])

    for c in range(chunks):
        copy(c).start()
    for c in range(2):
        for r in range(rows):
            windb[c, r] = jnp.broadcast_to(wind_ref[c, r : r + 1], (SUB, nx))
    for r in range(rows):
        fill(splat, 0, r, u_ref[r : r + 1], nx)
        fill(splat, 1, r, v_ref[r : r + 1], nx)
        fill(splat, 2, r, rim_ref[r : r + 1], nx)

    def before(i):
        @pl.when(i % turns == 0)
        def _():
            copy(i // turns).wait()

    def planes(sl):
        bw, we, wn = [wide(table_ref[s, sl, b : b + 1]) for b in (BW, WE, WN)]
        natural, grown = {}, {}
        for h in range(nx // LANES):
            natural[h] = jnp.swapaxes(raw[sl, :, half(h)], 0, 1)
            inner_ref[0, sl, half(h)] = natural[h][1]
            inner_ref[1, sl, half(h)] = natural[h][rows - 2]
            for r in range(rows):
                drive = we * windb[0, r, :, half(h)] + wn * windb[1, r, :, half(h)]
                grown[r, h] = 1.0 + jnp.maximum(drive - 0.05, 0.0)
                growth_ref[r, sl, half(h)] = grown[r, h]
        return lambda r, h: bw * natural[h][r], lambda r, h: grown[r, h]

    def store(r, sl, h, value):
        out_ref[r - 1, sl, half(h)] = value

    inner = list(range(1, rows - 1))
    advance([inner], fd, nx, s, table_ref, planes, store, splat, acc, False, before)
    finish_middle(inner, nx, acc, total_ref)


def finish_middle(inner, nx, acc, total_ref):
    zero = jnp.zeros((1, nx), jnp.float32)
    for kind in range(acc.shape[0]):
        total_ref[kind] = jnp.concatenate([zero] + folded(acc, kind, inner) + [zero], axis=0)


def middle_kernel(n, sums, table_ref, u_ref, v_ref, rim_ref, depth_ref, own_ref, got_ref, mid_ref, lo_ref, hi_ref,
                  growth_ref, out_ref, total_ref, breaking_ref, splat, acc):
    rows, fd, nx = n
    s = lax.axis_index("spec")
    breaking = rim_ref[0:rows] / (1.0 + (own_ref[...] + got_ref[...]) * depth_ref[...])
    breaking_ref[...] = breaking
    for r in range(rows):
        fill(splat, 0, r, u_ref[r : r + 1], nx)
        fill(splat, 1, r, v_ref[r : r + 1], nx)
        fill(splat, 2, r, breaking[r : r + 1], nx)

    def planes(sl):
        def energy(r, h):
            if r == 0:
                return lo_ref[sl, half(h)]
            if r == rows - 1:
                return hi_ref[sl, half(h)]
            return mid_ref[r - 1, sl, half(h)]

        return energy, lambda r, h: growth_ref[r, sl, half(h)]

    def store(r, sl, h, value):
        out_ref[r - 1, sl, half(h)] = value

    inner = list(range(1, rows - 1))
    advance([inner], fd, nx, s, table_ref, planes, store, splat, acc, sums)
    finish_middle(inner, nx, acc, total_ref)


def edge_kernel(n, begin, sums, *refs):
    rows, fd, nx, t_n, s_n, cols, own = n
    (table_ref, u_ref, v_ref, breaking_ref, vb_ref, va_ref, rim_ref, mid_ref, lo_ref, hi_ref,
     hb_ref, ha_ref, growth_ref, part_ref, *refs) = refs
    s = lax.axis_index("spec")
    if begin:
        level_ref, newlo_ref, newhi_ref, total_ref, splat, acc = refs
    elif sums:
        cb_ref, ca_ref, cross_ref, newlo_ref, newhi_ref, send_ref, splat, acc = refs
    else:
        cb_ref, ca_ref, newlo_ref, newhi_ref, total_ref, splat, acc = refs
    for r in (0, 1, rows - 2, rows - 1):
        fill(splat, 0, r, u_ref[r : r + 1], nx)
        fill(splat, 1, r, v_ref[r : r + 1], nx)
        fill(splat, 2, r, breaking_ref[r : r + 1], nx)
    below, above = vb_ref[rows - 1 : rows], va_ref[0:1]
    if not begin:
        low = hb_ref[fd : fd + 1] + cb_ref[rows - 1 : rows]
        high = ha_ref[fd : fd + 1] + ca_ref[0:1]
        below = below / (1.0 + low * vb_ref[3 * rows - 1 : 3 * rows])
        above = above / (1.0 + high * va_ref[2 * rows : 2 * rows + 1])
    fill(splat, 1, -1, vb_ref[2 * rows - 1 : 2 * rows], nx)
    fill(splat, 2, -1, below, nx)
    fill(splat, 1, rows, va_ref[rows : rows + 1], nx)
    fill(splat, 2, rows, above, nx)

    def planes(sl):
        bw = wide(table_ref[s, sl, BW : BW + 1]) if begin else None

        def plane(r, h):
            if r == -1:
                return hb_ref[sl, half(h)]
            if r == rows:
                return ha_ref[sl, half(h)]
            if r == 0:
                return lo_ref[sl, half(h)]
            if r == rows - 1:
                return hi_ref[sl, half(h)]
            return mid_ref[(0 if r == 1 else 1) if begin else r - 1, sl, half(h)]

        def energy(r, h):
            return bw * plane(r, h) if begin else plane(r, h)

        return energy, lambda r, h: growth_ref[r, sl, half(h)]

    def store(r, sl, h, value):
        (newlo_ref if r == 0 else newhi_ref)[sl, half(h)] = value

    advance([[0], [rows - 1]], fd, nx, s, table_ref, planes, store, splat, acc, sums)
    zero = jnp.zeros((rows - 2, nx), jnp.float32)
    kinds = []
    for kind in range(acc.shape[0]):
        low, high = folded(acc, kind, (0, rows - 1))
        kinds.append(part_ref[kind] + jnp.concatenate([low, zero, high], axis=0))
    if not sums:
        total_ref[...] = kinds[0]
        newlo_ref[fd : fd + SUB] = jnp.broadcast_to(kinds[0][0:1], (SUB, nx))
        newhi_ref[fd : fd + SUB] = jnp.broadcast_to(kinds[0][rows - 1 : rows], (SUB, nx))
    if begin:
        ny = level_ref.shape[1]

        @pl.when(lax.axis_index("grp") == 1)
        def _():
            for k in range(2):
                for ref, at in ((newlo_ref, k), (newhi_ref, cols - 2 + k)):
                    for c in range(6):
                        ref[k * SUB + c : k * SUB + c + 1, 0:ny] = level_ref[c * cols + at : c * cols + at + 1, :]

    if sums:
        wet = jnp.where(s == 0, rim_ref[0:rows], 0.0)
        shift = jnp.broadcast_to(cross_ref[:, 0:1], (rows, nx))
        moved = barrel(kinds + [wet], shift, nx, False)
        lane = lanes_of((rows, nx))
        size = cols + 8
        for t in range(t_n):
            chunk = jnp.zeros((rows, nx), jnp.float32)
            for q, value in enumerate(moved):
                amount = (q * size - (cols * t - 4)) % nx
                piece = pltpu.roll(value, amount, 1) if amount else value
                chunk = jnp.where((lane >= q * size) & (lane < (q + 1) * size), piece, chunk)
            for q in range(s_n):
                send_ref[(t_n + t) * s_n + q] = chunk
        mine = lax.axis_index("tile")
        for q in range(s_n):
            send_ref[mine * s_n + q] = kinds[0]


def last_kernel(n, table_ref, level_ref, got_ref, rim_ref, depth_ref, mid_ref, lo_ref, hi_ref, ocean_ref, sea_ref,
                hb_ref, ha_ref, cb_ref, ca_ref, lev_ref, waves_ref, next_ref,
                raw, brk, turn, field, mix, out, sem, osem):
    rows, fd, nx, t_n, s_n, cols, own, ny, chunks = n
    s = lax.axis_index("spec")
    g = lax.axis_index("grp")
    tile = lax.axis_index("tile")
    part = fd // chunks
    pad = turn.shape[0]
    size = cols + 8

    def write(c, source):
        return pltpu.make_async_copy(raw.at[pl.ds(source * part, part)], waves_ref.at[pl.ds(c * part, part)], sem.at[c])

    ocean_copy = pltpu.make_async_copy(out, next_ref, osem)

    @pl.when(g == 0)
    def _():
        total = got_ref[tile * s_n]
        for q in range(1, s_n):
            total = total + got_ref[tile * s_n + q]
        breaking = rim_ref[0:rows] / (1.0 + total * depth_ref[...])
        for r in range(rows):
            brk[r] = jnp.broadcast_to(breaking[r : r + 1], (SUB, nx))
        for c in range(chunks):

            def finish(i, carry):
                sl = pl.ds(pl.multiple_of(c * part + i * SUB, SUB), SUB)
                inv = wide(table_ref[s, sl, INV : INV + 1])
                for h in range(nx // LANES):
                    values = [lo_ref[sl, half(h)]]
                    values += [mid_ref[r, sl, half(h)] for r in range(rows - 2)]
                    values += [hi_ref[sl, half(h)]]
                    values = [value * brk[r, :, half(h)] * inv for r, value in enumerate(values)]
                    raw[sl, :, half(h)] = jnp.swapaxes(jnp.stack(values), 0, 1)
                return carry

            lax.fori_loop(0, part // SUB, finish, 0)
            write(c, c).start()
        out[...] = jnp.zeros((3, own, cols, ny), jnp.float32)
        ocean_copy.start()
        ocean_copy.wait()
        for c in range(chunks):
            write(c, c).wait()

    @pl.when(g == 1)
    def _():
        def clear(i, carry):
            raw[pl.ds(pl.multiple_of(i * SUB, SUB), SUB)] = jnp.zeros((SUB, rows, nx), jnp.float32)
            return carry

        lax.fori_loop(0, part // SUB, clear, 0)
        for c in range(chunks):
            write(c, 0).start()

        if pad > ny:
            turn[ny:pad] = jnp.zeros((pad - ny, nx), jnp.float32)
        for t in range(t_n):
            tilev = got_ref[t * s_n]
            for q in range(1, s_n):
                tilev = tilev + got_ref[t * s_n + q]
            turn[t * rows : (t + 1) * rows] = tilev
        turned = jnp.transpose(turn[...])
        total, sx, sy, dx, dy, wet = [turned[q * size : (q + 1) * size] for q in range(6)]
        row = lax.broadcasted_iota(jnp.int32, (size, pad), 0)
        column = row + (tile * cols - 4)
        wet = jnp.where((column >= 0) & (column < t_n * cols), wet, 0.0)
        stack = 3 * own
        mix[0] = jnp.zeros((size, pad), jnp.float32)
        mix[0, 4 : 4 + cols, 0:ny] = sea_ref[...]
        mix[0, 2:4, 0:ny] = hb_ref[2 * stack : 2 * stack + 2, 0:ny]
        mix[0, 4 + cols : 6 + cols, 0:ny] = ha_ref[2 * stack : 2 * stack + 2, 0:ny]
        depth = 10.0 + 4.0 * mix[0]
        breaking = 1.0 / (1.0 + 25.0 * total / (depth * depth))
        swept = wet * breaking
        sx, sy, dx, dy = sx * breaking, sy * breaking, dx * swept, dy * swept

        field[...] = jnp.zeros(field.shape, jnp.float32)
        ext = own + 4
        for c in range(3):
            for k in range(own):
                l = c * ext + 2 + k
                field[l, 4 : 4 + cols, 0:ny] = ocean_ref[c, k]
                for m in range(2):
                    at = m * stack + c * own + k
                    field[l, 2 + m : 3 + m, 0:ny] = hb_ref[at : at + 1, 0:ny]
                    field[l, 4 + cols + m : 5 + cols + m, 0:ny] = ha_ref[at : at + 1, 0:ny]
        for upper in range(2):
            @pl.when(s == 1 - upper)
            def _():
                for c in range(3):
                    for k in range(2):
                        l = c * ext + (own + 2 if upper else 0) + k
                        at = (c * 2 + k) * cols
                        field[l, 4 : 4 + cols, 0:ny] = lev_ref[at : at + cols, :]
                        for m in range(2):
                            at = m * SUB + c * 2 + k
                            field[l, 2 + m : 3 + m, 0:ny] = cb_ref[at : at + 1, 0:ny]
                            field[l, 4 + cols + m : 5 + cols + m, 0:ny] = ca_ref[at : at + 1, 0:ny]

        lane = lanes_of((size, pad))

        def new_fields(source, k):
            values = []
            for c in range(3):
                q = source[c * ext + k]
                lateral = (
                    pltpu.roll(q, size - 1, 0)
                    + pltpu.roll(q, 1, 0)
                    + jnp.where(lane == ny - 1, 0.0, pltpu.roll(q, pad - 1, 1))
                    + jnp.where(lane == 0, 0.0, pltpu.roll(q, 1, 1))
                    - 4.0 * q
                )
                vertical = source[c * ext + k + 1] + source[c * ext + k - 1] - 2.0 * q
                values.append((q, q + 0.1 * lateral + 0.2 * vertical))
            (u, du), (v, dv), (_, dt) = values
            shaped = level_ref[s, 1, k]
            top = jnp.where((s == 0) & (k == 2), 1.0, 0.0)
            east = du + 0.1 * (v + shaped * dy) + top * sx
            north = dv - 0.1 * (u + shaped * dx) + top * sy
            keep = wet * level_ref[s, 2, k]
            return keep * east, keep * north, keep * dt

        for k in range(1, ext - 1):
            for c, value in enumerate(new_fields(field, k)):
                mix[c * ext + k] = value
        for k in range(2, ext - 2):
            for c, value in enumerate(new_fields(mix, k)):
                out[c, k - 2] = value[4 : 4 + cols, 0:ny]
        ocean_copy.start()
        ocean_copy.wait()
        for c in range(chunks):
            write(c, 0).wait()


def body(spectrum, wind, land_mask, intersection, ocean_state, sea_level, *, mesh_shape):
    g_n, t_n, s_n = (mesh_shape[a] for a in AXES)
    _, freqs, dirs, rows, nx = spectrum.shape
    _, _, own, cols, ny = ocean_state.shape
    fd = freqs * dirs
    devices = g_n * t_n * s_n
    table = jnp.asarray(wave_table(freqs, dirs * s_n, s_n))
    levels = jnp.asarray(level_table(own * s_n, s_n, own))
    ocean = ocean_state[0]
    sea = sea_level[0]

    def in_hbm(x):
        return pltpu.with_memory_space_constraint(x, pltpu.HBM)

    natural = in_hbm(spectrum.reshape(fd, rows, nx))
    chunks = 6
    vm = pltpu.VMEM
    params = pltpu.CompilerParams(vmem_limit_bytes=24 << 20)

    def up(x):
        return lax.ppermute(x, "tile", [(i, i + 1) for i in range(t_n - 1)])

    def down(x):
        return lax.ppermute(x, "tile", [(i + 1, i) for i in range(t_n - 1)])

    def others(x):
        return added(lax.ppermute(x, "spec", [(i, (i + k) % s_n) for i in range(s_n)]) for k in range(1, s_n))

    def crossed(x, step):
        tiles = [(i, i + step) for i in range(t_n) if 0 <= i + step < t_n]
        return added(
            lax.ppermute(x, ("tile", "spec"), [(a * s_n + q, b * s_n + (q + k) % s_n) for a, b in tiles for q in range(s_n)])
            for k in range(1, s_n)
        )

    def added(values):
        return functools.reduce(lambda a, b: a + b, values)

    def call(kernel, name, args, specs, shapes, out_specs, scratch):
        return pl.pallas_call(
            kernel, out_shape=shapes, in_specs=specs, out_specs=out_specs,
            scratch_shapes=scratch, compiler_params=params, name=name,
        )(*args)

    send, level_rim, lo, hi = call(
        functools.partial(start_kernel, (t_n, s_n, rows, cols, own, ny, fd, nx, chunks)), "start",
        (levels, natural, in_hbm(ocean.reshape(3 * own, cols, ny)), in_hbm(sea)), [SM, HB, HB, HB],
        (f32(devices, rows, 4 * cols), f32(3, 2, cols, ny), f32(fd, nx), f32(fd, nx)), (VM,) * 4,
        [vm((fd, rows, nx), jnp.float32), vm((3 * own, cols, ny), jnp.float32), vm((cols, ny), jnp.float32),
         pltpu.SemaphoreType.DMA((chunks + 2,))],
    )
    arrived = lax.all_to_all(send, AXES, 0, 0, tiled=True)
    hb, ha = up(hi), down(lo)
    level_got = others(level_rim).reshape(6 * cols, ny)
    hb0, ha0 = hb, ha

    u, v, depth, rim = call(
        functools.partial(pick_kernel, (t_n, s_n, rows, cols, nx)), "pick",
        (arrived, land_mask, intersection), [VM] * 3,
        (f32(rows, nx), f32(rows, nx), f32(rows, nx), f32(3 * rows, nx)), (VM,) * 4, [],
    )
    vb, va = up(rim), down(rim)

    breaking = rim
    for step in range(WSTEPS):
        begin, sums = step == 0, step == WSTEPS - 1
        kinds = 5 if sums else 1
        scratch = [vm((3, rows + 2, SUB, nx), jnp.float32), vm((kinds, rows, SUB, nx), jnp.float32)]
        if begin:
            newmid, partial, growth, mid = call(
                functools.partial(first_middle_kernel, (rows, fd, nx, chunks)), "middle0",
                (table, u, v, rim, wind, natural), [VM] * 5 + [HB],
                (f32(rows - 2, fd, nx), f32(1, rows, nx), f32(rows, fd, nx), f32(2, fd, nx)), (VM,) * 4,
                [vm((fd, rows, nx), jnp.float32), vm((2, rows, SUB, nx), jnp.float32)] + scratch
                + [pltpu.SemaphoreType.DMA((chunks,))],
            )
        else:
            newmid, partial, breaking = call(
                functools.partial(middle_kernel, (rows, fd, nx), sums), f"middle{step}",
                (table, u, v, rim, depth, total, got, mid, lo, hi, growth), [VM] * 11,
                (f32(rows - 2, fd, nx), f32(kinds, rows, nx), f32(rows, nx)), (VM,) * 3, scratch,
            )
        args = (table, u, v, breaking, vb, va, rim, mid, lo, hi, hb, ha, growth, partial)
        args += (level_got,) if begin else (cb, ca)
        if sums:
            args += (intersection,)
            shapes = (f32(fd, nx), f32(fd, nx), f32(devices, rows, nx))
        else:
            shapes = (f32(fd + SUB, nx), f32(fd + SUB, nx), f32(rows, nx))
        newlo, newhi, total = call(
            functools.partial(edge_kernel, (rows, fd, nx, t_n, s_n, cols, own), begin, sums), f"edge{step}",
            args, [VM] * len(args), shapes, (VM,) * 3, scratch,
        )
        mid, lo, hi = newmid, newlo, newhi
        if not sums:
            got = others(total)
            hb, ha = up(hi), down(lo)
            cb, ca = crossed(total, 1), crossed(total, -1)
        if begin:
            hb1, ha1 = hb, ha

    landed = lax.all_to_all(total, AXES, 0, 0, tiled=True)
    pad = -(-ny // LANES) * LANES
    size = cols + 8
    ins = (table, levels, landed, rim, depth, mid, lo, hi, ocean, sea, hb0, ha0, hb1, ha1, level_got)
    waves, fields = call(
        functools.partial(last_kernel, (rows, fd, nx, t_n, s_n, cols, own, ny, chunks)), "last",
        ins, [VM, SM] + [VM] * (len(ins) - 2), (f32(fd, rows, nx), f32(3, own, cols, ny)), (HB, HB),
        [
            vm((fd, rows, nx), jnp.float32),
            vm((rows, SUB, nx), jnp.float32),
            vm((pad, nx), jnp.float32),
            vm((3 * (own + 4), size, pad), jnp.float32),
            vm((3 * (own + 4), size, pad), jnp.float32),
            vm((3, own, cols, ny), jnp.float32),
            pltpu.SemaphoreType.DMA((chunks,)),
            pltpu.SemaphoreType.DMA,
        ],
    )
    return waves.reshape(spectrum.shape), fields.reshape(ocean_state.shape)


def solution(mesh):
    return jax.shard_map(
        functools.partial(body, mesh_shape=dict(mesh.shape)),
        mesh=mesh,
        in_specs=(
            P("grp", None, "spec", "tile", None),
            P(None, "tile", None),
            P("tile", None),
            P("tile", None),
            P("grp", None, "spec", "tile", None),
            P("grp", "tile", None),
        ),
        out_specs=(P("grp", None, "spec", "tile", None), P("grp", None, "spec", "tile", None)),
        check_vma=False,
    )
```

```python
import functools
import math

import jax
import jax.numpy as jnp
import numpy as np
from jax import lax
from jax.experimental import pallas as pl
from jax.experimental.pallas import tpu as pltpu
from jax.sharding import PartitionSpec as P


WSTEPS = 4
HALO = WSTEPS
NEAR = 2
LANES = 128
SUB = 8
UNROLL = 4
AXES = ("grp", "tile", "spec")

BW, GE, GN, WE, WN, SX, SY, DX, DY, INV = range(10)

VM = pl.BlockSpec(memory_space=pltpu.VMEM)
SM = pl.BlockSpec(memory_space=pltpu.SMEM)
HB = pl.BlockSpec(memory_space=pltpu.HBM)


def f32(*shape):
    return jax.ShapeDtypeStruct(shape, jnp.float32)


def wave_table(freqs, dirs, parts):
    frequency = 0.04 * 1.1 ** np.arange(freqs)
    celerity = 1.56 / frequency
    group = 0.4 * 1.1 ** (-np.arange(freqs, dtype=np.float64))
    width = 0.1 * frequency * (2.0 * math.pi / dirs)
    angle = 2.0 * math.pi * (np.arange(dirs) + 0.5) / dirs
    cos, sin, one = np.cos(angle), np.sin(angle), np.ones(dirs)
    columns = [
        np.outer(width, one),
        np.outer(group, cos),
        np.outer(group, sin),
        np.outer(0.05 / celerity, cos),
        np.outer(0.05 / celerity, sin),
        np.outer(5.0 / celerity, cos),
        np.outer(5.0 / celerity, sin),
        np.outer(20.0 * frequency**3, cos),
        np.outer(20.0 * frequency**3, sin),
        np.outer(1.0 / width, one),
    ]
    table = np.zeros((parts, freqs * dirs // parts, 16), np.float32)
    for k, column in enumerate(columns):
        split = column.reshape(freqs, parts, dirs // parts).transpose(1, 0, 2)
        table[:, :, k] = split.reshape(parts, -1)
    return table


def level_table(levels, parts, own):
    depth = (np.arange(levels) + 0.5) / levels
    profile = np.exp(-2.0 * depth)
    weights = profile / profile.sum()
    table = np.zeros((parts, 3, own + 4), np.float32)
    for s in range(parts):
        table[s, 0, :own] = weights[s * own : (s + 1) * own]
        for l in range(own + 4):
            g = s * own + l - 2
            if 0 <= g < levels:
                table[s, 1, l] = profile[g]
                table[s, 2, l] = 1.0
    return table


def lanes_of(shape):
    return lax.broadcasted_iota(jnp.int32, shape, len(shape) - 1)


def wide(column):
    return jnp.broadcast_to(column, (SUB, LANES))


def half(h):
    return slice(h * LANES, (h + 1) * LANES)


def barrel(values, shift, size, left):
    bit = 1
    while bit < size:
        taken = (shift & bit) != 0
        amount = size - bit if left else bit
        values = [jnp.where(taken, pltpu.roll(v, amount, 1), v) for v in values]
        bit *= 2
    return values


def start_kernel(n, level_ref, spectrum_ref, ocean_hbm, sea_hbm, mask_hbm, wind_hbm, cross_hbm,
                 out_ref, rim_ref, near_lo_hbm, near_hi_hbm, far_lo_hbm, far_hi_hbm,
                 raw, ocean, sea, mask_ref, wind_ref, cross_ref, near_lo, near_hi, far_lo, far_hi, sem, out_sem):
    t_n, s_n, rows, cols, own, ny, fd, nx, chunks = n
    s = lax.axis_index("spec")
    pad = -(-ny // LANES) * LANES
    part = fd // chunks
    small = ((ocean_hbm, ocean), (sea_hbm, sea), (mask_hbm, mask_ref), (wind_hbm, wind_ref), (cross_hbm, cross_ref))
    first = [pltpu.make_async_copy(a, b, sem.at[chunks + k]) for k, (a, b) in enumerate(small)]
    copies = [
        pltpu.make_async_copy(spectrum_ref.at[pl.ds(c * part, part)], raw.at[pl.ds(c * part, part)], sem.at[c])
        for c in range(chunks)
    ]
    for copy in first + copies:
        copy.start()
    for copy in first:
        copy.wait()
    parts = []
    for c in range(2):
        total = None
        for k in range(own):
            term = level_ref[s, 0, k] * ocean[c * own + k]
            total = term if total is None else total + term
        parts.append(total)
    parts.append(jnp.where(s == 0, sea[...], 0.0))
    for c in range(3):
        for k in range(2):
            rim_ref[c, k] = jnp.where(s == 0, ocean[c * own + own - 2 + k], ocean[c * own + k])
    stack = jnp.concatenate(parts, axis=0)
    stack = jnp.pad(stack, ((0, LANES - 3 * cols), (0, pad - ny)))
    edge = jnp.zeros((HALO, LANES), jnp.float32)
    turned = jnp.concatenate([edge, jnp.transpose(stack)[:ny], edge], axis=0)
    for t in range(t_n):
        for q in range(s_n):
            out_ref[t * s_n + q] = turned[t * rows : (t + 1) * rows + 2 * HALO, : 4 * cols]
    aux = [mask_ref[...].astype(jnp.float32), wind_ref[0], wind_ref[1], cross_ref[...].astype(jnp.float32)]
    for k, value in enumerate(aux):
        at = NEAR * fd + k * HALO
        near_hi[at : at + HALO] = value[rows - HALO : rows]
        near_lo[at : at + HALO] = value[0:HALO]

    held = ((near_lo, near_lo_hbm), (near_hi, near_hi_hbm), (far_lo, far_lo_hbm), (far_hi, far_hi_hbm))
    outward = []

    def send_out(c):
        spans = [(c * part, part), (fd + c * part, part)]
        for k, (here, there) in enumerate(held):
            for j, (at, size) in enumerate(spans):
                span = pl.ds(at, size)
                outward.append(pltpu.make_async_copy(here.at[span], there.at[span], out_sem.at[c, k, j]))
                outward[-1].start()
            if c == 0 and k < 2:
                span = pl.ds(NEAR * fd, 4 * HALO)
                outward.append(pltpu.make_async_copy(here.at[span], there.at[span], out_sem.at[c, k, 2]))
                outward[-1].start()

    for c in range(chunks):
        copies[c].wait()

        def turn(i, carry):
            for k in range(2):
                at = pl.multiple_of(c * part + (2 * i + k) * SUB, SUB)
                for h in range(nx // LANES):
                    planes = jnp.swapaxes(raw[pl.ds(at, SUB), :, half(h)], 0, 1)
                    for j in range(HALO):
                        lo_ref, hi_ref = (near_lo, near_hi) if j < NEAR else (far_lo, far_hi)
                        sl = pl.ds(pl.multiple_of(at + (j % NEAR) * fd, SUB), SUB)
                        lo_ref[sl, half(h)] = planes[j]
                        hi_ref[sl, half(h)] = planes[rows - 1 - j]
            return carry

        lax.fori_loop(0, part // (2 * SUB), turn, 0)
        if c:
            send_out(c)

    @pl.when(lax.axis_index("grp") == 1)
    def _():
        stack = 3 * own
        for k in range(2):
            for ref, at in ((near_lo, k), (near_hi, cols - 2 + k)):
                for m in range(stack):
                    ref[k * stack + m : k * stack + m + 1, 0:ny] = ocean[m, at : at + 1, :]
                ref[2 * stack + k : 2 * stack + k + 1, 0:ny] = sea[at : at + 1, :]

    send_out(0)
    for copy in outward:
        copy.wait()


def pick_kernel(n, full, got_ref, mask_ref, cross_ref, *refs):
    t_n, s_n, rows, cols, nx, fd = n[:6]
    ext = rows + 2 * HALO
    lane = lanes_of((ext, LANES))
    per = LANES // cols
    fields = [[jnp.zeros((ext, LANES), jnp.float32) for _ in range(nx // LANES)] for _ in range(3)]
    for t in range(t_n):
        tile = got_ref[(t_n + t) * s_n]
        for q in range(1, s_n):
            tile = tile + got_ref[(t_n + t) * s_n + q]
        if tile.shape[1] < LANES:
            tile = jnp.pad(tile, ((0, 0), (0, LANES - tile.shape[1])))
        h, at = t // per, (t % per) * cols
        inside = (lane >= at) & (lane < at + cols)
        for c in range(3):
            moved = pltpu.roll(tile, (at - c * cols) % LANES, 1) if (at - c * cols) % LANES else tile
            fields[c][h] = jnp.where(inside, moved, fields[c][h])
    whole = [jnp.concatenate(f, axis=1) for f in fields]
    wet, shift = mask_ref[...].astype(jnp.float32), cross_ref[...].astype(jnp.float32)
    if full:
        wind_ref, hb_ref, ha_ref, rim_ref, geo_ref, out_ref, edge_ref = refs
        own, ny = n[6], rim_ref.shape[3]
        low = lax.axis_index("spec") == 0
        for c in range(3):
            for k in range(2):
                edge_ref[c * 2 + k] = jnp.zeros((cols + 8, ny), jnp.float32)
                edge_ref[c * 2 + k, 4 : 4 + cols] = rim_ref[c, k]
                for m in range(2):
                    for ref, at in ((hb_ref, 2 + m), (ha_ref, 4 + cols + m)):
                        top, bottom = [m * 3 * own + c * own + j for j in (own - 2 + k, k)]
                        value = jnp.where(low, ref[top : top + 1, 0:ny], ref[bottom : bottom + 1, 0:ny])
                        edge_ref[c * 2 + k, at : at + 1] = value

        def joined(k, own):
            span = slice(NEAR * fd + k * HALO, NEAR * fd + (k + 1) * HALO)
            return jnp.concatenate([hb_ref[span], own, ha_ref[span]], axis=0)

        wet, shift = joined(0, wet), joined(3, shift)
        for c in range(2):
            out_ref[c * ext : (c + 1) * ext] = joined(1 + c, wind_ref[c])
    else:
        (geo_ref,) = refs
        edge = jnp.zeros((HALO, nx), jnp.float32)
        wet, shift = [jnp.concatenate([edge, x, edge], axis=0) for x in (wet, shift)]
    shift = jnp.broadcast_to(shift[:, 0:1].astype(jnp.int32), (ext, nx))
    u, v, sea = barrel(whole, shift, nx, True)
    depth = 10.0 + 4.0 * sea
    for k, value in enumerate((0.1 * u, 0.1 * v, 25.0 / (depth * depth), wet)):
        geo_ref[k * ext : (k + 1) * ext] = value


def advance(segments, fd, nx, s, table_ref, planes, store, splat, acc, sums, before=None):
    halves = nx // LANES
    lane = lanes_of((SUB, LANES))
    first, last = lane == 0, lane == LANES - 1
    acc[...] = jnp.zeros(acc.shape, jnp.float32)

    def body(i, carry):
        if before is not None:
            before(i)
        totals = {}

        def add(key, value):
            totals[key] = totals[key] + value if key in totals else value

        for k in range(UNROLL):
            at = pl.multiple_of((i * UNROLL + k) * SUB, SUB)
            sl = pl.ds(at, SUB)
            ge, gn = wide(table_ref[s, sl, GE : GE + 1]), wide(table_ref[s, sl, GN : GN + 1])
            bands = [wide(table_ref[s, sl, b : b + 1]) for b in (SX, SY, DX, DY)] if sums else None
            energy, growth = planes(at)
            for segment in segments:
                def state(r):
                    e = [energy(r, h) * splat[2, r + HALO, :, half(h)] for h in range(halves)]
                    north = [(gn + splat[1, r + HALO, :, half(h)]) * e[h] for h in range(halves)]
                    return e, north

                here, below = state(segment[0]), state(segment[0] - 1)
                flow = [jnp.maximum(below[1][h], 0.0) + jnp.minimum(here[1][h], 0.0) for h in range(halves)]
                for r in segment:
                    above = state(r + 1)
                    e, north = here
                    upper = [jnp.maximum(north[h], 0.0) + jnp.minimum(above[1][h], 0.0) for h in range(halves)]
                    east = [(ge + splat[0, r + HALO, :, half(h)]) * e[h] for h in range(halves)]
                    left = [pltpu.roll(x, LANES - 1, 1) for x in east]
                    flux = [
                        jnp.maximum(east[h], 0.0)
                        + jnp.minimum(jnp.where(last, left[h + 1] if h + 1 < halves else 0.0, left[h]), 0.0)
                        for h in range(halves)
                    ]
                    right = [pltpu.roll(x, 1, 1) for x in flux]
                    for h in range(halves):
                        behind = jnp.where(first, right[h - 1] if h else jnp.minimum(east[0], 0.0), right[h])
                        advected = (e[h] - (flux[h] - behind)) - (upper[h] - flow[h])
                        g = growth(r, h)
                        add((0, r, h), advected)
                        if sums:
                            pushed = (g - 1.0) * advected
                            grown = advected + pushed
                            for b in range(2):
                                add((1 + b, r, h), bands[b] * pushed)
                                add((3 + b, r, h), bands[2 + b] * grown)
                        else:
                            grown = g * advected
                        store(r, at, h, grown)
                    here, flow = above, upper
        for (kind, r, h), value in totals.items():
            acc[kind, r + HALO, :, half(h)] += value
        return carry

    lax.fori_loop(0, fd // (SUB * UNROLL), body, 0)


def folded(acc, kind, rows):
    return [jnp.sum(acc[kind, r + HALO], axis=0, keepdims=True) for r in rows]


def fill(splat, kind, row, value, nx):
    splat[kind, row + HALO] = jnp.broadcast_to(value, (SUB, nx))


def geometry(geo_ref, ext, kind, r):
    at = kind * ext + r + HALO
    return geo_ref[at : at + 1]


def write_totals(total_ref, acc, rows, previous, ext, nx):
    total_ref[...] = jnp.zeros((ext, nx), jnp.float32) if previous is None else previous[...]
    for r, value in zip(rows, folded(acc, 0, rows)):
        total_ref[r + HALO : r + HALO + 1] = value


def first_middle_kernel(n, table_ref, geo_ref, wind_ref, spectrum_ref,
                        out_ref, total_ref, growth_ref, raw, windb, splat, acc, sem):
    rows, fd, nx, chunks = n
    ext = rows + 2 * HALO
    s = lax.axis_index("spec")
    part = fd // chunks
    turns = part // (SUB * UNROLL)

    def copy(c):
        span = pl.ds(pl.multiple_of(c * part, SUB), part)
        return pltpu.make_async_copy(spectrum_ref.at[span], raw.at[span], sem.at[c])

    for c in range(chunks):
        copy(c).start()
    for c in range(2):
        for r in range(rows):
            windb[c, r] = jnp.broadcast_to(wind_ref[c, r : r + 1], (SUB, nx))
    for r in range(rows):
        for kind, source in ((0, 0), (1, 1), (2, 3)):
            fill(splat, kind, r, geometry(geo_ref, ext, source, r), nx)

    def before(i):
        @pl.when(i % turns == 0)
        def _():
            copy(i // turns).wait()

    def planes(at):
        sl = pl.ds(at, SUB)
        bw, we, wn = [wide(table_ref[s, sl, b : b + 1]) for b in (BW, WE, WN)]
        natural, grown = {}, {}
        for h in range(nx // LANES):
            natural[h] = jnp.swapaxes(raw[sl, :, half(h)], 0, 1)
            for r in range(rows):
                drive = we * windb[0, r, :, half(h)] + wn * windb[1, r, :, half(h)]
                grown[r, h] = 1.0 + jnp.maximum(drive - 0.05, 0.0)
                growth_ref[pl.ds(pl.multiple_of(r * fd + at, SUB), SUB), half(h)] = grown[r, h]
        return lambda r, h: bw * natural[h][r], lambda r, h: grown[r, h]

    def store(r, at, h, value):
        out_ref[pl.ds(pl.multiple_of((r - 1) * fd + at, SUB), SUB), half(h)] = value

    inner = list(range(1, rows - 1))
    advance([inner], fd, nx, s, table_ref, planes, store, splat, acc, False, before)
    write_totals(total_ref, acc, inner, None, ext, nx)


def step_kernel(n, cfg, *refs):
    rows, fd, nx, t_n, s_n, cols = n
    segments, source, growth, grow, raw, sums, joined, count = cfg
    ext = rows + 2 * HALO
    refs = list(refs)
    table_ref, geo_ref = refs.pop(0), refs.pop(0)
    wind_ref = refs.pop(0) if grow else None
    own_ref, got_ref = (None, None) if raw else (refs.pop(0), refs.pop(0))
    previous = refs.pop(0) if joined else None
    cross_ref = refs.pop(0) if sums else None
    operands, refs = refs[:count], refs[count:]
    out_ref, total_ref = refs.pop(0), refs.pop(0)
    growth_ref = refs.pop(0) if grow else None
    splat, acc = refs.pop(0), refs.pop(0)
    windb = refs.pop(0) if grow else None
    s = lax.axis_index("spec")
    order = [r for segment in segments for r in segment]
    needed = sorted({r + d for r in order for d in (-1, 0, 1)})
    breaking = geo_ref[3 * ext : 4 * ext]
    if not raw:
        breaking = breaking / (1.0 + (own_ref[...] + got_ref[...]) * geo_ref[2 * ext : 3 * ext])
    for r in needed:
        fill(splat, 0, r, geometry(geo_ref, ext, 0, r), nx)
        fill(splat, 1, r, geometry(geo_ref, ext, 1, r), nx)
        fill(splat, 2, r, breaking[r + HALO : r + HALO + 1], nx)
    for c in range(2):
        for k, r in enumerate(grow):
            at = c * ext + r + HALO
            windb[c, k] = jnp.broadcast_to(wind_ref[at : at + 1], (SUB, nx))

    def planes(at):
        sl = pl.ds(at, SUB)
        bw = wide(table_ref[s, sl, BW : BW + 1]) if raw else None
        we, wn = [wide(table_ref[s, sl, b : b + 1]) for b in (WE, WN)] if grow else (None, None)

        def energy(r, h):
            operand, first = source[r]
            value = operands[operand][pl.ds(pl.multiple_of(first + at, SUB), SUB), half(h)]
            return bw * value if raw else value

        def factor(r, h):
            if r in grow:
                k = grow.index(r)
                drive = we * windb[0, k, :, half(h)] + wn * windb[1, k, :, half(h)]
                value = 1.0 + jnp.maximum(drive - 0.05, 0.0)
                growth_ref[pl.ds(pl.multiple_of(k * fd + at, SUB), SUB), half(h)] = value
                return value
            operand, first = growth[r]
            return operands[operand][pl.ds(pl.multiple_of(first + at, SUB), SUB), half(h)]

        return energy, factor

    def store(r, at, h, value):
        out_ref[pl.ds(pl.multiple_of(order.index(r) * fd + at, SUB), SUB), half(h)] = value

    advance(segments, fd, nx, s, table_ref, planes, store, splat, acc, sums)
    if not sums:
        write_totals(total_ref, acc, order, previous, ext, nx)
        return
    kinds = [jnp.concatenate(folded(acc, kind, order), axis=0) for kind in range(acc.shape[0])]
    wet = jnp.where(s == 0, geo_ref[3 * ext + HALO : 3 * ext + HALO + rows], 0.0)
    shift = jnp.broadcast_to(cross_ref[:, 0:1], (rows, nx))
    moved = barrel(kinds + [wet], shift, nx, False)
    lane = lanes_of((rows, nx))
    size = cols + 8
    for t in range(t_n):
        chunk = jnp.zeros((rows, nx), jnp.float32)
        for q, value in enumerate(moved):
            amount = (q * size - (cols * t - 4)) % nx
            piece = pltpu.roll(value, amount, 1) if amount else value
            chunk = jnp.where((lane >= q * size) & (lane < (q + 1) * size), piece, chunk)
        for q in range(s_n):
            total_ref[(t_n + t) * s_n + q] = chunk
    mine = lax.axis_index("tile")
    for q in range(s_n):
        total_ref[mine * s_n + q] = kinds[0]


def last_kernel(n, table_ref, level_ref, got_ref, geo_ref, wave_ref, ocean_ref, sea_ref,
                hb_ref, ha_ref, lev_ref, waves_ref, next_ref,
                raw, brk, turn, field, mix, out, sem, osem):
    rows, fd, nx, t_n, s_n, cols, own, ny, chunks = n
    s = lax.axis_index("spec")
    g = lax.axis_index("grp")
    tile = lax.axis_index("tile")
    part = fd // chunks
    pad = turn.shape[0]
    size = cols + 8

    def write(c, source):
        return pltpu.make_async_copy(raw.at[pl.ds(source * part, part)], waves_ref.at[pl.ds(c * part, part)], sem.at[c])

    ocean_copy = pltpu.make_async_copy(out, next_ref, osem)

    @pl.when(g == 0)
    def _():
        total = got_ref[tile * s_n]
        for q in range(1, s_n):
            total = total + got_ref[tile * s_n + q]
        ext = rows + 2 * HALO
        wet = geo_ref[3 * ext + HALO : 3 * ext + HALO + rows]
        breaking = wet / (1.0 + total * geo_ref[2 * ext + HALO : 2 * ext + HALO + rows])
        for r in range(rows):
            brk[r] = jnp.broadcast_to(breaking[r : r + 1], (SUB, nx))
        for c in range(chunks):

            def finish(i, carry):
                for k in range(2):
                    at = pl.multiple_of(c * part + (2 * i + k) * SUB, SUB)
                    sl = pl.ds(at, SUB)
                    inv = wide(table_ref[s, sl, INV : INV + 1])
                    for h in range(nx // LANES):
                        spans = [pl.ds(pl.multiple_of(r * fd + at, SUB), SUB) for r in range(rows)]
                        values = [wave_ref[span, half(h)] for span in spans]
                        values = [value * brk[r, :, half(h)] * inv for r, value in enumerate(values)]
                        raw[sl, :, half(h)] = jnp.swapaxes(jnp.stack(values), 0, 1)
                return carry

            lax.fori_loop(0, part // (2 * SUB), finish, 0)
            write(c, c).start()
        out[...] = jnp.zeros((3, own, cols, ny), jnp.float32)
        ocean_copy.start()
        ocean_copy.wait()
        for c in range(chunks):
            write(c, c).wait()

    @pl.when(g == 1)
    def _():
        def clear(i, carry):
            raw[pl.ds(pl.multiple_of(i * SUB, SUB), SUB)] = jnp.zeros((SUB, rows, nx), jnp.float32)
            return carry

        lax.fori_loop(0, part // SUB, clear, 0)
        for c in range(chunks):
            write(c, 0).start()

        if pad > ny:
            turn[ny:pad] = jnp.zeros((pad - ny, nx), jnp.float32)
        for t in range(t_n):
            tilev = got_ref[t * s_n]
            for q in range(1, s_n):
                tilev = tilev + got_ref[t * s_n + q]
            turn[t * rows : (t + 1) * rows] = tilev
        turned = jnp.transpose(turn[...])
        total, sx, sy, dx, dy, wet = [turned[q * size : (q + 1) * size] for q in range(6)]
        row = lax.broadcasted_iota(jnp.int32, (size, pad), 0)
        column = row + (tile * cols - 4)
        wet = jnp.where((column >= 0) & (column < t_n * cols), wet, 0.0)
        stack = 3 * own
        mix[0] = jnp.zeros((size, pad), jnp.float32)
        mix[0, 4 : 4 + cols, 0:ny] = sea_ref[...]
        mix[0, 2:4, 0:ny] = hb_ref[2 * stack : 2 * stack + 2, 0:ny]
        mix[0, 4 + cols : 6 + cols, 0:ny] = ha_ref[2 * stack : 2 * stack + 2, 0:ny]
        depth = 10.0 + 4.0 * mix[0]
        breaking = 1.0 / (1.0 + 25.0 * total / (depth * depth))
        swept = wet * breaking
        sx, sy, dx, dy = sx * breaking, sy * breaking, dx * swept, dy * swept

        field[...] = jnp.zeros(field.shape, jnp.float32)
        ext = own + 4
        for c in range(3):
            for k in range(own):
                l = c * ext + 2 + k
                field[l, 4 : 4 + cols, 0:ny] = ocean_ref[c, k]
                for m in range(2):
                    at = m * stack + c * own + k
                    field[l, 2 + m : 3 + m, 0:ny] = hb_ref[at : at + 1, 0:ny]
                    field[l, 4 + cols + m : 5 + cols + m, 0:ny] = ha_ref[at : at + 1, 0:ny]
        for upper in range(2):
            @pl.when(s == 1 - upper)
            def _():
                for c in range(3):
                    for k in range(2):
                        l = c * ext + (own + 2 if upper else 0) + k
                        field[l, :, 0:ny] = lev_ref[c * 2 + k]

        lane = lanes_of((size, pad))

        def new_fields(source, k):
            values = []
            for c in range(3):
                q = source[c * ext + k]
                lateral = (
                    pltpu.roll(q, size - 1, 0)
                    + pltpu.roll(q, 1, 0)
                    + jnp.where(lane == ny - 1, 0.0, pltpu.roll(q, pad - 1, 1))
                    + jnp.where(lane == 0, 0.0, pltpu.roll(q, 1, 1))
                    - 4.0 * q
                )
                vertical = source[c * ext + k + 1] + source[c * ext + k - 1] - 2.0 * q
                values.append((q, q + 0.1 * lateral + 0.2 * vertical))
            (u, du), (v, dv), (_, dt) = values
            shaped = level_ref[s, 1, k]
            top = jnp.where((s == 0) & (k == 2), 1.0, 0.0)
            east = du + 0.1 * (v + shaped * dy) + top * sx
            north = dv - 0.1 * (u + shaped * dx) + top * sy
            keep = wet * level_ref[s, 2, k]
            return keep * east, keep * north, keep * dt

        for k in range(1, ext - 1):
            for c, value in enumerate(new_fields(field, k)):
                mix[c * ext + k] = value
        for k in range(2, ext - 2):
            for c, value in enumerate(new_fields(mix, k)):
                out[c, k - 2] = value[4 : 4 + cols, 0:ny]
        ocean_copy.start()
        ocean_copy.wait()
        for c in range(chunks):
            write(c, 0).wait()


def program(spectrum, wind, land_mask, intersection, ocean_state, sea_level, *, mesh_shape):
    g_n, t_n, s_n = (mesh_shape[a] for a in AXES)
    _, freqs, dirs, rows, nx = spectrum.shape
    _, _, own, cols, ny = ocean_state.shape
    fd = freqs * dirs
    devices = g_n * t_n * s_n
    table = jnp.asarray(wave_table(freqs, dirs * s_n, s_n))
    levels = jnp.asarray(level_table(own * s_n, s_n, own))
    ocean = ocean_state[0]
    sea = sea_level[0]

    def in_hbm(x):
        return pltpu.with_memory_space_constraint(x, pltpu.HBM)

    natural = in_hbm(spectrum.reshape(fd, rows, nx))
    chunks = 6
    vm = pltpu.VMEM
    params = pltpu.CompilerParams(vmem_limit_bytes=24 << 20)

    def up(x):
        return lax.ppermute(x, "tile", [(i, i + 1) for i in range(t_n - 1)])

    def down(x):
        return lax.ppermute(x, "tile", [(i + 1, i) for i in range(t_n - 1)])

    def others(x):
        return added(lax.ppermute(x, "spec", [(i, (i + k) % s_n) for i in range(s_n)]) for k in range(1, s_n))

    def added(values):
        return functools.reduce(lambda a, b: a + b, values)

    def call(kernel, args, specs, shapes, out_specs, scratch):
        return pl.pallas_call(
            kernel, out_shape=shapes, in_specs=specs, out_specs=out_specs,
            scratch_shapes=scratch, compiler_params=params,
        )(*args)

    ext = rows + 2 * HALO
    near, far = f32(NEAR * fd + 4 * HALO, nx), f32((HALO - NEAR) * fd, nx)

    def hbm(shape):
        return pltpu.HBM(shape.shape, shape.dtype)

    send, level_rim, near_lo, near_hi, far_lo, far_hi = call(
        functools.partial(start_kernel, (t_n, s_n, rows, cols, own, ny, fd, nx, chunks)),
        (levels, natural, in_hbm(ocean.reshape(3 * own, cols, ny)), in_hbm(sea), in_hbm(land_mask), in_hbm(wind), in_hbm(intersection)),
        [SM] + [HB] * 6,
        (f32(devices, ext, 4 * cols), f32(3, 2, cols, ny), hbm(near), hbm(near), hbm(far), hbm(far)),
        (VM,) * 2 + (HB,) * 4,
        [vm((fd, rows, nx), jnp.float32), vm((3 * own, cols, ny), jnp.float32), vm((cols, ny), jnp.float32),
         vm((rows, nx), jnp.int32), vm((2, rows, nx), jnp.float32), vm((rows, nx), jnp.int32),
         vm(near.shape, jnp.float32), vm(near.shape, jnp.float32), vm(far.shape, jnp.float32), vm(far.shape, jnp.float32),
         pltpu.SemaphoreType.DMA((chunks + 5,)), pltpu.SemaphoreType.DMA((chunks, 4, 3))],
    )
    hb, ha = up(near_hi), down(near_lo)
    arrived = lax.all_to_all(send, AXES, 0, 0, tiled=True)
    hbf, haf = up(far_hi), down(far_lo)

    geo = call(
        functools.partial(pick_kernel, (t_n, s_n, rows, cols, nx, fd), False),
        (arrived, land_mask, intersection), [VM] * 3, f32(4 * ext, nx), VM, [],
    )

    def scratch(kinds, grow):
        result = [vm((3, ext, SUB, nx), jnp.float32), vm((kinds, ext, SUB, nx), jnp.float32)]
        return result + [vm((2, grow, SUB, nx), jnp.float32)] if grow else result

    mid, total, growth0 = call(
        functools.partial(first_middle_kernel, (rows, fd, nx, chunks)),
        (table, geo, wind, natural), [VM] * 3 + [HB],
        (f32((rows - 2) * fd, nx), f32(ext, nx), f32(rows * fd, nx)), (VM,) * 3,
        [vm((fd, rows, nx), jnp.float32), vm((2, rows, SUB, nx), jnp.float32)] + scratch(1, 0)
        + [pltpu.SemaphoreType.DMA((chunks,))],
    )
    geo, winds, level_rim = call(
        functools.partial(pick_kernel, (t_n, s_n, rows, cols, nx, fd, own), True),
        (arrived, land_mask, intersection, wind, hb, ha, level_rim), [VM] * 7,
        (f32(4 * ext, nx), f32(2 * ext, nx), f32(6, cols + 8, ny)), (VM,) * 3, [],
    )

    planes = {k: {} for k in range(WSTEPS + 1)}
    for j in range(HALO):
        for base, sign, (a, b) in ((-1, -1, (hb, hbf)), (rows, 1, (ha, haf))):
            planes[0][base + sign * j] = (a if j < NEAR else b, (j % NEAR) * fd)
    for j in range(NEAR):
        planes[0][j] = (near_lo, j * fd)
        planes[0][rows - 1 - j] = (near_hi, j * fd)
    for k, r in enumerate(range(1, rows - 1)):
        planes[1][r] = (mid, k * fd)
    grown = {r: (growth0, r * fd) for r in range(rows)}
    totals, gots = {1: total}, {}

    def advanced(step, segments, exchange=True):
        raw, sums = step == 1, step == WSTEPS
        order = [r for segment in segments for r in segment]
        grow = [r for r in order if r not in grown]
        operands = []

        def place(pair):
            for k, array in enumerate(operands):
                if array is pair[0]:
                    return k, pair[1]
            operands.append(pair[0])
            return len(operands) - 1, pair[1]

        source = {r: place(planes[step - 1][r]) for r in sorted({r + d for r in order for d in (-1, 0, 1)})}
        growth = {r: place(grown[r]) for r in order if r in grown}
        args = [table, geo]
        if grow:
            args.append(winds)
        if not raw:
            args += [totals[step - 1], gots[step - 1]]
        joined = step in totals
        if joined:
            args.append(totals[step])
        if sums:
            args.append(intersection)
        args += operands
        shapes = [f32(len(order) * fd, nx), f32(devices, rows, nx) if sums else f32(ext, nx)]
        if grow:
            shapes.append(f32(len(grow) * fd, nx))
        cfg = (segments, source, growth, grow, raw, sums, joined, len(operands))
        outs = call(
            functools.partial(step_kernel, (rows, fd, nx, t_n, s_n, cols), cfg),
            args, [VM] * len(args), tuple(shapes), (VM,) * len(shapes), scratch(5 if sums else 1, len(grow)),
        )
        for k, r in enumerate(order):
            planes[step][r] = (outs[0], k * fd)
        for k, r in enumerate(grow):
            grown[r] = (outs[2], k * fd)
        totals[step] = outs[1]
        if exchange and not sums:
            gots[step] = others(outs[1])

    def pair(first, last):
        return [list(range(first, last + 1)), list(range(rows - 1 - last, rows - first))]

    advanced(1, pair(-1, 0))
    advanced(2, [list(range(rows))])
    advanced(3, [list(range(1, rows - 1))], exchange=False)
    level_got = others(level_rim)
    advanced(1, pair(-3, -2))
    advanced(2, pair(-2, -1))
    advanced(3, pair(-1, 0))
    totals[3], level_got = lax.optimization_barrier((totals[3], level_got))
    advanced(4, [list(range(rows))])

    landed = lax.all_to_all(totals[WSTEPS], AXES, 0, 0, tiled=True)
    pad = -(-ny // LANES) * LANES
    size = cols + 8
    ins = (table, levels, landed, geo, planes[WSTEPS][0][0], ocean, sea, hb, ha, level_got)
    waves, fields = call(
        functools.partial(last_kernel, (rows, fd, nx, t_n, s_n, cols, own, ny, chunks)),
        ins, [VM, SM] + [VM] * (len(ins) - 2), (f32(fd, rows, nx), f32(3, own, cols, ny)), (HB, HB),
        [
            vm((fd, rows, nx), jnp.float32),
            vm((rows, SUB, nx), jnp.float32),
            vm((pad, nx), jnp.float32),
            vm((3 * (own + 4), size, pad), jnp.float32),
            vm((3 * (own + 4), size, pad), jnp.float32),
            vm((3, own, cols, ny), jnp.float32),
            pltpu.SemaphoreType.DMA((chunks,)),
            pltpu.SemaphoreType.DMA,
        ],
    )
    return waves.reshape(spectrum.shape), fields.reshape(ocean_state.shape)


def solution(mesh):
    return jax.shard_map(
        functools.partial(program, mesh_shape=dict(mesh.shape)),
        mesh=mesh,
        in_specs=(
            P("grp", None, "spec", "tile", None),
            P(None, "tile", None),
            P("tile", None),
            P("tile", None),
            P("grp", None, "spec", "tile", None),
            P("grp", "tile", None),
        ),
        out_specs=(P("grp", None, "spec", "tile", None), P("grp", None, "spec", "tile", None)),
        check_vma=False,
    )
```

```python
import functools
import math

import jax
import jax.numpy as jnp
import numpy as np
from jax import lax
from jax.experimental import pallas as pl
from jax.experimental.pallas import tpu as pltpu
from jax.sharding import PartitionSpec as P


WSTEPS = 4
HALO = WSTEPS
LANES = 128
SUB = 8
UNROLL = 4
AXES = ("grp", "tile", "spec")

BW, GE, GN, WE, WN, SX, SY, DX, DY, INV = range(10)

VM = pl.BlockSpec(memory_space=pltpu.VMEM)
SM = pl.BlockSpec(memory_space=pltpu.SMEM)
HB = pl.BlockSpec(memory_space=pltpu.HBM)


def f32(*shape):
    return jax.ShapeDtypeStruct(shape, jnp.float32)


def wave_table(freqs, dirs, parts):
    frequency = 0.04 * 1.1 ** np.arange(freqs)
    celerity = 1.56 / frequency
    group = 0.4 * 1.1 ** (-np.arange(freqs, dtype=np.float64))
    width = 0.1 * frequency * (2.0 * math.pi / dirs)
    angle = 2.0 * math.pi * (np.arange(dirs) + 0.5) / dirs
    cos, sin, one = np.cos(angle), np.sin(angle), np.ones(dirs)
    columns = [
        np.outer(width, one),
        np.outer(group, cos),
        np.outer(group, sin),
        np.outer(0.05 / celerity, cos),
        np.outer(0.05 / celerity, sin),
        np.outer(5.0 / celerity, cos),
        np.outer(5.0 / celerity, sin),
        np.outer(20.0 * frequency**3, cos),
        np.outer(20.0 * frequency**3, sin),
        np.outer(1.0 / width, one),
    ]
    table = np.zeros((parts, freqs * dirs // parts, 16), np.float32)
    for k, column in enumerate(columns):
        split = column.reshape(freqs, parts, dirs // parts).transpose(1, 0, 2)
        table[:, :, k] = split.reshape(parts, -1)
    return table


def level_table(levels, parts, own):
    depth = (np.arange(levels) + 0.5) / levels
    profile = np.exp(-2.0 * depth)
    weights = profile / profile.sum()
    table = np.zeros((parts, 3, own + 4), np.float32)
    for s in range(parts):
        table[s, 0, :own] = weights[s * own : (s + 1) * own]
        for l in range(own + 4):
            g = s * own + l - 2
            if 0 <= g < levels:
                table[s, 1, l] = profile[g]
                table[s, 2, l] = 1.0
    return table


def lanes_of(shape):
    return lax.broadcasted_iota(jnp.int32, shape, len(shape) - 1)


def wide(column):
    return jnp.broadcast_to(column, (SUB, LANES))


def half(h):
    return slice(h * LANES, (h + 1) * LANES)


def barrel(values, shift, size, left):
    bit = 1
    while bit < size:
        taken = (shift & bit) != 0
        amount = size - bit if left else bit
        values = [jnp.where(taken, pltpu.roll(v, amount, 1), v) for v in values]
        bit *= 2
    return values


def start_kernel(n, level_ref, spectrum_ref, ocean_hbm, sea_hbm, mask_hbm, wind_hbm, cross_hbm,
                 out_ref, rim_ref, near_lo_hbm, near_hi_hbm, next_lo_hbm, next_hi_hbm, far_lo_hbm, far_hi_hbm,
                 raw, ocean, sea, mask_ref, wind_ref, cross_ref, near_lo, near_hi, next_lo, next_hi, far_lo, far_hi, sem, out_sem):
    t_n, s_n, rows, cols, own, ny, fd, nx, chunks = n
    s = lax.axis_index("spec")
    pad = -(-ny // LANES) * LANES
    part = fd // chunks
    small = ((ocean_hbm, ocean), (sea_hbm, sea), (mask_hbm, mask_ref), (wind_hbm, wind_ref), (cross_hbm, cross_ref))
    first = [pltpu.make_async_copy(a, b, sem.at[chunks + k]) for k, (a, b) in enumerate(small)]
    copies = [
        pltpu.make_async_copy(spectrum_ref.at[pl.ds(c * part, part)], raw.at[pl.ds(c * part, part)], sem.at[c])
        for c in range(chunks)
    ]
    for copy in first + copies:
        copy.start()
    for copy in first:
        copy.wait()
    parts = []
    for c in range(2):
        total = None
        for k in range(own):
            term = level_ref[s, 0, k] * ocean[c * own + k]
            total = term if total is None else total + term
        parts.append(total)
    parts.append(jnp.where(s == 0, sea[...], 0.0))
    for c in range(3):
        for k in range(2):
            rim_ref[c, k] = jnp.where(s == 0, ocean[c * own + own - 2 + k], ocean[c * own + k])
    stack = jnp.concatenate(parts, axis=0)
    stack = jnp.pad(stack, ((0, LANES - 3 * cols), (0, pad - ny)))
    edge = jnp.zeros((HALO, LANES), jnp.float32)
    turned = jnp.concatenate([edge, jnp.transpose(stack)[:ny], edge], axis=0)
    for t in range(t_n):
        for q in range(s_n):
            out_ref[t * s_n + q] = turned[t * rows : (t + 1) * rows + 2 * HALO, : 4 * cols]
    aux = [mask_ref[...].astype(jnp.float32), wind_ref[0], wind_ref[1], cross_ref[...].astype(jnp.float32)]
    for k, value in enumerate(aux):
        at = fd + k * HALO
        near_hi[at : at + HALO] = value[rows - HALO : rows]
        near_lo[at : at + HALO] = value[0:HALO]

    held = ((near_lo, near_lo_hbm), (near_hi, near_hi_hbm), (next_lo, next_lo_hbm), (next_hi, next_hi_hbm),
            (far_lo, far_lo_hbm), (far_hi, far_hi_hbm))
    outward = []

    def send_out(c):
        for k, (here, there) in enumerate(held):
            for j in range(here.shape[0] // fd):
                span = pl.ds(j * fd + c * part, part)
                outward.append(pltpu.make_async_copy(here.at[span], there.at[span], out_sem.at[c, k, j]))
                outward[-1].start()
            if c == 0 and k < 2:
                span = pl.ds(fd, 4 * HALO)
                outward.append(pltpu.make_async_copy(here.at[span], there.at[span], out_sem.at[c, k, HALO]))
                outward[-1].start()

    for c in range(chunks):
        copies[c].wait()

        def turn(i, carry):
            for k in range(2):
                at = pl.multiple_of(c * part + (2 * i + k) * SUB, SUB)
                for h in range(nx // LANES):
                    planes = jnp.swapaxes(raw[pl.ds(at, SUB), :, half(h)], 0, 1)
                    for j in range(HALO):
                        lo_ref, hi_ref = ((near_lo, near_hi), (next_lo, next_hi), (far_lo, far_hi))[min(j, 2)]
                        sl = pl.ds(pl.multiple_of(at + max(j - 2, 0) * fd, SUB), SUB)
                        lo_ref[sl, half(h)] = planes[j]
                        hi_ref[sl, half(h)] = planes[rows - 1 - j]
            return carry

        lax.fori_loop(0, part // (2 * SUB), turn, 0)
        if c:
            send_out(c)

    @pl.when(lax.axis_index("grp") == 1)
    def _():
        stack = 3 * own
        for k in range(2):
            for ref, at in ((near_lo, k), (near_hi, cols - 2 + k)):
                for m in range(stack):
                    ref[k * stack + m : k * stack + m + 1, 0:ny] = ocean[m, at : at + 1, :]
                ref[2 * stack + k : 2 * stack + k + 1, 0:ny] = sea[at : at + 1, :]

    send_out(0)
    for copy in outward:
        copy.wait()


def pick_kernel(n, full, got_ref, mask_ref, cross_ref, *refs):
    t_n, s_n, rows, cols, nx, fd = n[:6]
    ext = rows + 2 * HALO
    lane = lanes_of((ext, LANES))
    per = LANES // cols
    fields = [[jnp.zeros((ext, LANES), jnp.float32) for _ in range(nx // LANES)] for _ in range(3)]
    for t in range(t_n):
        tile = got_ref[(t_n + t) * s_n]
        for q in range(1, s_n):
            tile = tile + got_ref[(t_n + t) * s_n + q]
        if tile.shape[1] < LANES:
            tile = jnp.pad(tile, ((0, 0), (0, LANES - tile.shape[1])))
        h, at = t // per, (t % per) * cols
        inside = (lane >= at) & (lane < at + cols)
        for c in range(3):
            moved = pltpu.roll(tile, (at - c * cols) % LANES, 1) if (at - c * cols) % LANES else tile
            fields[c][h] = jnp.where(inside, moved, fields[c][h])
    whole = [jnp.concatenate(f, axis=1) for f in fields]
    wet, shift = mask_ref[...].astype(jnp.float32), cross_ref[...].astype(jnp.float32)
    if full:
        wind_ref, hb_ref, ha_ref, rim_ref, geo_ref, out_ref, edge_ref = refs
        own, ny = n[6], rim_ref.shape[3]
        low = lax.axis_index("spec") == 0
        for c in range(3):
            for k in range(2):
                edge_ref[c * 2 + k] = jnp.zeros((cols + 8, ny), jnp.float32)
                edge_ref[c * 2 + k, 4 : 4 + cols] = rim_ref[c, k]
                for m in range(2):
                    for ref, at in ((hb_ref, 2 + m), (ha_ref, 4 + cols + m)):
                        top, bottom = [m * 3 * own + c * own + j for j in (own - 2 + k, k)]
                        value = jnp.where(low, ref[top : top + 1, 0:ny], ref[bottom : bottom + 1, 0:ny])
                        edge_ref[c * 2 + k, at : at + 1] = value

        def joined(k, own):
            span = slice(fd + k * HALO, fd + (k + 1) * HALO)
            return jnp.concatenate([hb_ref[span], own, ha_ref[span]], axis=0)

        wet, shift = joined(0, wet), joined(3, shift)
        for c in range(2):
            out_ref[c * ext : (c + 1) * ext] = joined(1 + c, wind_ref[c])
    else:
        (geo_ref,) = refs
        edge = jnp.zeros((HALO, nx), jnp.float32)
        wet, shift = [jnp.concatenate([edge, x, edge], axis=0) for x in (wet, shift)]
    shift = jnp.broadcast_to(shift[:, 0:1].astype(jnp.int32), (ext, nx))
    u, v, sea = barrel(whole, shift, nx, True)
    depth = 10.0 + 4.0 * sea
    for k, value in enumerate((0.1 * u, 0.1 * v, 25.0 / (depth * depth), wet)):
        geo_ref[k * ext : (k + 1) * ext] = value


def advance(segments, fd, nx, s, table_ref, planes, store, splat, acc, sums, before=None):
    halves = nx // LANES
    lane = lanes_of((SUB, LANES))
    first, last = lane == 0, lane == LANES - 1
    acc[...] = jnp.zeros(acc.shape, jnp.float32)

    def body(i, carry):
        if before is not None:
            before(i)
        totals = {}

        def add(key, value):
            totals[key] = totals[key] + value if key in totals else value

        for k in range(UNROLL):
            at = pl.multiple_of((i * UNROLL + k) * SUB, SUB)
            sl = pl.ds(at, SUB)
            ge, gn = wide(table_ref[s, sl, GE : GE + 1]), wide(table_ref[s, sl, GN : GN + 1])
            bands = [wide(table_ref[s, sl, b : b + 1]) for b in (SX, SY, DX, DY)] if sums else None
            energy, growth = planes(at)
            for segment in segments:
                def state(r):
                    e = [energy(r, h) * splat[2, r + HALO, :, half(h)] for h in range(halves)]
                    north = [(gn + splat[1, r + HALO, :, half(h)]) * e[h] for h in range(halves)]
                    return e, north

                here, below = state(segment[0]), state(segment[0] - 1)
                flow = [jnp.maximum(below[1][h], 0.0) + jnp.minimum(here[1][h], 0.0) for h in range(halves)]
                for r in segment:
                    above = state(r + 1)
                    e, north = here
                    upper = [jnp.maximum(north[h], 0.0) + jnp.minimum(above[1][h], 0.0) for h in range(halves)]
                    east = [(ge + splat[0, r + HALO, :, half(h)]) * e[h] for h in range(halves)]
                    left = [pltpu.roll(x, LANES - 1, 1) for x in east]
                    flux = [
                        jnp.maximum(east[h], 0.0)
                        + jnp.minimum(jnp.where(last, left[h + 1] if h + 1 < halves else 0.0, left[h]), 0.0)
                        for h in range(halves)
                    ]
                    right = [pltpu.roll(x, 1, 1) for x in flux]
                    for h in range(halves):
                        behind = jnp.where(first, right[h - 1] if h else jnp.minimum(east[0], 0.0), right[h])
                        advected = (e[h] - (flux[h] - behind)) - (upper[h] - flow[h])
                        g = growth(r, h)
                        add((0, r, h), advected)
                        if sums:
                            grown = g * advected
                            pushed = grown - advected
                            for b in range(2):
                                add((1 + b, r, h), bands[b] * pushed)
                                add((3 + b, r, h), bands[2 + b] * grown)
                        else:
                            grown = g * advected
                        store(r, at, h, grown)
                    here, flow = above, upper
        for (kind, r, h), value in totals.items():
            acc[kind, r + HALO, :, half(h)] += value
        return carry

    lax.fori_loop(0, fd // (SUB * UNROLL), body, 0)


def folded(acc, kind, rows):
    return [jnp.sum(acc[kind, r + HALO], axis=0, keepdims=True) for r in rows]


def fill(splat, kind, row, value, nx):
    splat[kind, row + HALO] = jnp.broadcast_to(value, (SUB, nx))


def geometry(geo_ref, ext, kind, r):
    at = kind * ext + r + HALO
    return geo_ref[at : at + 1]


def write_totals(total_ref, acc, rows, previous, ext, nx):
    total_ref[...] = jnp.zeros((ext, nx), jnp.float32) if previous is None else previous[...]
    for r, value in zip(rows, folded(acc, 0, rows)):
        total_ref[r + HALO : r + HALO + 1] = value


def first_middle_kernel(n, table_ref, geo_ref, wind_ref, spectrum_ref,
                        out_ref, total_ref, growth_ref, raw, windb, splat, acc, sem):
    rows, fd, nx, chunks = n
    ext = rows + 2 * HALO
    s = lax.axis_index("spec")
    part = fd // chunks
    turns = part // (SUB * UNROLL)

    def copy(c):
        span = pl.ds(pl.multiple_of(c * part, SUB), part)
        return pltpu.make_async_copy(spectrum_ref.at[span], raw.at[span], sem.at[c])

    for c in range(chunks):
        copy(c).start()
    for c in range(2):
        for r in range(rows):
            windb[c, r] = jnp.broadcast_to(wind_ref[c, r : r + 1], (SUB, nx))
    for r in range(rows):
        for kind, source in ((0, 0), (1, 1), (2, 3)):
            fill(splat, kind, r, geometry(geo_ref, ext, source, r), nx)

    def before(i):
        @pl.when(i % turns == 0)
        def _():
            copy(i // turns).wait()

    def planes(at):
        sl = pl.ds(at, SUB)
        bw, we, wn = [wide(table_ref[s, sl, b : b + 1]) for b in (BW, WE, WN)]
        natural, grown = {}, {}
        for h in range(nx // LANES):
            natural[h] = jnp.swapaxes(raw[sl, :, half(h)], 0, 1)
            for r in range(rows):
                drive = we * windb[0, r, :, half(h)] + wn * windb[1, r, :, half(h)]
                grown[r, h] = 1.0 + jnp.maximum(drive - 0.05, 0.0)
                growth_ref[pl.ds(pl.multiple_of(r * fd + at, SUB), SUB), half(h)] = grown[r, h]
        return lambda r, h: bw * natural[h][r], lambda r, h: grown[r, h]

    def store(r, at, h, value):
        out_ref[pl.ds(pl.multiple_of((r - 1) * fd + at, SUB), SUB), half(h)] = value

    inner = list(range(1, rows - 1))
    advance([inner], fd, nx, s, table_ref, planes, store, splat, acc, False, before)
    write_totals(total_ref, acc, inner, None, ext, nx)


def step_kernel(n, cfg, *refs):
    rows, fd, nx, t_n, s_n, cols = n
    segments, source, growth, grow, raw, sums, joined, count = cfg
    ext = rows + 2 * HALO
    refs = list(refs)
    table_ref, geo_ref = refs.pop(0), refs.pop(0)
    wind_ref = refs.pop(0) if grow else None
    own_ref, got_ref = (None, None) if raw else (refs.pop(0), refs.pop(0))
    previous = refs.pop(0) if joined else None
    cross_ref = refs.pop(0) if sums else None
    operands, refs = refs[:count], refs[count:]
    out_ref, total_ref = refs.pop(0), refs.pop(0)
    growth_ref = refs.pop(0) if grow else None
    splat, acc = refs.pop(0), refs.pop(0)
    windb = refs.pop(0) if grow else None
    s = lax.axis_index("spec")
    order = [r for segment in segments for r in segment]
    needed = sorted({r + d for r in order for d in (-1, 0, 1)})
    breaking = geo_ref[3 * ext : 4 * ext]
    if not raw:
        breaking = breaking / (1.0 + (own_ref[...] + got_ref[...]) * geo_ref[2 * ext : 3 * ext])
    for r in needed:
        fill(splat, 0, r, geometry(geo_ref, ext, 0, r), nx)
        fill(splat, 1, r, geometry(geo_ref, ext, 1, r), nx)
        fill(splat, 2, r, breaking[r + HALO : r + HALO + 1], nx)
    for c in range(2):
        for k, r in enumerate(grow):
            at = c * ext + r + HALO
            windb[c, k] = jnp.broadcast_to(wind_ref[at : at + 1], (SUB, nx))

    def load(place, at, h):
        found, first = place
        parts = [operands[k][pl.ds(pl.multiple_of(first + at, SUB), SUB), half(h)] for k in found]
        return functools.reduce(lambda a, b: a + b, parts)

    def planes(at):
        sl = pl.ds(at, SUB)
        bw = wide(table_ref[s, sl, BW : BW + 1]) if raw else None
        we, wn = [wide(table_ref[s, sl, b : b + 1]) for b in (WE, WN)] if grow else (None, None)

        def energy(r, h):
            value = load(source[r], at, h)
            return bw * value if raw else value

        def factor(r, h):
            if r in grow:
                k = grow.index(r)
                drive = we * windb[0, k, :, half(h)] + wn * windb[1, k, :, half(h)]
                value = 1.0 + jnp.maximum(drive - 0.05, 0.0)
                growth_ref[pl.ds(pl.multiple_of(k * fd + at, SUB), SUB), half(h)] = value
                return value
            return load(growth[r], at, h)

        return energy, factor

    def store(r, at, h, value):
        out_ref[pl.ds(pl.multiple_of(order.index(r) * fd + at, SUB), SUB), half(h)] = value

    advance(segments, fd, nx, s, table_ref, planes, store, splat, acc, sums)
    if not sums:
        write_totals(total_ref, acc, order, previous, ext, nx)
        return
    kinds = [jnp.concatenate(folded(acc, kind, order), axis=0) for kind in range(acc.shape[0])]
    wet = jnp.where(s == 0, geo_ref[3 * ext + HALO : 3 * ext + HALO + rows], 0.0)
    shift = jnp.broadcast_to(cross_ref[:, 0:1], (rows, nx))
    moved = barrel(kinds + [wet], shift, nx, False)
    lane = lanes_of((rows, nx))
    size = cols + 8
    for t in range(t_n):
        chunk = jnp.zeros((rows, nx), jnp.float32)
        for q, value in enumerate(moved):
            amount = (q * size - (cols * t - 4)) % nx
            piece = pltpu.roll(value, amount, 1) if amount else value
            chunk = jnp.where((lane >= q * size) & (lane < (q + 1) * size), piece, chunk)
        for q in range(s_n):
            total_ref[(t_n + t) * s_n + q] = chunk
    mine = lax.axis_index("tile")
    for q in range(s_n):
        total_ref[mine * s_n + q] = kinds[0]


def last_kernel(n, table_ref, level_ref, got_ref, geo_ref, wave_ref, ocean_ref, sea_ref,
                hb_ref, ha_ref, lev_ref, waves_ref, next_ref,
                raw, brk, turn, field, mix, out, sem, osem):
    rows, fd, nx, t_n, s_n, cols, own, ny, chunks = n
    s = lax.axis_index("spec")
    g = lax.axis_index("grp")
    tile = lax.axis_index("tile")
    part = fd // chunks
    pad = turn.shape[0]
    size = cols + 8

    def write(c, source):
        return pltpu.make_async_copy(raw.at[pl.ds(source * part, part)], waves_ref.at[pl.ds(c * part, part)], sem.at[c])

    ocean_copy = pltpu.make_async_copy(out, next_ref, osem)

    @pl.when(g == 0)
    def _():
        total = got_ref[tile * s_n]
        for q in range(1, s_n):
            total = total + got_ref[tile * s_n + q]
        ext = rows + 2 * HALO
        wet = geo_ref[3 * ext + HALO : 3 * ext + HALO + rows]
        breaking = wet / (1.0 + total * geo_ref[2 * ext + HALO : 2 * ext + HALO + rows])
        for r in range(rows):
            brk[r] = jnp.broadcast_to(breaking[r : r + 1], (SUB, nx))
        for c in range(chunks):

            def finish(i, carry):
                for k in range(2):
                    at = pl.multiple_of(c * part + (2 * i + k) * SUB, SUB)
                    sl = pl.ds(at, SUB)
                    inv = wide(table_ref[s, sl, INV : INV + 1])
                    for h in range(nx // LANES):
                        spans = [pl.ds(pl.multiple_of(r * fd + at, SUB), SUB) for r in range(rows)]
                        values = [wave_ref[span, half(h)] for span in spans]
                        values = [value * brk[r, :, half(h)] * inv for r, value in enumerate(values)]
                        raw[sl, :, half(h)] = jnp.swapaxes(jnp.stack(values), 0, 1)
                return carry

            lax.fori_loop(0, part // (2 * SUB), finish, 0)
            write(c, c).start()
        out[...] = jnp.zeros((3, own, cols, ny), jnp.float32)
        ocean_copy.start()
        ocean_copy.wait()
        for c in range(chunks):
            write(c, c).wait()

    @pl.when(g == 1)
    def _():
        def clear(i, carry):
            raw[pl.ds(pl.multiple_of(i * SUB, SUB), SUB)] = jnp.zeros((SUB, rows, nx), jnp.float32)
            return carry

        lax.fori_loop(0, part // SUB, clear, 0)
        for c in range(chunks):
            write(c, 0).start()

        if pad > ny:
            turn[ny:pad] = jnp.zeros((pad - ny, nx), jnp.float32)
        for t in range(t_n):
            tilev = got_ref[t * s_n]
            for q in range(1, s_n):
                tilev = tilev + got_ref[t * s_n + q]
            turn[t * rows : (t + 1) * rows] = tilev
        turned = jnp.transpose(turn[...])
        total, sx, sy, dx, dy, wet = [turned[q * size : (q + 1) * size] for q in range(6)]
        row = lax.broadcasted_iota(jnp.int32, (size, pad), 0)
        column = row + (tile * cols - 4)
        wet = jnp.where((column >= 0) & (column < t_n * cols), wet, 0.0)
        stack = 3 * own
        mix[0] = jnp.zeros((size, pad), jnp.float32)
        mix[0, 4 : 4 + cols, 0:ny] = sea_ref[...]
        mix[0, 2:4, 0:ny] = hb_ref[2 * stack : 2 * stack + 2, 0:ny]
        mix[0, 4 + cols : 6 + cols, 0:ny] = ha_ref[2 * stack : 2 * stack + 2, 0:ny]
        depth = 10.0 + 4.0 * mix[0]
        breaking = 1.0 / (1.0 + 25.0 * total / (depth * depth))
        swept = wet * breaking
        sx, sy, dx, dy = sx * breaking, sy * breaking, dx * swept, dy * swept

        field[...] = jnp.zeros(field.shape, jnp.float32)
        ext = own + 4
        for c in range(3):
            for k in range(own):
                l = c * ext + 2 + k
                field[l, 4 : 4 + cols, 0:ny] = ocean_ref[c, k]
                for m in range(2):
                    at = m * stack + c * own + k
                    field[l, 2 + m : 3 + m, 0:ny] = hb_ref[at : at + 1, 0:ny]
                    field[l, 4 + cols + m : 5 + cols + m, 0:ny] = ha_ref[at : at + 1, 0:ny]
        for upper in range(2):
            @pl.when(s == 1 - upper)
            def _():
                for c in range(3):
                    for k in range(2):
                        l = c * ext + (own + 2 if upper else 0) + k
                        field[l, :, 0:ny] = lev_ref[c * 2 + k]

        lane = lanes_of((size, pad))

        def new_fields(source, k):
            values = []
            for c in range(3):
                q = source[c * ext + k]
                lateral = (
                    pltpu.roll(q, size - 1, 0)
                    + pltpu.roll(q, 1, 0)
                    + jnp.where(lane == ny - 1, 0.0, pltpu.roll(q, pad - 1, 1))
                    + jnp.where(lane == 0, 0.0, pltpu.roll(q, 1, 1))
                    - 4.0 * q
                )
                vertical = source[c * ext + k + 1] + source[c * ext + k - 1] - 2.0 * q
                values.append((q, q + 0.1 * lateral + 0.2 * vertical))
            (u, du), (v, dv), (_, dt) = values
            shaped = level_ref[s, 1, k]
            top = jnp.where((s == 0) & (k == 2), 1.0, 0.0)
            east = du + 0.1 * (v + shaped * dy) + top * sx
            north = dv - 0.1 * (u + shaped * dx) + top * sy
            keep = wet * level_ref[s, 2, k]
            return keep * east, keep * north, keep * dt

        for k in range(1, ext - 1):
            for c, value in enumerate(new_fields(field, k)):
                mix[c * ext + k] = value
        for k in range(2, ext - 2):
            for c, value in enumerate(new_fields(mix, k)):
                out[c, k - 2] = value[4 : 4 + cols, 0:ny]
        ocean_copy.start()
        ocean_copy.wait()
        for c in range(chunks):
            write(c, 0).wait()


def program(spectrum, wind, land_mask, intersection, ocean_state, sea_level, *, mesh_shape):
    g_n, t_n, s_n = (mesh_shape[a] for a in AXES)
    _, freqs, dirs, rows, nx = spectrum.shape
    _, _, own, cols, ny = ocean_state.shape
    fd = freqs * dirs
    devices = g_n * t_n * s_n
    table = jnp.asarray(wave_table(freqs, dirs * s_n, s_n))
    levels = jnp.asarray(level_table(own * s_n, s_n, own))
    ocean = ocean_state[0]
    sea = sea_level[0]

    def in_hbm(x):
        return pltpu.with_memory_space_constraint(x, pltpu.HBM)

    natural = in_hbm(spectrum.reshape(fd, rows, nx))
    chunks = 6
    vm = pltpu.VMEM
    params = pltpu.CompilerParams(vmem_limit_bytes=24 << 20)

    def up(x, without=None):
        return lax.ppermute(x, "tile", [(i, i + 1) for i in range(t_n - 1) if i + 1 != without])

    def down(x, without=None):
        return lax.ppermute(x, "tile", [(i + 1, i) for i in range(t_n - 1) if i + 1 != without])

    def others(x):
        return added(lax.ppermute(x, "spec", [(i, (i + k) % s_n) for i in range(s_n)]) for k in range(1, s_n))

    def added(values):
        return functools.reduce(lambda a, b: a + b, values)

    def call(kernel, args, specs, shapes, out_specs, scratch):
        return pl.pallas_call(
            kernel, out_shape=shapes, in_specs=specs, out_specs=out_specs,
            scratch_shapes=scratch, compiler_params=params,
        )(*args)

    ext = rows + 2 * HALO
    near, second, far = f32(fd + 4 * HALO, nx), f32(fd, nx), f32((HALO - 2) * fd, nx)

    def hbm(shape):
        return pltpu.HBM(shape.shape, shape.dtype)

    send, level_rim, near_lo, near_hi, next_lo, next_hi, far_lo, far_hi = call(
        functools.partial(start_kernel, (t_n, s_n, rows, cols, own, ny, fd, nx, chunks)),
        (levels, natural, in_hbm(ocean.reshape(3 * own, cols, ny)), in_hbm(sea), in_hbm(land_mask), in_hbm(wind), in_hbm(intersection)),
        [SM] + [HB] * 6,
        (f32(devices, ext, 4 * cols), f32(3, 2, cols, ny), hbm(near), hbm(near), hbm(second), hbm(second), hbm(far), hbm(far)),
        (VM,) * 2 + (HB,) * 6,
        [vm((fd, rows, nx), jnp.float32), vm((3 * own, cols, ny), jnp.float32), vm((cols, ny), jnp.float32),
         vm((rows, nx), jnp.int32), vm((2, rows, nx), jnp.float32), vm((rows, nx), jnp.int32),
         vm(near.shape, jnp.float32), vm(near.shape, jnp.float32),
         vm(second.shape, jnp.float32), vm(second.shape, jnp.float32), vm(far.shape, jnp.float32), vm(far.shape, jnp.float32),
         pltpu.SemaphoreType.DMA((chunks + 5,)), pltpu.SemaphoreType.DMA((chunks, 6, HALO + 1))],
    )
    hb, ha = up(near_hi), down(near_lo)
    arrived = lax.all_to_all(send, AXES, 0, 0, tiled=True)
    hbn, han = up(next_hi), down(next_lo)
    middle = t_n // 2
    turn_up = lax.ppermute(far_hi, "tile", [(middle - 1, t_n - 1)])
    turn_down = lax.ppermute(far_lo, "tile", [(middle, 0)])
    hbf, haf = up(far_hi, middle), down(far_lo, middle)
    hbt = lax.ppermute(turn_up, "tile", [(t_n - 1, middle)])
    hat = lax.ppermute(turn_down, "tile", [(0, middle - 1)])

    geo = call(
        functools.partial(pick_kernel, (t_n, s_n, rows, cols, nx, fd), False),
        (arrived, land_mask, intersection), [VM] * 3, f32(4 * ext, nx), VM, [],
    )

    def scratch(kinds, grow):
        result = [vm((3, ext, SUB, nx), jnp.float32), vm((kinds, ext, SUB, nx), jnp.float32)]
        return result + [vm((2, grow, SUB, nx), jnp.float32)] if grow else result

    mid, total, growth0 = call(
        functools.partial(first_middle_kernel, (rows, fd, nx, chunks)),
        (table, geo, wind, natural), [VM] * 3 + [HB],
        (f32((rows - 2) * fd, nx), f32(ext, nx), f32(rows * fd, nx)), (VM,) * 3,
        [vm((fd, rows, nx), jnp.float32), vm((2, rows, SUB, nx), jnp.float32)] + scratch(1, 0)
        + [pltpu.SemaphoreType.DMA((chunks,))],
    )
    geo, winds, level_rim = call(
        functools.partial(pick_kernel, (t_n, s_n, rows, cols, nx, fd, own), True),
        (arrived, land_mask, intersection, wind, hb, ha, level_rim), [VM] * 7,
        (f32(4 * ext, nx), f32(2 * ext, nx), f32(6, cols + 8, ny)), (VM,) * 3, [],
    )

    planes = {k: {} for k in range(WSTEPS + 1)}
    for j in range(HALO):
        k, at = min(j, 2), max(j - 2, 0) * fd
        planes[0][-1 - j] = (((hb,), (hbn,), (hbf, hbt))[k], at)
        planes[0][rows + j] = (((ha,), (han,), (haf, hat))[k], at)
        if j < 2:
            planes[0][j] = (((near_lo,), (next_lo,))[j], 0)
            planes[0][rows - 1 - j] = (((near_hi,), (next_hi,))[j], 0)
    for k, r in enumerate(range(1, rows - 1)):
        planes[1][r] = ((mid,), k * fd)
    grown = {r: ((growth0,), r * fd) for r in range(rows)}
    totals, gots = {1: total}, {}

    def advanced(step, segments, exchange=True):
        raw, sums = step == 1, step == WSTEPS
        order = [r for segment in segments for r in segment]
        grow = [r for r in order if r not in grown]
        operands = []

        def place(item):
            found = []
            for array in item[0]:
                known = [k for k, other in enumerate(operands) if other is array]
                if not known:
                    operands.append(array)
                found.append(known[0] if known else len(operands) - 1)
            return tuple(found), item[1]

        source = {r: place(planes[step - 1][r]) for r in sorted({r + d for r in order for d in (-1, 0, 1)})}
        growth = {r: place(grown[r]) for r in order if r in grown}
        args = [table, geo]
        if grow:
            args.append(winds)
        if not raw:
            args += [totals[step - 1], gots[step - 1]]
        joined = step in totals
        if joined:
            args.append(totals[step])
        if sums:
            args.append(intersection)
        args += operands
        shapes = [f32(len(order) * fd, nx), f32(devices, rows, nx) if sums else f32(ext, nx)]
        if grow:
            shapes.append(f32(len(grow) * fd, nx))
        cfg = (segments, source, growth, grow, raw, sums, joined, len(operands))
        outs = call(
            functools.partial(step_kernel, (rows, fd, nx, t_n, s_n, cols), cfg),
            args, [VM] * len(args), tuple(shapes), (VM,) * len(shapes), scratch(5 if sums else 1, len(grow)),
        )
        for k, r in enumerate(order):
            planes[step][r] = ((outs[0],), k * fd)
        for k, r in enumerate(grow):
            grown[r] = ((outs[2],), k * fd)
        totals[step] = outs[1]
        if exchange and not sums:
            gots[step] = others(outs[1])

    def pair(first, last):
        return [list(range(first, last + 1)), list(range(rows - 1 - last, rows - first))]

    advanced(1, pair(-1, 0))
    advanced(2, [list(range(rows))])
    advanced(1, pair(-3, -2))
    advanced(3, [list(range(1, rows - 1))], exchange=False)
    level_got = others(level_rim)
    advanced(2, pair(-2, -1))
    advanced(3, pair(-1, 0))
    totals[3], level_got = lax.optimization_barrier((totals[3], level_got))
    advanced(4, [list(range(rows))])

    landed = lax.all_to_all(totals[WSTEPS], AXES, 0, 0, tiled=True)
    pad = -(-ny // LANES) * LANES
    size = cols + 8
    ins = (table, levels, landed, geo, planes[WSTEPS][0][0][0], ocean, sea, hb, ha, level_got)
    waves, fields = call(
        functools.partial(last_kernel, (rows, fd, nx, t_n, s_n, cols, own, ny, chunks)),
        ins, [VM, SM] + [VM] * (len(ins) - 2), (f32(fd, rows, nx), f32(3, own, cols, ny)), (HB, HB),
        [
            vm((fd, rows, nx), jnp.float32),
            vm((rows, SUB, nx), jnp.float32),
            vm((pad, nx), jnp.float32),
            vm((3 * (own + 4), size, pad), jnp.float32),
            vm((3 * (own + 4), size, pad), jnp.float32),
            vm((3, own, cols, ny), jnp.float32),
            pltpu.SemaphoreType.DMA((chunks,)),
            pltpu.SemaphoreType.DMA,
        ],
    )
    return waves.reshape(spectrum.shape), fields.reshape(ocean_state.shape)


def solution(mesh):
    return jax.shard_map(
        functools.partial(program, mesh_shape=dict(mesh.shape)),
        mesh=mesh,
        in_specs=(
            P("grp", None, "spec", "tile", None),
            P(None, "tile", None),
            P("tile", None),
            P("tile", None),
            P("grp", None, "spec", "tile", None),
            P("grp", "tile", None),
        ),
        out_specs=(P("grp", None, "spec", "tile", None), P("grp", None, "spec", "tile", None)),
        check_vma=False,
    )
```

```python
import functools
import math

import jax
import jax.numpy as jnp
import numpy as np
from jax import lax
from jax.experimental import pallas as pl
from jax.experimental.pallas import tpu as pltpu
from jax.sharding import PartitionSpec as P


WSTEPS = 4
HALO = WSTEPS
LANES = 128
SUB = 8
UNROLL = 4
AXES = ("grp", "tile", "spec")

BW, GE, GN, WE, WN, SX, SY, DX, DY, INV = range(10)

VM = pl.BlockSpec(memory_space=pltpu.VMEM)
SM = pl.BlockSpec(memory_space=pltpu.SMEM)
HB = pl.BlockSpec(memory_space=pltpu.HBM)


def f32(*shape):
    return jax.ShapeDtypeStruct(shape, jnp.float32)


def wave_table(freqs, dirs, parts):
    frequency = 0.04 * 1.1 ** np.arange(freqs)
    celerity = 1.56 / frequency
    group = 0.4 * 1.1 ** (-np.arange(freqs, dtype=np.float64))
    width = 0.1 * frequency * (2.0 * math.pi / dirs)
    angle = 2.0 * math.pi * (np.arange(dirs) + 0.5) / dirs
    cos, sin, one = np.cos(angle), np.sin(angle), np.ones(dirs)
    columns = [
        np.outer(width, one),
        np.outer(group, cos),
        np.outer(group, sin),
        np.outer(0.05 / celerity, cos),
        np.outer(0.05 / celerity, sin),
        np.outer(5.0 / celerity, cos),
        np.outer(5.0 / celerity, sin),
        np.outer(20.0 * frequency**3, cos),
        np.outer(20.0 * frequency**3, sin),
        np.outer(1.0 / width, one),
    ]
    table = np.zeros((parts, freqs * dirs // parts, 16), np.float32)
    for k, column in enumerate(columns):
        split = column.reshape(freqs, parts, dirs // parts).transpose(1, 0, 2)
        table[:, :, k] = split.reshape(parts, -1)
    return table


def level_table(levels, parts, own):
    depth = (np.arange(levels) + 0.5) / levels
    profile = np.exp(-2.0 * depth)
    weights = profile / profile.sum()
    table = np.zeros((parts, 3, own + 4), np.float32)
    for s in range(parts):
        table[s, 0, :own] = weights[s * own : (s + 1) * own]
        for l in range(own + 4):
            g = s * own + l - 2
            if 0 <= g < levels:
                table[s, 1, l] = profile[g]
                table[s, 2, l] = 1.0
    return table


def lanes_of(shape):
    return lax.broadcasted_iota(jnp.int32, shape, len(shape) - 1)


def wide(column):
    return jnp.broadcast_to(column, (SUB, LANES))


def half(h):
    return slice(h * LANES, (h + 1) * LANES)


def barrel(values, shift, size, left):
    bit = 1
    while bit < size:
        taken = (shift & bit) != 0
        amount = size - bit if left else bit
        values = [jnp.where(taken, pltpu.roll(v, amount, 1), v) for v in values]
        bit *= 2
    return values


def start_kernel(n, level_ref, spectrum_ref, ocean_hbm, sea_hbm, mask_hbm, wind_hbm, cross_hbm,
                 out_ref, rim_ref, near_a, near_b, next_a, next_b, far_a, far_b, turn_hbm,
                 raw, ocean, sea, mask_ref, wind_ref, cross_ref, near_lo, near_hi, next_lo, next_hi, far_lo, far_hi, sem, out_sem):
    t_n, s_n, rows, cols, own, ny, fd, nx, chunks = n
    s = lax.axis_index("spec")
    pad = -(-ny // LANES) * LANES
    part = fd // chunks
    small = ((ocean_hbm, ocean), (sea_hbm, sea), (mask_hbm, mask_ref), (wind_hbm, wind_ref), (cross_hbm, cross_ref))
    first = [pltpu.make_async_copy(a, b, sem.at[chunks + k]) for k, (a, b) in enumerate(small)]
    copies = [
        pltpu.make_async_copy(spectrum_ref.at[pl.ds(c * part, part)], raw.at[pl.ds(c * part, part)], sem.at[c])
        for c in range(chunks)
    ]
    for copy in first + copies:
        copy.start()
    for copy in first:
        copy.wait()
    parts = []
    for c in range(2):
        total = None
        for k in range(own):
            term = level_ref[s, 0, k] * ocean[c * own + k]
            total = term if total is None else total + term
        parts.append(total)
    parts.append(jnp.where(s == 0, sea[...], 0.0))
    for c in range(3):
        for k in range(2):
            rim_ref[c, k] = jnp.where(s == 0, ocean[c * own + own - 2 + k], ocean[c * own + k])
    stack = jnp.concatenate(parts, axis=0)
    stack = jnp.pad(stack, ((0, LANES - 3 * cols), (0, pad - ny)))
    edge = jnp.zeros((HALO, LANES), jnp.float32)
    turned = jnp.concatenate([edge, jnp.transpose(stack)[:ny], edge], axis=0)
    for t in range(t_n):
        for q in range(s_n):
            out_ref[t * s_n + q] = turned[t * rows : (t + 1) * rows + 2 * HALO, : 4 * cols]
    aux = [mask_ref[...].astype(jnp.float32), wind_ref[0], wind_ref[1], cross_ref[...].astype(jnp.float32)]
    for k, value in enumerate(aux):
        at = fd + k * HALO
        near_hi[at : at + HALO] = value[rows - HALO : rows]
        near_lo[at : at + HALO] = value[0:HALO]

    held = ((near_lo, near_hi, near_a, near_b), (next_lo, next_hi, next_a, next_b), (far_lo, far_hi, far_a, far_b))
    tile = lax.axis_index("tile")
    even = tile % 2 == 0
    outward = []

    def send_out(c):
        moves = []
        for k, (low, high, a, b) in enumerate(held):
            spans = [pl.ds(j * fd + c * part, part) for j in range(low.shape[0] // fd)]
            if c == 0 and k == 0:
                spans.append(pl.ds(fd, 4 * HALO))
            for j, span in enumerate(spans):
                moves.append((low, high, a, span, out_sem.at[c, 2 * k, j]))
                moves.append((high, low, b, span, out_sem.at[c, 2 * k + 1, j]))
        for side in range(2):

            @pl.when(even if side else jnp.logical_not(even))
            def _():
                for move in moves:
                    source, target, span, mark = move[side], *move[2:]
                    pltpu.make_async_copy(source.at[span], target.at[span], mark).start()

        outward.extend(pltpu.make_async_copy(x.at[span], target.at[span], mark) for x, _, target, span, mark in moves)

    for c in range(chunks):
        copies[c].wait()

        def turn(i, carry):
            for k in range(2):
                at = pl.multiple_of(c * part + (2 * i + k) * SUB, SUB)
                for h in range(nx // LANES):
                    planes = jnp.swapaxes(raw[pl.ds(at, SUB), :, half(h)], 0, 1)
                    for j in range(HALO):
                        lo_ref, hi_ref = ((near_lo, near_hi), (next_lo, next_hi), (far_lo, far_hi))[min(j, 2)]
                        sl = pl.ds(pl.multiple_of(at + max(j - 2, 0) * fd, SUB), SUB)
                        lo_ref[sl, half(h)] = planes[j]
                        hi_ref[sl, half(h)] = planes[rows - 1 - j]
            return carry

        lax.fori_loop(0, part // (2 * SUB), turn, 0)
        if c:
            send_out(c)

    @pl.when(lax.axis_index("grp") == 1)
    def _():
        stack = 3 * own
        for k in range(2):
            for ref, at in ((near_lo, k), (near_hi, cols - 2 + k)):
                for m in range(stack):
                    ref[k * stack + m : k * stack + m + 1, 0:ny] = ocean[m, at : at + 1, :]
                ref[2 * stack + k : 2 * stack + k + 1, 0:ny] = sea[at : at + 1, :]

    send_out(0)
    for at, source in ((t_n // 2 - 1, far_hi), (t_n // 2, far_lo)):

        @pl.when(tile == at)
        def _():
            copy = pltpu.make_async_copy(source, turn_hbm, sem.at[chunks + 5])
            copy.start()
            copy.wait()

    for copy in outward:
        copy.wait()


def pick_kernel(n, full, got_ref, mask_ref, cross_ref, *refs):
    t_n, s_n, rows, cols, nx, fd = n[:6]
    ext = rows + 2 * HALO
    lane = lanes_of((ext, LANES))
    per = LANES // cols
    fields = [[jnp.zeros((ext, LANES), jnp.float32) for _ in range(nx // LANES)] for _ in range(3)]
    for t in range(t_n):
        tile = got_ref[(t_n + t) * s_n]
        for q in range(1, s_n):
            tile = tile + got_ref[(t_n + t) * s_n + q]
        if tile.shape[1] < LANES:
            tile = jnp.pad(tile, ((0, 0), (0, LANES - tile.shape[1])))
        h, at = t // per, (t % per) * cols
        inside = (lane >= at) & (lane < at + cols)
        for c in range(3):
            moved = pltpu.roll(tile, (at - c * cols) % LANES, 1) if (at - c * cols) % LANES else tile
            fields[c][h] = jnp.where(inside, moved, fields[c][h])
    whole = [jnp.concatenate(f, axis=1) for f in fields]
    wet, shift = mask_ref[...].astype(jnp.float32), cross_ref[...].astype(jnp.float32)
    if full:
        wind_ref, a_ref, b_ref, rim_ref, geo_ref, out_ref, edge_ref, hb_ref, ha_ref = refs
        even = lax.axis_index("tile") % 2 == 0
        count = hb_ref.shape[0]
        hb_ref[...] = jnp.where(even, b_ref[0:count], a_ref[0:count])
        ha_ref[...] = jnp.where(even, a_ref[0:count], b_ref[0:count])
        own, ny = n[6], rim_ref.shape[3]
        low = lax.axis_index("spec") == 0
        for c in range(3):
            for k in range(2):
                edge_ref[c * 2 + k] = jnp.zeros((cols + 8, ny), jnp.float32)
                edge_ref[c * 2 + k, 4 : 4 + cols] = rim_ref[c, k]
                for m in range(2):
                    for ref, at in ((hb_ref, 2 + m), (ha_ref, 4 + cols + m)):
                        top, bottom = [m * 3 * own + c * own + j for j in (own - 2 + k, k)]
                        value = jnp.where(low, ref[top : top + 1, 0:ny], ref[bottom : bottom + 1, 0:ny])
                        edge_ref[c * 2 + k, at : at + 1] = value

        def joined(k, own):
            span = slice(fd + k * HALO, fd + (k + 1) * HALO)
            first, second = a_ref[span], b_ref[span]
            return jnp.concatenate([jnp.where(even, second, first), own, jnp.where(even, first, second)], axis=0)

        wet, shift = joined(0, wet), joined(3, shift)
        for c in range(2):
            out_ref[c * ext : (c + 1) * ext] = joined(1 + c, wind_ref[c])
    else:
        (geo_ref,) = refs
        edge = jnp.zeros((HALO, nx), jnp.float32)
        wet, shift = [jnp.concatenate([edge, x, edge], axis=0) for x in (wet, shift)]
    shift = jnp.broadcast_to(shift[:, 0:1].astype(jnp.int32), (ext, nx))
    u, v, sea = barrel(whole, shift, nx, True)
    depth = 10.0 + 4.0 * sea
    for k, value in enumerate((0.1 * u, 0.1 * v, 25.0 / (depth * depth), wet)):
        geo_ref[k * ext : (k + 1) * ext] = value


def advance(segments, fd, nx, s, table_ref, planes, store, splat, acc, sums, before=None):
    halves = nx // LANES
    lane = lanes_of((SUB, LANES))
    first, last = lane == 0, lane == LANES - 1
    acc[...] = jnp.zeros(acc.shape, jnp.float32)

    def body(i, carry):
        if before is not None:
            before(i)
        totals = {}

        def add(key, value):
            totals[key] = totals[key] + value if key in totals else value

        for k in range(UNROLL):
            at = pl.multiple_of((i * UNROLL + k) * SUB, SUB)
            sl = pl.ds(at, SUB)
            ge, gn = wide(table_ref[s, sl, GE : GE + 1]), wide(table_ref[s, sl, GN : GN + 1])
            bands = [wide(table_ref[s, sl, b : b + 1]) for b in (SX, SY, DX, DY)] if sums else None
            energy, growth = planes(at)
            for segment in segments:
                def state(r):
                    e = [energy(r, h) * splat[2, r + HALO, :, half(h)] for h in range(halves)]
                    north = [(gn + splat[1, r + HALO, :, half(h)]) * e[h] for h in range(halves)]
                    return e, north

                here, below = state(segment[0]), state(segment[0] - 1)
                flow = [jnp.maximum(below[1][h], 0.0) + jnp.minimum(here[1][h], 0.0) for h in range(halves)]
                for r in segment:
                    above = state(r + 1)
                    e, north = here
                    upper = [jnp.maximum(north[h], 0.0) + jnp.minimum(above[1][h], 0.0) for h in range(halves)]
                    east = [(ge + splat[0, r + HALO, :, half(h)]) * e[h] for h in range(halves)]
                    left = [pltpu.roll(x, LANES - 1, 1) for x in east]
                    flux = [
                        jnp.maximum(east[h], 0.0)
                        + jnp.minimum(jnp.where(last, left[h + 1] if h + 1 < halves else 0.0, left[h]), 0.0)
                        for h in range(halves)
                    ]
                    right = [pltpu.roll(x, 1, 1) for x in flux]
                    for h in range(halves):
                        behind = jnp.where(first, right[h - 1] if h else jnp.minimum(east[0], 0.0), right[h])
                        advected = (e[h] - (flux[h] - behind)) - (upper[h] - flow[h])
                        g = growth(r, h)
                        add((0, r, h), advected)
                        if sums:
                            grown = g * advected
                            pushed = grown - advected
                            for b in range(2):
                                add((1 + b, r, h), bands[b] * pushed)
                                add((3 + b, r, h), bands[2 + b] * grown)
                        else:
                            grown = g * advected
                        store(r, at, h, grown)
                    here, flow = above, upper
        for (kind, r, h), value in totals.items():
            acc[kind, r + HALO, :, half(h)] += value
        return carry

    lax.fori_loop(0, fd // (SUB * UNROLL), body, 0)


def folded(acc, kind, rows):
    return [jnp.sum(acc[kind, r + HALO], axis=0, keepdims=True) for r in rows]


def fill(splat, kind, row, value, nx):
    splat[kind, row + HALO] = jnp.broadcast_to(value, (SUB, nx))


def geometry(geo_ref, ext, kind, r):
    at = kind * ext + r + HALO
    return geo_ref[at : at + 1]


def write_totals(total_ref, acc, rows, previous, ext, nx):
    total_ref[...] = jnp.zeros((ext, nx), jnp.float32) if previous is None else previous[...]
    for r, value in zip(rows, folded(acc, 0, rows)):
        total_ref[r + HALO : r + HALO + 1] = value


def first_middle_kernel(n, table_ref, geo_ref, wind_ref, spectrum_ref,
                        out_ref, total_ref, growth_ref, raw, windb, splat, acc, sem):
    rows, fd, nx, chunks = n
    ext = rows + 2 * HALO
    s = lax.axis_index("spec")
    part = fd // chunks
    turns = part // (SUB * UNROLL)

    def copy(c):
        span = pl.ds(pl.multiple_of(c * part, SUB), part)
        return pltpu.make_async_copy(spectrum_ref.at[span], raw.at[span], sem.at[c])

    for c in range(chunks):
        copy(c).start()
    for c in range(2):
        for r in range(rows):
            windb[c, r] = jnp.broadcast_to(wind_ref[c, r : r + 1], (SUB, nx))
    for r in range(rows):
        for kind, source in ((0, 0), (1, 1), (2, 3)):
            fill(splat, kind, r, geometry(geo_ref, ext, source, r), nx)

    def before(i):
        @pl.when(i % turns == 0)
        def _():
            copy(i // turns).wait()

    def planes(at):
        sl = pl.ds(at, SUB)
        bw, we, wn = [wide(table_ref[s, sl, b : b + 1]) for b in (BW, WE, WN)]
        natural, grown = {}, {}
        for h in range(nx // LANES):
            natural[h] = jnp.swapaxes(raw[sl, :, half(h)], 0, 1)
            for r in range(rows):
                drive = we * windb[0, r, :, half(h)] + wn * windb[1, r, :, half(h)]
                grown[r, h] = 1.0 + jnp.maximum(drive - 0.05, 0.0)
                growth_ref[pl.ds(pl.multiple_of(r * fd + at, SUB), SUB), half(h)] = grown[r, h]
        return lambda r, h: bw * natural[h][r], lambda r, h: grown[r, h]

    def store(r, at, h, value):
        out_ref[pl.ds(pl.multiple_of((r - 1) * fd + at, SUB), SUB), half(h)] = value

    inner = list(range(1, rows - 1))
    advance([inner], fd, nx, s, table_ref, planes, store, splat, acc, False, before)
    write_totals(total_ref, acc, inner, None, ext, nx)


def step_kernel(n, cfg, *refs):
    rows, fd, nx, t_n, s_n, cols = n
    segments, source, growth, grow, raw, sums, joined, count = cfg
    ext = rows + 2 * HALO
    refs = list(refs)
    table_ref, geo_ref = refs.pop(0), refs.pop(0)
    wind_ref = refs.pop(0) if grow else None
    own_ref, got_ref = (None, None) if raw else (refs.pop(0), refs.pop(0))
    previous = refs.pop(0) if joined else None
    cross_ref = refs.pop(0) if sums else None
    operands, refs = refs[:count], refs[count:]
    out_ref, total_ref = refs.pop(0), refs.pop(0)
    growth_ref = refs.pop(0) if grow else None
    splat, acc = refs.pop(0), refs.pop(0)
    windb = refs.pop(0) if grow else None
    s = lax.axis_index("spec")
    order = [r for segment in segments for r in segment]
    needed = sorted({r + d for r in order for d in (-1, 0, 1)})
    breaking = geo_ref[3 * ext : 4 * ext]
    if not raw:
        breaking = breaking / (1.0 + (own_ref[...] + got_ref[...]) * geo_ref[2 * ext : 3 * ext])
    for r in needed:
        fill(splat, 0, r, geometry(geo_ref, ext, 0, r), nx)
        fill(splat, 1, r, geometry(geo_ref, ext, 1, r), nx)
        fill(splat, 2, r, breaking[r + HALO : r + HALO + 1], nx)
    for c in range(2):
        for k, r in enumerate(grow):
            at = c * ext + r + HALO
            windb[c, k] = jnp.broadcast_to(wind_ref[at : at + 1], (SUB, nx))

    tile = lax.axis_index("tile")
    even = tile % 2 == 0

    def load(place, at, h):
        found, first = place[:2]
        parts = [operands[k][pl.ds(pl.multiple_of(first + at, SUB), SUB), half(h)] for k in found]
        value = parts[0] if len(parts) == 1 else jnp.where(even, parts[0], parts[1])
        if len(parts) == 3:
            value = jnp.where(tile == (t_n // 2 if place[2] < 0 else t_n // 2 - 1), parts[2], value)
        return value

    def planes(at):
        sl = pl.ds(at, SUB)
        bw = wide(table_ref[s, sl, BW : BW + 1]) if raw else None
        we, wn = [wide(table_ref[s, sl, b : b + 1]) for b in (WE, WN)] if grow else (None, None)

        def energy(r, h):
            value = load(source[r] + (r,), at, h)
            return bw * value if raw else value

        def factor(r, h):
            if r in grow:
                k = grow.index(r)
                drive = we * windb[0, k, :, half(h)] + wn * windb[1, k, :, half(h)]
                value = 1.0 + jnp.maximum(drive - 0.05, 0.0)
                growth_ref[pl.ds(pl.multiple_of(k * fd + at, SUB), SUB), half(h)] = value
                return value
            return load(growth[r], at, h)

        return energy, factor

    def store(r, at, h, value):
        out_ref[pl.ds(pl.multiple_of(order.index(r) * fd + at, SUB), SUB), half(h)] = value

    advance(segments, fd, nx, s, table_ref, planes, store, splat, acc, sums)
    if not sums:
        write_totals(total_ref, acc, order, previous, ext, nx)
        return
    kinds = [jnp.concatenate(folded(acc, kind, order), axis=0) for kind in range(acc.shape[0])]
    wet = jnp.where(s == 0, geo_ref[3 * ext + HALO : 3 * ext + HALO + rows], 0.0)
    shift = jnp.broadcast_to(cross_ref[:, 0:1], (rows, nx))
    moved = barrel(kinds + [wet], shift, nx, False)
    lane = lanes_of((rows, nx))
    size = cols + 8
    for t in range(t_n):
        chunk = jnp.zeros((rows, nx), jnp.float32)
        for q, value in enumerate(moved):
            amount = (q * size - (cols * t - 4)) % nx
            piece = pltpu.roll(value, amount, 1) if amount else value
            chunk = jnp.where((lane >= q * size) & (lane < (q + 1) * size), piece, chunk)
        for q in range(s_n):
            total_ref[(t_n + t) * s_n + q] = chunk
    mine = lax.axis_index("tile")
    for q in range(s_n):
        total_ref[mine * s_n + q] = kinds[0]


def last_kernel(n, table_ref, level_ref, got_ref, geo_ref, wave_ref, ocean_ref, sea_ref,
                hb_ref, ha_ref, lev_ref, waves_ref, next_ref,
                raw, brk, turn, field, mix, out, sem, osem):
    rows, fd, nx, t_n, s_n, cols, own, ny, chunks = n
    s = lax.axis_index("spec")
    g = lax.axis_index("grp")
    tile = lax.axis_index("tile")
    part = fd // chunks
    pad = turn.shape[0]
    size = cols + 8

    def write(c, source):
        return pltpu.make_async_copy(raw.at[pl.ds(source * part, part)], waves_ref.at[pl.ds(c * part, part)], sem.at[c])

    ocean_copy = pltpu.make_async_copy(out, next_ref, osem)

    @pl.when(g == 0)
    def _():
        total = got_ref[tile * s_n]
        for q in range(1, s_n):
            total = total + got_ref[tile * s_n + q]
        ext = rows + 2 * HALO
        wet = geo_ref[3 * ext + HALO : 3 * ext + HALO + rows]
        breaking = wet / (1.0 + total * geo_ref[2 * ext + HALO : 2 * ext + HALO + rows])
        for r in range(rows):
            brk[r] = jnp.broadcast_to(breaking[r : r + 1], (SUB, nx))
        for c in range(chunks):

            def finish(i, carry):
                for k in range(2):
                    at = pl.multiple_of(c * part + (2 * i + k) * SUB, SUB)
                    sl = pl.ds(at, SUB)
                    inv = wide(table_ref[s, sl, INV : INV + 1])
                    for h in range(nx // LANES):
                        spans = [pl.ds(pl.multiple_of(r * fd + at, SUB), SUB) for r in range(rows)]
                        values = [wave_ref[span, half(h)] for span in spans]
                        values = [value * brk[r, :, half(h)] * inv for r, value in enumerate(values)]
                        raw[sl, :, half(h)] = jnp.swapaxes(jnp.stack(values), 0, 1)
                return carry

            lax.fori_loop(0, part // (2 * SUB), finish, 0)
            write(c, c).start()
        out[...] = jnp.zeros((3, own, cols, ny), jnp.float32)
        ocean_copy.start()
        ocean_copy.wait()
        for c in range(chunks):
            write(c, c).wait()

    @pl.when(g == 1)
    def _():
        def clear(i, carry):
            raw[pl.ds(pl.multiple_of(i * SUB, SUB), SUB)] = jnp.zeros((SUB, rows, nx), jnp.float32)
            return carry

        lax.fori_loop(0, part // SUB, clear, 0)
        for c in range(chunks):
            write(c, 0).start()

        if pad > ny:
            turn[ny:pad] = jnp.zeros((pad - ny, nx), jnp.float32)
        for t in range(t_n):
            tilev = got_ref[t * s_n]
            for q in range(1, s_n):
                tilev = tilev + got_ref[t * s_n + q]
            turn[t * rows : (t + 1) * rows] = tilev
        turned = jnp.transpose(turn[...])
        total, sx, sy, dx, dy, wet = [turned[q * size : (q + 1) * size] for q in range(6)]
        row = lax.broadcasted_iota(jnp.int32, (size, pad), 0)
        column = row + (tile * cols - 4)
        wet = jnp.where((column >= 0) & (column < t_n * cols), wet, 0.0)
        stack = 3 * own
        mix[0] = jnp.zeros((size, pad), jnp.float32)
        mix[0, 4 : 4 + cols, 0:ny] = sea_ref[...]
        mix[0, 2:4, 0:ny] = hb_ref[2 * stack : 2 * stack + 2, 0:ny]
        mix[0, 4 + cols : 6 + cols, 0:ny] = ha_ref[2 * stack : 2 * stack + 2, 0:ny]
        depth = 10.0 + 4.0 * mix[0]
        breaking = 1.0 / (1.0 + 25.0 * total / (depth * depth))
        swept = wet * breaking
        sx, sy, dx, dy = sx * breaking, sy * breaking, dx * swept, dy * swept

        field[...] = jnp.zeros(field.shape, jnp.float32)
        ext = own + 4
        for c in range(3):
            for k in range(own):
                l = c * ext + 2 + k
                field[l, 4 : 4 + cols, 0:ny] = ocean_ref[c, k]
                for m in range(2):
                    at = m * stack + c * own + k
                    field[l, 2 + m : 3 + m, 0:ny] = hb_ref[at : at + 1, 0:ny]
                    field[l, 4 + cols + m : 5 + cols + m, 0:ny] = ha_ref[at : at + 1, 0:ny]
        for upper in range(2):
            @pl.when(s == 1 - upper)
            def _():
                for c in range(3):
                    for k in range(2):
                        l = c * ext + (own + 2 if upper else 0) + k
                        field[l, :, 0:ny] = lev_ref[c * 2 + k]

        lane = lanes_of((size, pad))

        def new_fields(source, k):
            values = []
            for c in range(3):
                q = source[c * ext + k]
                lateral = (
                    pltpu.roll(q, size - 1, 0)
                    + pltpu.roll(q, 1, 0)
                    + jnp.where(lane == ny - 1, 0.0, pltpu.roll(q, pad - 1, 1))
                    + jnp.where(lane == 0, 0.0, pltpu.roll(q, 1, 1))
                    - 4.0 * q
                )
                vertical = source[c * ext + k + 1] + source[c * ext + k - 1] - 2.0 * q
                values.append((q, q + 0.1 * lateral + 0.2 * vertical))
            (u, du), (v, dv), (_, dt) = values
            shaped = level_ref[s, 1, k]
            top = jnp.where((s == 0) & (k == 2), 1.0, 0.0)
            east = du + 0.1 * (v + shaped * dy) + top * sx
            north = dv - 0.1 * (u + shaped * dx) + top * sy
            keep = wet * level_ref[s, 2, k]
            return keep * east, keep * north, keep * dt

        for k in range(1, ext - 1):
            for c, value in enumerate(new_fields(field, k)):
                mix[c * ext + k] = value
        for k in range(2, ext - 2):
            for c, value in enumerate(new_fields(mix, k)):
                out[c, k - 2] = value[4 : 4 + cols, 0:ny]
        ocean_copy.start()
        ocean_copy.wait()
        for c in range(chunks):
            write(c, 0).wait()


def program(spectrum, wind, land_mask, intersection, ocean_state, sea_level, *, mesh_shape):
    g_n, t_n, s_n = (mesh_shape[a] for a in AXES)
    _, freqs, dirs, rows, nx = spectrum.shape
    _, _, own, cols, ny = ocean_state.shape
    fd = freqs * dirs
    devices = g_n * t_n * s_n
    table = jnp.asarray(wave_table(freqs, dirs * s_n, s_n))
    levels = jnp.asarray(level_table(own * s_n, s_n, own))
    ocean = ocean_state[0]
    sea = sea_level[0]

    def in_hbm(x):
        return pltpu.with_memory_space_constraint(x, pltpu.HBM)

    natural = in_hbm(spectrum.reshape(fd, rows, nx))
    chunks = 6
    vm = pltpu.VMEM
    params = pltpu.CompilerParams(vmem_limit_bytes=24 << 20)

    def swapped(x, start, without=None):
        lower = [i for i in range(start, t_n - 1, 2) if i + 1 != without]
        return lax.ppermute(x, "tile", [(i, i + 1) for i in lower] + [(i + 1, i) for i in lower])

    def others(x):
        return added(lax.ppermute(x, "spec", [(i, (i + k) % s_n) for i in range(s_n)]) for k in range(1, s_n))

    def added(values):
        return functools.reduce(lambda a, b: a + b, values)

    def call(kernel, args, specs, shapes, out_specs, scratch):
        return pl.pallas_call(
            kernel, out_shape=shapes, in_specs=specs, out_specs=out_specs,
            scratch_shapes=scratch, compiler_params=params,
        )(*args)

    ext = rows + 2 * HALO
    near, second, far = f32(fd + 4 * HALO, nx), f32(fd, nx), f32((HALO - 2) * fd, nx)

    def hbm(shape):
        return pltpu.HBM(shape.shape, shape.dtype)

    send, level_rim, near_a, near_b, next_a, next_b, far_a, far_b, turn = call(
        functools.partial(start_kernel, (t_n, s_n, rows, cols, own, ny, fd, nx, chunks)),
        (levels, natural, in_hbm(ocean.reshape(3 * own, cols, ny)), in_hbm(sea), in_hbm(land_mask), in_hbm(wind), in_hbm(intersection)),
        [SM] + [HB] * 6,
        (f32(devices, ext, 4 * cols), f32(3, 2, cols, ny), hbm(near), hbm(near), hbm(second), hbm(second), hbm(far), hbm(far), hbm(far)),
        (VM,) * 2 + (HB,) * 7,
        [vm((fd, rows, nx), jnp.float32), vm((3 * own, cols, ny), jnp.float32), vm((cols, ny), jnp.float32),
         vm((rows, nx), jnp.int32), vm((2, rows, nx), jnp.float32), vm((rows, nx), jnp.int32),
         vm(near.shape, jnp.float32), vm(near.shape, jnp.float32),
         vm(second.shape, jnp.float32), vm(second.shape, jnp.float32), vm(far.shape, jnp.float32), vm(far.shape, jnp.float32),
         pltpu.SemaphoreType.DMA((chunks + 6,)), pltpu.SemaphoreType.DMA((chunks, 6, HALO + 1))],
    )
    got_a, got_b = swapped(near_a, 0), swapped(near_b, 1)
    arrived = lax.all_to_all(send, AXES, 0, 0, tiled=True)
    next_got = swapped(next_a, 0), swapped(next_b, 1)
    middle = t_n // 2
    turned = lax.ppermute(turn, "tile", [(middle - 1, t_n - 1), (middle, 0)])
    far_got = swapped(far_a, 0, middle), swapped(far_b, 1, middle)
    turned = lax.ppermute(turned, "tile", [(t_n - 1, middle), (0, middle - 1)])

    geo = call(
        functools.partial(pick_kernel, (t_n, s_n, rows, cols, nx, fd), False),
        (arrived, land_mask, intersection), [VM] * 3, f32(4 * ext, nx), VM, [],
    )

    def scratch(kinds, grow):
        result = [vm((3, ext, SUB, nx), jnp.float32), vm((kinds, ext, SUB, nx), jnp.float32)]
        return result + [vm((2, grow, SUB, nx), jnp.float32)] if grow else result

    mid, total, growth0 = call(
        functools.partial(first_middle_kernel, (rows, fd, nx, chunks)),
        (table, geo, wind, natural), [VM] * 3 + [HB],
        (f32((rows - 2) * fd, nx), f32(ext, nx), f32(rows * fd, nx)), (VM,) * 3,
        [vm((fd, rows, nx), jnp.float32), vm((2, rows, SUB, nx), jnp.float32)] + scratch(1, 0)
        + [pltpu.SemaphoreType.DMA((chunks,))],
    )
    riding = f32(-(-(6 * own + 2) // SUB) * SUB, nx)
    geo, winds, level_rim, hb, ha = call(
        functools.partial(pick_kernel, (t_n, s_n, rows, cols, nx, fd, own), True),
        (arrived, land_mask, intersection, wind, got_a, got_b, level_rim), [VM] * 7,
        (f32(4 * ext, nx), f32(2 * ext, nx), f32(6, cols + 8, ny), riding, riding), (VM,) * 5, [],
    )

    planes = {k: {} for k in range(WSTEPS + 1)}
    for j in range(HALO):
        k, at = min(j, 2), max(j - 2, 0) * fd
        a, b = ((got_a, got_b), next_got, far_got)[k]
        corner = (turned,) if k == 2 else ()
        planes[0][-1 - j] = ((b, a) + corner, at)
        planes[0][rows + j] = ((a, b) + corner, at)
        if j < 2:
            a, b = ((near_a, near_b), (next_a, next_b))[j]
            planes[0][j] = ((b, a), 0)
            planes[0][rows - 1 - j] = ((a, b), 0)
    for k, r in enumerate(range(1, rows - 1)):
        planes[1][r] = ((mid,), k * fd)
    grown = {r: ((growth0,), r * fd) for r in range(rows)}
    totals, gots = {1: total}, {}

    def advanced(step, segments, exchange=True):
        raw, sums = step == 1, step == WSTEPS
        order = [r for segment in segments for r in segment]
        grow = [r for r in order if r not in grown]
        operands = []

        def place(item):
            found = []
            for array in item[0]:
                known = [k for k, other in enumerate(operands) if other is array]
                if not known:
                    operands.append(array)
                found.append(known[0] if known else len(operands) - 1)
            return tuple(found), item[1]

        source = {r: place(planes[step - 1][r]) for r in sorted({r + d for r in order for d in (-1, 0, 1)})}
        growth = {r: place(grown[r]) for r in order if r in grown}
        args = [table, geo]
        if grow:
            args.append(winds)
        if not raw:
            args += [totals[step - 1], gots[step - 1]]
        joined = step in totals
        if joined:
            args.append(totals[step])
        if sums:
            args.append(intersection)
        args += operands
        shapes = [f32(len(order) * fd, nx), f32(devices, rows, nx) if sums else f32(ext, nx)]
        if grow:
            shapes.append(f32(len(grow) * fd, nx))
        cfg = (segments, source, growth, grow, raw, sums, joined, len(operands))
        outs = call(
            functools.partial(step_kernel, (rows, fd, nx, t_n, s_n, cols), cfg),
            args, [VM] * len(args), tuple(shapes), (VM,) * len(shapes), scratch(5 if sums else 1, len(grow)),
        )
        for k, r in enumerate(order):
            planes[step][r] = ((outs[0],), k * fd)
        for k, r in enumerate(grow):
            grown[r] = ((outs[2],), k * fd)
        totals[step] = outs[1]
        if exchange and not sums:
            gots[step] = others(outs[1])

    def pair(first, last):
        return [list(range(first, last + 1)), list(range(rows - 1 - last, rows - first))]

    advanced(1, pair(-1, 0))
    advanced(2, [list(range(rows))])
    advanced(1, pair(-3, -2))
    advanced(3, [list(range(1, rows - 1))], exchange=False)
    level_got = others(level_rim)
    advanced(2, pair(-2, -1))
    advanced(3, pair(-1, 0))
    totals[3], level_got = lax.optimization_barrier((totals[3], level_got))
    advanced(4, [list(range(rows))])

    landed = lax.all_to_all(totals[WSTEPS], AXES, 0, 0, tiled=True)
    pad = -(-ny // LANES) * LANES
    size = cols + 8
    ins = (table, levels, landed, geo, planes[WSTEPS][0][0][0], ocean, sea, hb, ha, level_got)
    waves, fields = call(
        functools.partial(last_kernel, (rows, fd, nx, t_n, s_n, cols, own, ny, chunks)),
        ins, [VM, SM] + [VM] * (len(ins) - 2), (f32(fd, rows, nx), f32(3, own, cols, ny)), (HB, HB),
        [
            vm((fd, rows, nx), jnp.float32),
            vm((rows, SUB, nx), jnp.float32),
            vm((pad, nx), jnp.float32),
            vm((3 * (own + 4), size, pad), jnp.float32),
            vm((3 * (own + 4), size, pad), jnp.float32),
            vm((3, own, cols, ny), jnp.float32),
            pltpu.SemaphoreType.DMA((chunks,)),
            pltpu.SemaphoreType.DMA,
        ],
    )
    return waves.reshape(spectrum.shape), fields.reshape(ocean_state.shape)


def solution(mesh):
    return jax.shard_map(
        functools.partial(program, mesh_shape=dict(mesh.shape)),
        mesh=mesh,
        in_specs=(
            P("grp", None, "spec", "tile", None),
            P(None, "tile", None),
            P("tile", None),
            P("tile", None),
            P("grp", None, "spec", "tile", None),
            P("grp", "tile", None),
        ),
        out_specs=(P("grp", None, "spec", "tile", None), P("grp", None, "spec", "tile", None)),
        check_vma=False,
    )
```

```python
import functools
import math

import jax
import jax.numpy as jnp
import numpy as np
from jax import lax
from jax.experimental import pallas as pl
from jax.experimental.pallas import tpu as pltpu
from jax.sharding import PartitionSpec as P


WSTEPS = 4
HALO = WSTEPS
LANES = 128
SUB = 8
UNROLL = 6
UNROLL_SUMS = 4
AXES = ("grp", "tile", "spec")

BW, GE, GN, WE, WN, SX, SY, DX, DY, INV = range(10)

VM = pl.BlockSpec(memory_space=pltpu.VMEM)
SM = pl.BlockSpec(memory_space=pltpu.SMEM)
HB = pl.BlockSpec(memory_space=pltpu.HBM)


def f32(*shape):
    return jax.ShapeDtypeStruct(shape, jnp.float32)


def wave_table(freqs, dirs, parts):
    frequency = 0.04 * 1.1 ** np.arange(freqs)
    celerity = 1.56 / frequency
    group = 0.4 * 1.1 ** (-np.arange(freqs, dtype=np.float64))
    width = 0.1 * frequency * (2.0 * math.pi / dirs)
    angle = 2.0 * math.pi * (np.arange(dirs) + 0.5) / dirs
    cos, sin, one = np.cos(angle), np.sin(angle), np.ones(dirs)
    columns = [
        np.outer(width, one),
        np.outer(group, cos),
        np.outer(group, sin),
        np.outer(0.05 / celerity, cos),
        np.outer(0.05 / celerity, sin),
        np.outer(5.0 / celerity, cos),
        np.outer(5.0 / celerity, sin),
        np.outer(20.0 * frequency**3, cos),
        np.outer(20.0 * frequency**3, sin),
        np.outer(1.0 / width, one),
    ]
    table = np.zeros((parts, freqs * dirs // parts, 16), np.float32)
    for k, column in enumerate(columns):
        split = column.reshape(freqs, parts, dirs // parts).transpose(1, 0, 2)
        table[:, :, k] = split.reshape(parts, -1)
    return table


def level_table(levels, parts, own):
    depth = (np.arange(levels) + 0.5) / levels
    profile = np.exp(-2.0 * depth)
    weights = profile / profile.sum()
    table = np.zeros((parts, 3, own + 4), np.float32)
    for s in range(parts):
        table[s, 0, :own] = weights[s * own : (s + 1) * own]
        for l in range(own + 4):
            g = s * own + l - 2
            if 0 <= g < levels:
                table[s, 1, l] = profile[g]
                table[s, 2, l] = 1.0
    return table


def lanes_of(shape):
    return lax.broadcasted_iota(jnp.int32, shape, len(shape) - 1)


def wide(column):
    return jnp.broadcast_to(column, (SUB, LANES))


def half(h):
    return slice(h * LANES, (h + 1) * LANES)


def barrel(values, shift, size, left):
    bit = 1
    while bit < size:
        taken = (shift & bit) != 0
        amount = size - bit if left else bit
        values = [jnp.where(taken, pltpu.roll(v, amount, 1), v) for v in values]
        bit *= 2
    return values


def start_kernel(n, level_ref, spectrum_ref, ocean_hbm, sea_hbm, mask_hbm, wind_hbm, cross_hbm,
                 out_ref, rim_ref, near_a, near_b, next_a, next_b, far_a, far_b, turn_hbm,
                 raw, ocean, sea, mask_ref, wind_ref, cross_ref, near_lo, near_hi, next_lo, next_hi, far_lo, far_hi, sem, out_sem):
    t_n, s_n, rows, cols, own, ny, fd, nx, chunks = n
    s = lax.axis_index("spec")
    pad = -(-ny // LANES) * LANES
    part = fd // chunks
    small = ((ocean_hbm, ocean), (sea_hbm, sea), (mask_hbm, mask_ref), (wind_hbm, wind_ref), (cross_hbm, cross_ref))
    first = [pltpu.make_async_copy(a, b, sem.at[chunks + k]) for k, (a, b) in enumerate(small)]
    copies = [
        pltpu.make_async_copy(spectrum_ref.at[pl.ds(c * part, part)], raw.at[pl.ds(c * part, part)], sem.at[c])
        for c in range(chunks)
    ]
    for copy in first + copies:
        copy.start()
    for copy in first:
        copy.wait()
    parts = []
    for c in range(2):
        total = None
        for k in range(own):
            term = level_ref[s, 0, k] * ocean[c * own + k]
            total = term if total is None else total + term
        parts.append(total)
    parts.append(jnp.where(s == 0, sea[...], 0.0))
    for c in range(3):
        for k in range(2):
            rim_ref[c, k] = jnp.where(s == 0, ocean[c * own + own - 2 + k], ocean[c * own + k])
    stack = jnp.concatenate(parts, axis=0)
    stack = jnp.pad(stack, ((0, LANES - 3 * cols), (0, pad - ny)))
    edge = jnp.zeros((HALO, LANES), jnp.float32)
    turned = jnp.concatenate([edge, jnp.transpose(stack)[:ny], edge], axis=0)
    for t in range(t_n):
        for q in range(s_n):
            out_ref[t * s_n + q] = turned[t * rows : (t + 1) * rows + 2 * HALO, : 4 * cols]
    aux = [mask_ref[...].astype(jnp.float32), wind_ref[0], wind_ref[1], cross_ref[...].astype(jnp.float32)]
    for k, value in enumerate(aux):
        at = fd + k * HALO
        near_hi[at : at + HALO] = value[rows - HALO : rows]
        near_lo[at : at + HALO] = value[0:HALO]

    held = ((near_lo, near_hi, near_a, near_b), (next_lo, next_hi, next_a, next_b), (far_lo, far_hi, far_a, far_b))
    tile = lax.axis_index("tile")
    even = tile % 2 == 0
    outward = []

    def send_out(c):
        moves = []
        for k, (low, high, a, b) in enumerate(held):
            spans = [pl.ds(j * fd + c * part, part) for j in range(low.shape[0] // fd)]
            if c == 0 and k == 0:
                spans.append(pl.ds(fd, 4 * HALO))
            for j, span in enumerate(spans):
                moves.append((low, high, a, span, out_sem.at[c, 2 * k, j]))
                moves.append((high, low, b, span, out_sem.at[c, 2 * k + 1, j]))
        for side in range(2):

            @pl.when(even if side else jnp.logical_not(even))
            def _():
                for move in moves:
                    source, target, span, mark = move[side], *move[2:]
                    pltpu.make_async_copy(source.at[span], target.at[span], mark).start()

        outward.extend(pltpu.make_async_copy(x.at[span], target.at[span], mark) for x, _, target, span, mark in moves)

    for c in range(chunks):
        copies[c].wait()

        def turn(i, carry):
            for k in range(2):
                at = pl.multiple_of(c * part + (2 * i + k) * SUB, SUB)
                for h in range(nx // LANES):
                    planes = jnp.swapaxes(raw[pl.ds(at, SUB), :, half(h)], 0, 1)
                    for j in range(HALO):
                        lo_ref, hi_ref = ((near_lo, near_hi), (next_lo, next_hi), (far_lo, far_hi))[min(j, 2)]
                        sl = pl.ds(pl.multiple_of(at + max(j - 2, 0) * fd, SUB), SUB)
                        lo_ref[sl, half(h)] = planes[j]
                        hi_ref[sl, half(h)] = planes[rows - 1 - j]
            return carry

        lax.fori_loop(0, part // (2 * SUB), turn, 0)
        if c:
            send_out(c)

    @pl.when(lax.axis_index("grp") == 1)
    def _():
        stack = 3 * own
        for k in range(2):
            for ref, at in ((near_lo, k), (near_hi, cols - 2 + k)):
                for m in range(stack):
                    ref[k * stack + m : k * stack + m + 1, 0:ny] = ocean[m, at : at + 1, :]
                ref[2 * stack + k : 2 * stack + k + 1, 0:ny] = sea[at : at + 1, :]

    turns = [(t_n // 2 - 1, far_hi), (t_n // 2, far_lo)]

    def turning(source):
        return pltpu.make_async_copy(source, turn_hbm, sem.at[chunks + 5])

    for at, source in turns:
        pl.when(tile == at)(turning(source).start)
    send_out(0)
    for copy in outward:
        copy.wait()
    for at, source in turns:
        pl.when(tile == at)(turning(source).wait)


def pick_kernel(n, full, got_ref, mask_ref, cross_ref, *refs):
    t_n, s_n, rows, cols, nx, fd = n[:6]
    ext = rows + 2 * HALO
    lane = lanes_of((ext, LANES))
    per = LANES // cols
    fields = [[jnp.zeros((ext, LANES), jnp.float32) for _ in range(nx // LANES)] for _ in range(3)]
    for t in range(t_n):
        tile = got_ref[(t_n + t) * s_n]
        for q in range(1, s_n):
            tile = tile + got_ref[(t_n + t) * s_n + q]
        if tile.shape[1] < LANES:
            tile = jnp.pad(tile, ((0, 0), (0, LANES - tile.shape[1])))
        h, at = t // per, (t % per) * cols
        inside = (lane >= at) & (lane < at + cols)
        for c in range(3):
            moved = pltpu.roll(tile, (at - c * cols) % LANES, 1) if (at - c * cols) % LANES else tile
            fields[c][h] = jnp.where(inside, moved, fields[c][h])
    whole = [jnp.concatenate(f, axis=1) for f in fields]
    wet, shift = mask_ref[...].astype(jnp.float32), cross_ref[...].astype(jnp.float32)
    if full:
        wind_ref, a_ref, b_ref, rim_ref, geo_ref, out_ref, edge_ref, hb_ref, ha_ref = refs
        even = lax.axis_index("tile") % 2 == 0
        count = hb_ref.shape[0]
        hb_ref[...] = jnp.where(even, b_ref[0:count], a_ref[0:count])
        ha_ref[...] = jnp.where(even, a_ref[0:count], b_ref[0:count])
        own, ny = n[6], rim_ref.shape[3]
        low = lax.axis_index("spec") == 0
        for c in range(3):
            for k in range(2):
                edge_ref[c * 2 + k] = jnp.zeros((cols + 8, ny), jnp.float32)
                edge_ref[c * 2 + k, 4 : 4 + cols] = rim_ref[c, k]
                for m in range(2):
                    for ref, at in ((hb_ref, 2 + m), (ha_ref, 4 + cols + m)):
                        top, bottom = [m * 3 * own + c * own + j for j in (own - 2 + k, k)]
                        value = jnp.where(low, ref[top : top + 1, 0:ny], ref[bottom : bottom + 1, 0:ny])
                        edge_ref[c * 2 + k, at : at + 1] = value

        def joined(k, own):
            span = slice(fd + k * HALO, fd + (k + 1) * HALO)
            first, second = a_ref[span], b_ref[span]
            return jnp.concatenate([jnp.where(even, second, first), own, jnp.where(even, first, second)], axis=0)

        wet, shift = joined(0, wet), joined(3, shift)
        for c in range(2):
            out_ref[c * ext : (c + 1) * ext] = joined(1 + c, wind_ref[c])
    else:
        (geo_ref,) = refs
        edge = jnp.zeros((HALO, nx), jnp.float32)
        wet, shift = [jnp.concatenate([edge, x, edge], axis=0) for x in (wet, shift)]
    shift = jnp.broadcast_to(shift[:, 0:1].astype(jnp.int32), (ext, nx))
    u, v, sea = barrel(whole, shift, nx, True)
    depth = 10.0 + 4.0 * sea
    for k, value in enumerate((0.1 * u, 0.1 * v, 25.0 / (depth * depth), wet)):
        geo_ref[k * ext : (k + 1) * ext] = value


def advance(segments, fd, nx, s, table_ref, planes, store, splat, acc, sums, before=None):
    halves = nx // LANES
    unroll = UNROLL_SUMS if sums else UNROLL
    lane = lanes_of((SUB, LANES))
    first, last = lane == 0, lane == LANES - 1
    acc[...] = jnp.zeros(acc.shape, jnp.float32)

    def body(i, carry):
        if before is not None:
            before(i)
        totals = {}

        def add(key, value):
            totals[key] = totals[key] + value if key in totals else value

        for k in range(unroll):
            at = pl.multiple_of((i * unroll + k) * SUB, SUB)
            sl = pl.ds(at, SUB)
            ge, gn = wide(table_ref[s, sl, GE : GE + 1]), wide(table_ref[s, sl, GN : GN + 1])
            bands = [wide(table_ref[s, sl, b : b + 1]) for b in (SX, SY, DX, DY)] if sums else None
            energy, growth = planes(at)
            for segment in segments:
                def state(r):
                    e = [energy(r, h) * splat[2, r + HALO, :, half(h)] for h in range(halves)]
                    north = [(gn + splat[1, r + HALO, :, half(h)]) * e[h] for h in range(halves)]
                    return e, north

                here, below = state(segment[0]), state(segment[0] - 1)
                flow = [jnp.maximum(below[1][h], 0.0) + jnp.minimum(here[1][h], 0.0) for h in range(halves)]
                for r in segment:
                    above = state(r + 1)
                    e, north = here
                    upper = [jnp.maximum(north[h], 0.0) + jnp.minimum(above[1][h], 0.0) for h in range(halves)]
                    east = [(ge + splat[0, r + HALO, :, half(h)]) * e[h] for h in range(halves)]
                    left = [pltpu.roll(x, LANES - 1, 1) for x in east]
                    flux = [
                        jnp.maximum(east[h], 0.0)
                        + jnp.minimum(jnp.where(last, left[h + 1] if h + 1 < halves else 0.0, left[h]), 0.0)
                        for h in range(halves)
                    ]
                    right = [pltpu.roll(x, 1, 1) for x in flux]
                    for h in range(halves):
                        behind = jnp.where(first, right[h - 1] if h else jnp.minimum(east[0], 0.0), right[h])
                        advected = (e[h] - (flux[h] - behind)) - (upper[h] - flow[h])
                        g = growth(r, h)
                        add((0, r, h), advected)
                        if sums:
                            grown = g * advected
                            pushed = grown - advected
                            for b in range(2):
                                add((1 + b, r, h), bands[b] * pushed)
                                add((3 + b, r, h), bands[2 + b] * grown)
                        else:
                            grown = g * advected
                        store(r, at, h, grown)
                    here, flow = above, upper
        for (kind, r, h), value in totals.items():
            acc[kind, r + HALO, :, half(h)] += value
        return carry

    lax.fori_loop(0, fd // (SUB * unroll), body, 0)


def folded(acc, kind, rows):
    return [jnp.sum(acc[kind, r + HALO], axis=0, keepdims=True) for r in rows]


def fill(splat, kind, row, value, nx):
    splat[kind, row + HALO] = jnp.broadcast_to(value, (SUB, nx))


def geometry(geo_ref, ext, kind, r):
    at = kind * ext + r + HALO
    return geo_ref[at : at + 1]


def write_totals(total_ref, acc, rows, previous, ext, nx):
    total_ref[...] = jnp.zeros((ext, nx), jnp.float32) if previous is None else previous[...]
    for r, value in zip(rows, folded(acc, 0, rows)):
        total_ref[r + HALO : r + HALO + 1] = value


def first_middle_kernel(n, table_ref, geo_ref, wind_ref, spectrum_ref,
                        out_ref, total_ref, growth_ref, raw, windb, splat, acc, sem):
    rows, fd, nx, chunks = n
    ext = rows + 2 * HALO
    s = lax.axis_index("spec")
    part = fd // chunks
    turns = part // (SUB * UNROLL)

    def copy(c):
        span = pl.ds(pl.multiple_of(c * part, SUB), part)
        return pltpu.make_async_copy(spectrum_ref.at[span], raw.at[span], sem.at[c])

    for c in range(chunks):
        copy(c).start()
    for c in range(2):
        for r in range(rows):
            windb[c, r] = jnp.broadcast_to(wind_ref[c, r : r + 1], (SUB, nx))
    for r in range(rows):
        for kind, source in ((0, 0), (1, 1), (2, 3)):
            fill(splat, kind, r, geometry(geo_ref, ext, source, r), nx)

    def before(i):
        @pl.when(i % turns == 0)
        def _():
            copy(i // turns).wait()

    def planes(at):
        sl = pl.ds(at, SUB)
        bw, we, wn = [wide(table_ref[s, sl, b : b + 1]) for b in (BW, WE, WN)]
        natural, grown = {}, {}
        for h in range(nx // LANES):
            natural[h] = jnp.swapaxes(raw[sl, :, half(h)], 0, 1)
            for r in range(rows):
                drive = we * windb[0, r, :, half(h)] + wn * windb[1, r, :, half(h)]
                grown[r, h] = 1.0 + jnp.maximum(drive - 0.05, 0.0)
                growth_ref[pl.ds(pl.multiple_of(r * fd + at, SUB), SUB), half(h)] = grown[r, h]
        return lambda r, h: bw * natural[h][r], lambda r, h: grown[r, h]

    def store(r, at, h, value):
        out_ref[pl.ds(pl.multiple_of((r - 1) * fd + at, SUB), SUB), half(h)] = value

    inner = list(range(1, rows - 1))
    advance([inner], fd, nx, s, table_ref, planes, store, splat, acc, False, before)
    write_totals(total_ref, acc, inner, None, ext, nx)


def step_kernel(n, cfg, *refs):
    rows, fd, nx, t_n, s_n, cols = n
    segments, source, growth, grow, raw, sums, joined, count = cfg
    ext = rows + 2 * HALO
    refs = list(refs)
    table_ref, geo_ref = refs.pop(0), refs.pop(0)
    wind_ref = refs.pop(0) if grow else None
    own_ref, got_ref = (None, None) if raw else (refs.pop(0), refs.pop(0))
    previous = refs.pop(0) if joined else None
    cross_ref = refs.pop(0) if sums else None
    operands, refs = refs[:count], refs[count:]
    out_ref, total_ref = refs.pop(0), refs.pop(0)
    growth_ref = refs.pop(0) if grow else None
    splat, acc = refs.pop(0), refs.pop(0)
    windb = refs.pop(0) if grow else None
    s = lax.axis_index("spec")
    order = [r for segment in segments for r in segment]
    needed = sorted({r + d for r in order for d in (-1, 0, 1)})
    breaking = geo_ref[3 * ext : 4 * ext]
    if not raw:
        breaking = breaking / (1.0 + (own_ref[...] + got_ref[...]) * geo_ref[2 * ext : 3 * ext])
    for r in needed:
        fill(splat, 0, r, geometry(geo_ref, ext, 0, r), nx)
        fill(splat, 1, r, geometry(geo_ref, ext, 1, r), nx)
        fill(splat, 2, r, breaking[r + HALO : r + HALO + 1], nx)
    for c in range(2):
        for k, r in enumerate(grow):
            at = c * ext + r + HALO
            windb[c, k] = jnp.broadcast_to(wind_ref[at : at + 1], (SUB, nx))

    tile = lax.axis_index("tile")
    even = tile % 2 == 0

    def load(place, at, h):
        found, first = place[:2]
        parts = [operands[k][pl.ds(pl.multiple_of(first + at, SUB), SUB), half(h)] for k in found]
        value = parts[0] if len(parts) == 1 else jnp.where(even, parts[0], parts[1])
        if len(parts) == 3:
            value = jnp.where(tile == (t_n // 2 if place[2] < 0 else t_n // 2 - 1), parts[2], value)
        return value

    def planes(at):
        sl = pl.ds(at, SUB)
        bw = wide(table_ref[s, sl, BW : BW + 1]) if raw else None
        we, wn = [wide(table_ref[s, sl, b : b + 1]) for b in (WE, WN)] if grow else (None, None)

        def energy(r, h):
            value = load(source[r] + (r,), at, h)
            return bw * value if raw else value

        def factor(r, h):
            if r in grow:
                k = grow.index(r)
                drive = we * windb[0, k, :, half(h)] + wn * windb[1, k, :, half(h)]
                value = 1.0 + jnp.maximum(drive - 0.05, 0.0)
                growth_ref[pl.ds(pl.multiple_of(k * fd + at, SUB), SUB), half(h)] = value
                return value
            return load(growth[r], at, h)

        return energy, factor

    def store(r, at, h, value):
        out_ref[pl.ds(pl.multiple_of(order.index(r) * fd + at, SUB), SUB), half(h)] = value

    advance(segments, fd, nx, s, table_ref, planes, store, splat, acc, sums)
    if not sums:
        write_totals(total_ref, acc, order, previous, ext, nx)
        return
    kinds = [jnp.concatenate(folded(acc, kind, order), axis=0) for kind in range(acc.shape[0])]
    wet = jnp.where(s == 0, geo_ref[3 * ext + HALO : 3 * ext + HALO + rows], 0.0)
    shift = jnp.broadcast_to(cross_ref[:, 0:1], (rows, nx))
    moved = barrel(kinds + [wet], shift, nx, False)
    lane = lanes_of((rows, nx))
    size = cols + 8
    for t in range(t_n):
        chunk = jnp.zeros((rows, nx), jnp.float32)
        for q, value in enumerate(moved):
            amount = (q * size - (cols * t - 4)) % nx
            piece = pltpu.roll(value, amount, 1) if amount else value
            chunk = jnp.where((lane >= q * size) & (lane < (q + 1) * size), piece, chunk)
        for q in range(s_n):
            total_ref[(t_n + t) * s_n + q] = chunk
    mine = lax.axis_index("tile")
    for q in range(s_n):
        total_ref[mine * s_n + q] = kinds[0]


def last_kernel(n, table_ref, level_ref, got_ref, geo_ref, wave_ref, ocean_ref, sea_ref,
                hb_ref, ha_ref, lev_ref, waves_ref, next_ref,
                raw, brk, turn, field, mix, out, sem, osem):
    rows, fd, nx, t_n, s_n, cols, own, ny, chunks = n
    s = lax.axis_index("spec")
    g = lax.axis_index("grp")
    tile = lax.axis_index("tile")
    part = fd // chunks
    pad = turn.shape[0]
    size = cols + 8

    def write(c, source):
        return pltpu.make_async_copy(raw.at[pl.ds(source * part, part)], waves_ref.at[pl.ds(c * part, part)], sem.at[c])

    ocean_copy = pltpu.make_async_copy(out, next_ref, osem)

    @pl.when(g == 0)
    def _():
        total = got_ref[tile * s_n]
        for q in range(1, s_n):
            total = total + got_ref[tile * s_n + q]
        ext = rows + 2 * HALO
        wet = geo_ref[3 * ext + HALO : 3 * ext + HALO + rows]
        breaking = wet / (1.0 + total * geo_ref[2 * ext + HALO : 2 * ext + HALO + rows])
        for r in range(rows):
            brk[r] = jnp.broadcast_to(breaking[r : r + 1], (SUB, nx))
        for c in range(chunks):

            def finish(i, carry):
                for k in range(4):
                    at = pl.multiple_of(c * part + (4 * i + k) * SUB, SUB)
                    sl = pl.ds(at, SUB)
                    inv = wide(table_ref[s, sl, INV : INV + 1])
                    for h in range(nx // LANES):
                        spans = [pl.ds(pl.multiple_of(r * fd + at, SUB), SUB) for r in range(rows)]
                        values = [wave_ref[span, half(h)] for span in spans]
                        values = [value * brk[r, :, half(h)] * inv for r, value in enumerate(values)]
                        raw[sl, :, half(h)] = jnp.swapaxes(jnp.stack(values), 0, 1)
                return carry

            lax.fori_loop(0, part // (4 * SUB), finish, 0)
            write(c, c).start()
        out[...] = jnp.zeros((3, own, cols, ny), jnp.float32)
        ocean_copy.start()
        ocean_copy.wait()
        for c in range(chunks):
            write(c, c).wait()

    @pl.when(g == 1)
    def _():
        def clear(i, carry):
            raw[pl.ds(pl.multiple_of(i * SUB, SUB), SUB)] = jnp.zeros((SUB, rows, nx), jnp.float32)
            return carry

        lax.fori_loop(0, part // SUB, clear, 0)
        for c in range(chunks):
            write(c, 0).start()

        if pad > ny:
            turn[ny:pad] = jnp.zeros((pad - ny, nx), jnp.float32)
        for t in range(t_n):
            tilev = got_ref[t * s_n]
            for q in range(1, s_n):
                tilev = tilev + got_ref[t * s_n + q]
            turn[t * rows : (t + 1) * rows] = tilev
        turned = jnp.transpose(turn[...])
        total, sx, sy, dx, dy, wet = [turned[q * size : (q + 1) * size] for q in range(6)]
        row = lax.broadcasted_iota(jnp.int32, (size, pad), 0)
        column = row + (tile * cols - 4)
        wet = jnp.where((column >= 0) & (column < t_n * cols), wet, 0.0)
        stack = 3 * own
        mix[0] = jnp.zeros((size, pad), jnp.float32)
        mix[0, 4 : 4 + cols, 0:ny] = sea_ref[...]
        mix[0, 2:4, 0:ny] = hb_ref[2 * stack : 2 * stack + 2, 0:ny]
        mix[0, 4 + cols : 6 + cols, 0:ny] = ha_ref[2 * stack : 2 * stack + 2, 0:ny]
        depth = 10.0 + 4.0 * mix[0]
        breaking = 1.0 / (1.0 + 25.0 * total / (depth * depth))
        swept = wet * breaking
        sx, sy, dx, dy = sx * breaking, sy * breaking, dx * swept, dy * swept

        field[...] = jnp.zeros(field.shape, jnp.float32)
        ext = own + 4
        for c in range(3):
            for k in range(own):
                l = c * ext + 2 + k
                field[l, 4 : 4 + cols, 0:ny] = ocean_ref[c, k]
                for m in range(2):
                    at = m * stack + c * own + k
                    field[l, 2 + m : 3 + m, 0:ny] = hb_ref[at : at + 1, 0:ny]
                    field[l, 4 + cols + m : 5 + cols + m, 0:ny] = ha_ref[at : at + 1, 0:ny]
        for upper in range(2):
            @pl.when(s == 1 - upper)
            def _():
                for c in range(3):
                    for k in range(2):
                        l = c * ext + (own + 2 if upper else 0) + k
                        field[l, :, 0:ny] = lev_ref[c * 2 + k]

        lane = lanes_of((size, pad))

        def new_fields(source, k):
            values = []
            for c in range(3):
                q = source[c * ext + k]
                lateral = (
                    pltpu.roll(q, size - 1, 0)
                    + pltpu.roll(q, 1, 0)
                    + jnp.where(lane == ny - 1, 0.0, pltpu.roll(q, pad - 1, 1))
                    + jnp.where(lane == 0, 0.0, pltpu.roll(q, 1, 1))
                    - 4.0 * q
                )
                vertical = source[c * ext + k + 1] + source[c * ext + k - 1] - 2.0 * q
                values.append((q, q + 0.1 * lateral + 0.2 * vertical))
            (u, du), (v, dv), (_, dt) = values
            shaped = level_ref[s, 1, k]
            top = jnp.where((s == 0) & (k == 2), 1.0, 0.0)
            east = du + 0.1 * (v + shaped * dy) + top * sx
            north = dv - 0.1 * (u + shaped * dx) + top * sy
            keep = wet * level_ref[s, 2, k]
            return keep * east, keep * north, keep * dt

        for k in range(1, ext - 1):
            for c, value in enumerate(new_fields(field, k)):
                mix[c * ext + k] = value
        for k in range(2, ext - 2):
            for c, value in enumerate(new_fields(mix, k)):
                out[c, k - 2] = value[4 : 4 + cols, 0:ny]
        ocean_copy.start()
        ocean_copy.wait()
        for c in range(chunks):
            write(c, 0).wait()


def program(spectrum, wind, land_mask, intersection, ocean_state, sea_level, *, mesh_shape):
    g_n, t_n, s_n = (mesh_shape[a] for a in AXES)
    _, freqs, dirs, rows, nx = spectrum.shape
    _, _, own, cols, ny = ocean_state.shape
    fd = freqs * dirs
    devices = g_n * t_n * s_n
    table = jnp.asarray(wave_table(freqs, dirs * s_n, s_n))
    levels = jnp.asarray(level_table(own * s_n, s_n, own))
    ocean = ocean_state[0]
    sea = sea_level[0]

    def in_hbm(x):
        return pltpu.with_memory_space_constraint(x, pltpu.HBM)

    natural = in_hbm(spectrum.reshape(fd, rows, nx))
    chunks = 6
    vm = pltpu.VMEM
    params = pltpu.CompilerParams(vmem_limit_bytes=24 << 20)

    def swapped(x, start, without=None):
        lower = [i for i in range(start, t_n - 1, 2) if i + 1 != without]
        return lax.ppermute(x, "tile", [(i, i + 1) for i in lower] + [(i + 1, i) for i in lower])

    def others(x):
        return added(lax.ppermute(x, "spec", [(i, (i + k) % s_n) for i in range(s_n)]) for k in range(1, s_n))

    def added(values):
        return functools.reduce(lambda a, b: a + b, values)

    def call(kernel, args, specs, shapes, out_specs, scratch):
        return pl.pallas_call(
            kernel, out_shape=shapes, in_specs=specs, out_specs=out_specs,
            scratch_shapes=scratch, compiler_params=params,
        )(*args)

    ext = rows + 2 * HALO
    near, second, far = f32(fd + 4 * HALO, nx), f32(fd, nx), f32((HALO - 2) * fd, nx)

    def hbm(shape):
        return pltpu.HBM(shape.shape, shape.dtype)

    send, level_rim, near_a, near_b, next_a, next_b, far_a, far_b, turn = call(
        functools.partial(start_kernel, (t_n, s_n, rows, cols, own, ny, fd, nx, chunks)),
        (levels, natural, in_hbm(ocean.reshape(3 * own, cols, ny)), in_hbm(sea), in_hbm(land_mask), in_hbm(wind), in_hbm(intersection)),
        [SM] + [HB] * 6,
        (f32(devices, ext, 4 * cols), f32(3, 2, cols, ny), hbm(near), hbm(near), hbm(second), hbm(second), hbm(far), hbm(far), hbm(far)),
        (VM,) * 2 + (HB,) * 7,
        [vm((fd, rows, nx), jnp.float32), vm((3 * own, cols, ny), jnp.float32), vm((cols, ny), jnp.float32),
         vm((rows, nx), jnp.int32), vm((2, rows, nx), jnp.float32), vm((rows, nx), jnp.int32),
         vm(near.shape, jnp.float32), vm(near.shape, jnp.float32),
         vm(second.shape, jnp.float32), vm(second.shape, jnp.float32), vm(far.shape, jnp.float32), vm(far.shape, jnp.float32),
         pltpu.SemaphoreType.DMA((chunks + 6,)), pltpu.SemaphoreType.DMA((chunks, 6, HALO + 1))],
    )
    got_a, got_b = swapped(near_a, 0), swapped(near_b, 1)
    arrived = lax.all_to_all(send, AXES, 0, 0, tiled=True)
    next_got = swapped(next_a, 0), swapped(next_b, 1)
    middle = t_n // 2
    turned = lax.ppermute(turn, "tile", [(middle - 1, t_n - 1), (middle, 0)])
    far_got = swapped(far_a, 0, middle), swapped(far_b, 1, middle)
    turned = lax.ppermute(turned, "tile", [(t_n - 1, middle), (0, middle - 1)])

    geo = call(
        functools.partial(pick_kernel, (t_n, s_n, rows, cols, nx, fd), False),
        (arrived, land_mask, intersection), [VM] * 3, f32(4 * ext, nx), VM, [],
    )

    def scratch(kinds, grow):
        result = [vm((3, ext, SUB, nx), jnp.float32), vm((kinds, ext, SUB, nx), jnp.float32)]
        return result + [vm((2, grow, SUB, nx), jnp.float32)] if grow else result

    mid, total, growth0 = call(
        functools.partial(first_middle_kernel, (rows, fd, nx, chunks)),
        (table, geo, wind, natural), [VM] * 3 + [HB],
        (f32((rows - 2) * fd, nx), f32(ext, nx), f32(rows * fd, nx)), (VM,) * 3,
        [vm((fd, rows, nx), jnp.float32), vm((2, rows, SUB, nx), jnp.float32)] + scratch(1, 0)
        + [pltpu.SemaphoreType.DMA((chunks,))],
    )
    riding = f32(-(-(6 * own + 2) // SUB) * SUB, nx)
    geo, winds, level_rim, hb, ha = call(
        functools.partial(pick_kernel, (t_n, s_n, rows, cols, nx, fd, own), True),
        (arrived, land_mask, intersection, wind, got_a, got_b, level_rim), [VM] * 7,
        (f32(4 * ext, nx), f32(2 * ext, nx), f32(6, cols + 8, ny), riding, riding), (VM,) * 5, [],
    )

    planes = {k: {} for k in range(WSTEPS + 1)}
    for j in range(HALO):
        k, at = min(j, 2), max(j - 2, 0) * fd
        a, b = ((got_a, got_b), next_got, far_got)[k]
        corner = (turned,) if k == 2 else ()
        planes[0][-1 - j] = ((b, a) + corner, at)
        planes[0][rows + j] = ((a, b) + corner, at)
        if j < 2:
            a, b = ((near_a, near_b), (next_a, next_b))[j]
            planes[0][j] = ((b, a), 0)
            planes[0][rows - 1 - j] = ((a, b), 0)
    for k, r in enumerate(range(1, rows - 1)):
        planes[1][r] = ((mid,), k * fd)
    grown = {r: ((growth0,), r * fd) for r in range(rows)}
    totals, gots = {1: total}, {}

    def advanced(step, segments, exchange=True):
        raw, sums = step == 1, step == WSTEPS
        order = [r for segment in segments for r in segment]
        grow = [r for r in order if r not in grown]
        operands = []

        def place(item):
            found = []
            for array in item[0]:
                known = [k for k, other in enumerate(operands) if other is array]
                if not known:
                    operands.append(array)
                found.append(known[0] if known else len(operands) - 1)
            return tuple(found), item[1]

        source = {r: place(planes[step - 1][r]) for r in sorted({r + d for r in order for d in (-1, 0, 1)})}
        growth = {r: place(grown[r]) for r in order if r in grown}
        args = [table, geo]
        if grow:
            args.append(winds)
        if not raw:
            args += [totals[step - 1], gots[step - 1]]
        joined = step in totals
        if joined:
            args.append(totals[step])
        if sums:
            args.append(intersection)
        args += operands
        shapes = [f32(len(order) * fd, nx), f32(devices, rows, nx) if sums else f32(ext, nx)]
        if grow:
            shapes.append(f32(len(grow) * fd, nx))
        cfg = (segments, source, growth, grow, raw, sums, joined, len(operands))
        outs = call(
            functools.partial(step_kernel, (rows, fd, nx, t_n, s_n, cols), cfg),
            args, [VM] * len(args), tuple(shapes), (VM,) * len(shapes), scratch(5 if sums else 1, len(grow)),
        )
        for k, r in enumerate(order):
            planes[step][r] = ((outs[0],), k * fd)
        for k, r in enumerate(grow):
            grown[r] = ((outs[2],), k * fd)
        totals[step] = outs[1]
        if exchange and not sums:
            gots[step] = others(outs[1])

    def pair(first, last):
        return [list(range(first, last + 1)), list(range(rows - 1 - last, rows - first))]

    advanced(1, pair(-1, 0))
    advanced(2, [list(range(rows))])
    advanced(1, pair(-3, -2))
    advanced(3, [list(range(1, rows - 1))], exchange=False)
    level_got = others(level_rim)
    advanced(2, pair(-2, -1))
    advanced(3, pair(-1, 0))
    totals[3], level_got = lax.optimization_barrier((totals[3], level_got))
    advanced(4, [list(range(rows))])

    landed = lax.all_to_all(totals[WSTEPS], AXES, 0, 0, tiled=True)
    pad = -(-ny // LANES) * LANES
    size = cols + 8
    ins = (table, levels, landed, geo, planes[WSTEPS][0][0][0], ocean, sea, hb, ha, level_got)
    waves, fields = call(
        functools.partial(last_kernel, (rows, fd, nx, t_n, s_n, cols, own, ny, chunks)),
        ins, [VM, SM] + [VM] * (len(ins) - 2), (f32(fd, rows, nx), f32(3, own, cols, ny)), (HB, HB),
        [
            vm((fd, rows, nx), jnp.float32),
            vm((rows, SUB, nx), jnp.float32),
            vm((pad, nx), jnp.float32),
            vm((3 * (own + 4), size, pad), jnp.float32),
            vm((3 * (own + 4), size, pad), jnp.float32),
            vm((3, own, cols, ny), jnp.float32),
            pltpu.SemaphoreType.DMA((chunks,)),
            pltpu.SemaphoreType.DMA,
        ],
    )
    return waves.reshape(spectrum.shape), fields.reshape(ocean_state.shape)


def solution(mesh):
    return jax.shard_map(
        functools.partial(program, mesh_shape=dict(mesh.shape)),
        mesh=mesh,
        in_specs=(
            P("grp", None, "spec", "tile", None),
            P(None, "tile", None),
            P("tile", None),
            P("tile", None),
            P("grp", None, "spec", "tile", None),
            P("grp", "tile", None),
        ),
        out_specs=(P("grp", None, "spec", "tile", None), P("grp", None, "spec", "tile", None)),
        check_vma=False,
    )
```
